32 devices in a mesh: old: 4 (over x, core), new: 8 (over z, y).
Axes of the slice: x: 2, y: 2, z: 4, core: 2. Of those that a mesh axis runs over, the one named last changes fastest.
Arguments:
- old_emb: bfloat16 [768, 8192], P('new', 'old'), may hold values from -16 to 16
- new_emb: bfloat16 [768, 8192], P('old', 'new'), may hold values from -16 to 16
- old_logw: float32 [8192], P('old'), may hold values from -1 to 1
- new_logw: float32 [8192], P('new'), may hold values from -1 to 1
Outputs:
- old_pot: float32 [8192], P('old')
- new_pot: float32 [8192], P('new')
- old_map: float32 [768, 8192], P('new', 'old')
- new_map: float32 [768, 8192], P('old', 'new')
The draws below stay inside these ranges and needn't reach their ends.
All inputs are finite; a program needn't handle non-finite values.
Results may differ from the reference program's by a relative error of at most 0.0026.
Values may be sent and summed in bfloat16 or wider, within the bound.
No kernel may reach another device: no remote copies, remote signals or barrier semaphores. Data moves between devices by JAX's collectives and lax.ppermute only.
A program may use at most 128 MiB of HBM per device.

```python
import math
import jax
import jax.numpy as jnp
from jax import lax

D = 768
ITERS = 3
NO = 8192
NN = 8192


EPSILON = 0.5


def planted(key):
    base = jax.random.fold_in(key, 4242)
    keys = jax.random.split(base, 4)
    targets = jnp.array([240.0, 190.0, 150.0], jnp.float32)
    shared = jnp.clip(jax.random.normal(keys[0], (3, D), jnp.float32), -3.0, 3.0)
    old_rows = jax.random.permutation(keys[1], NO)[:3]
    new_rows = jax.random.permutation(keys[2], NN)[:6]
    noise = jnp.clip(jax.random.normal(keys[3], (3, D), jnp.float32), -3.0, 3.0)
    along = jnp.sum(noise * shared, axis=1) / jnp.sum(shared * shared, axis=1)
    other = noise - along[:, None] * shared
    squares = jnp.sum(shared * shared, axis=1)
    strengths = jnp.sqrt(targets * math.sqrt(D) * EPSILON / squares)
    lowered = 2.0 / targets
    first = strengths[:, None] * shared
    second = strengths[:, None] * ((1.0 - lowered)[:, None] * shared + 0.25 * other)
    return (old_rows, new_rows, first, second)


def draw_old_emb(key, part):
    values = jnp.clip(jax.random.normal(jax.random.fold_in(key, 1), (D, NO), jnp.float32), -4.0, 4.0)
    old_rows, new_rows, first, second = planted(key)
    values = values.at[:, old_rows].set(first.T)
    return jnp.clip(values, -16.0, 16.0).astype(jnp.bfloat16)


def draw_new_emb(key, part):
    values = jnp.clip(jax.random.normal(jax.random.fold_in(key, 3), (D, NN), jnp.float32), -4.0, 4.0)
    old_rows, new_rows, first, second = planted(key)
    values = values.at[:, new_rows[:3]].set(first.T)
    values = values.at[:, new_rows[3:]].set(second.T)
    return jnp.clip(values, -16.0, 16.0).astype(jnp.bfloat16)


def block_scale(stream_key, dims, pieces, smallest, top_value):
    factor_of, own = 1.0, jax.random.fold_in(stream_key, 6)
    for position, blocks in pieces:
        steps = jnp.exp(jax.random.uniform(jax.random.fold_in(own, position), (blocks,), jnp.float32, smallest / len(pieces), top_value / len(pieces)))
        factor_of = factor_of * jnp.repeat(steps, dims[position] // blocks).reshape([-1 if axis == position else 1 for axis in range(len(dims))])
    return factor_of


def setup_inputs(seed: int = 0) -> dict:
    splits = jax.random.split(jax.random.key(seed), 5)
    return {
        "old_emb": draw_old_emb(jax.random.fold_in(splits[4], 71), 0),
        "new_emb": draw_new_emb(jax.random.fold_in(splits[4], 71), 0),
        "old_logw": jnp.clip(jax.random.uniform(splits[2], (NO,), jnp.float32, -1.0, 1.0) * block_scale(splits[2], (NO,), ((0, 4),), -0.4, 0.0), -1.0, 1.0),
        "new_logw": jnp.clip(jax.random.uniform(splits[3], (NN,), jnp.float32, -1.0, 1.0) * block_scale(splits[3], (NN,), ((0, 8),), -0.4, 0.0), -1.0, 1.0),
    }


EPSILON = 0.5

def lse_along(values, axis):
    peak = lax.optimization_barrier(jnp.max(values, axis=axis, keepdims=True))
    total = lax.optimization_barrier(jnp.sum(jnp.exp(values - peak), axis=axis, keepdims=True))
    return jnp.squeeze(peak + jnp.log(total), axis=axis)

def reference(old_emb, new_emb, old_logw, new_logw):
    scale = 1.0 / (math.sqrt(D) * EPSILON)
    logits = lax.dot_general(old_emb, new_emb, (((0,), (0,)), ((), ())), preferred_element_type=jnp.float32) * scale
    old_pot = jnp.zeros((NO,), jnp.float32)
    new_pot = jnp.zeros((NN,), jnp.float32)
    for step in range(ITERS):
        old_pot = old_logw - lse_along(logits + new_pot[None, :], 1)
        new_pot = new_logw - lse_along(logits + old_pot[:, None], 0)
    plan = jnp.exp(logits + old_pot[:, None] + new_pot[None, :])
    mass = lax.optimization_barrier(jnp.sum(plan, axis=1))
    plan_low = plan.astype(jnp.bfloat16)
    old_terms = lax.dot_general(new_emb, plan_low, (((1,), (1,)), ((), ())), preferred_element_type=jnp.float32)
    new_terms = jnp.dot(old_emb, plan_low, preferred_element_type=jnp.float32)
    old_map = old_terms / mass[None, :]
    new_map = new_terms / jnp.exp(new_logw)[None, :]
    return (old_pot, new_pot, old_map, new_map)
```

```python
import functools
import math

import jax
import jax.numpy as jnp
from jax import lax
from jax.experimental import pallas as pl
from jax.experimental.pallas import tpu as pltpu
from jax.sharding import PartitionSpec as P

ITERS = 3
EPSILON = 0.5
LANES = 128
SAFE = 1e-20
CUT_IN = 2
CUT_OUT = 2
BF16 = jnp.bfloat16
F32 = jnp.float32
VMEM_LIMIT = 44 * 2**20


def call(kernel, outs, scratch, args, name, flops=0, nbytes=0, exps=0):
    out_shape, arrays, in_specs = [], [], []
    for shape, dtype, resident in outs:
        out_shape.append(
            pltpu.VMEM(shape, dtype) if resident else jax.ShapeDtypeStruct(shape, dtype)
        )
    for array, where in args:
        if where == "resident":
            array = pltpu.with_memory_space_constraint(array, pltpu.VMEM)
        arrays.append(array)
        space = {"smem": pltpu.SMEM, "any": pl.ANY}.get(where, pltpu.VMEM)
        in_specs.append(pl.BlockSpec(memory_space=space))
    return pl.pallas_call(
        kernel,
        out_shape=tuple(out_shape),
        in_specs=in_specs,
        out_specs=tuple(pl.BlockSpec(memory_space=pltpu.VMEM) for _ in outs),
        scratch_shapes=scratch,
        compiler_params=pltpu.CompilerParams(vmem_limit_bytes=VMEM_LIMIT),
        cost_estimate=pl.CostEstimate(flops=flops, bytes_accessed=nbytes, transcendentals=exps),
        name=name,
    )(*arrays)


def diagonal():
    shape = (LANES, LANES)
    return lax.broadcasted_iota(jnp.int32, shape, 0) == lax.broadcasted_iota(jnp.int32, shape, 1)


def to_column(row8, eye):
    rows = jnp.concatenate([row8] * (LANES // 8), axis=0)
    return jnp.sum(jnp.where(eye, rows, 0.0), axis=1, keepdims=True)


def to_row(column, eye):
    return jnp.sum(jnp.where(eye, column, 0.0), axis=0, keepdims=True)


def folded(tile, op):
    return op(tile.reshape(LANES // 8, 8, LANES), axis=0)


def repeated(ref, row):
    return ref[pl.ds(row, 8, stride=0), :]


def spread(row8):
    return jnp.concatenate([row8] * (LANES // 8), axis=0)


def logits_kernel(n_old, n_new, cut, scale, devices, where_ref, *refs):
    old_refs, refs = refs[: n_old * cut], refs[n_old * cut :]
    new_refs, refs = refs[:n_new], refs[n_new:]
    lt_ref, k_ref, of_ref, nf_ref, a_ref, msg_ref, nt_ref, m_ref = refs
    depth, rows = nf_ref.shape
    columns = of_ref.shape[1]
    for p in range(n_old):
        for h in range(cut):
            piece = old_refs[p * cut + h]
            r, w = piece.shape
            start = pl.multiple_of(where_ref[p] * r, r)
            of_ref[pl.ds(start, r), h * w : (h + 1) * w] = piece[...]
    for p in range(n_new):
        piece = new_refs[p]
        r = piece.shape[0]
        start = pl.multiple_of(where_ref[n_old + p] * r, r)
        nf_ref[pl.ds(start, r), :] = piece[...]
    for c in range(rows // LANES):
        nt_ref[c * LANES : (c + 1) * LANES, :] = nf_ref[:, c * LANES : (c + 1) * LANES].T
    wide = 2 * LANES

    def block(b, carry):
        at = pl.ds(pl.multiple_of(b * wide, wide), wide)
        lt_ref[:, at] = (
            lax.dot_general(
                nt_ref[...], of_ref[:, at], (((1,), (0,)), ((), ())), preferred_element_type=F32
            )
            * scale
        )
        for t in range(2):
            lane = pl.ds(pl.multiple_of(b * wide + t * LANES, LANES), LANES)
            top = jnp.full((8, LANES), -jnp.inf, F32)
            for j in range(rows // LANES):
                top = jnp.maximum(top, folded(lt_ref[j * LANES : (j + 1) * LANES, lane], jnp.max))
            top = jnp.max(top, axis=0, keepdims=True)
            a_ref[pl.ds(2 * b + t, 1), :] = top
            m_ref[pl.ds(2 * b + t, 1), :] = top
            high = spread(jnp.broadcast_to(top, (8, LANES)))
            total = jnp.zeros((8, LANES), F32)
            for j in range(rows // LANES):
                tile = jnp.exp(lt_ref[j * LANES : (j + 1) * LANES, lane] - high)
                k_ref[j * LANES : (j + 1) * LANES, lane] = tile
                total = total + folded(tile, jnp.sum)
            m_ref[pl.ds(columns // LANES + 2 * b + t, 1), :] = jnp.sum(total, axis=0, keepdims=True)
        return carry

    lax.fori_loop(0, columns // wide, block, 0)
    for d in range(devices):
        msg_ref[d] = m_ref[...]


def combine(parts):
    peak = functools.reduce(jnp.maximum, [m for m, _ in parts])
    sums = [s * jnp.exp(m - peak) for m, s in parts]
    while len(sums) > 1:
        sums = [sums[i] + sums[i + 1] for i in range(0, len(sums), 2)]
    return peak + jnp.log(sums[0])


def column_kernel(got_ref, a_ref, logw_ref, k_ref, lt_hbm, f_ref, msg_ref, w_ref, chunk_ref, sem):
    wide = a_ref.shape[0]
    tall = k_ref.shape[0] // LANES
    got = [(got_ref[d, :wide, :], got_ref[d, wide:, :]) for d in range(got_ref.shape[0])]
    f = logw_ref[...] - combine(got)
    f_ref[...] = f
    fa = f + a_ref[...]
    high = jnp.max(jnp.max(fa, axis=1, keepdims=True), axis=0, keepdims=True)
    w_ref[...] = jnp.exp(fa - high)
    eye = diagonal()

    def block(j, least):
        at = pl.ds(pl.multiple_of(j * LANES, LANES), LANES)
        acc = jnp.zeros((LANES // 8, 8, LANES), F32)
        for c in range(wide):
            tile = k_ref[at, c * LANES : (c + 1) * LANES].reshape(LANES // 8, 8, LANES)
            acc = acc + tile * repeated(w_ref, c)[None]
        total = to_row(jnp.sum(acc.reshape(LANES, LANES), axis=1, keepdims=True), eye)
        msg_ref[pl.ds(tall + j, 1), :] = total
        return jnp.minimum(least, total)

    least = lax.fori_loop(0, tall, block, jnp.full((1, LANES), jnp.inf, F32))
    msg_ref[:tall, :] = jnp.broadcast_to(high, (tall, LANES))

    @pl.when(jnp.logical_not(jnp.min(least) > SAFE))
    def _():
        def exact(j, carry):
            at = pl.ds(pl.multiple_of(j * LANES, LANES), LANES)
            copy = pltpu.make_async_copy(lt_hbm.at[at, :], chunk_ref, sem)
            copy.start()
            copy.wait()
            top = jnp.full((LANES, LANES), -jnp.inf, F32)
            for c in range(wide):
                lane = slice(c * LANES, (c + 1) * LANES)
                shifted = chunk_ref[:, lane] + spread(repeated(f_ref, c))
                chunk_ref[:, lane] = shifted
                top = jnp.maximum(top, shifted)
            top = jnp.max(top, axis=1, keepdims=True)
            acc = jnp.zeros((LANES, LANES), F32)
            for c in range(wide):
                acc = acc + jnp.exp(chunk_ref[:, c * LANES : (c + 1) * LANES] - top)
            msg_ref[pl.ds(j, 1), :] = to_row(top, eye)
            msg_ref[pl.ds(tall + j, 1), :] = to_row(jnp.sum(acc, axis=1, keepdims=True), eye)
            return carry

        lax.fori_loop(0, tall, exact, 0)


def row_kernel(n_got, *refs):
    got_refs, refs = refs[:n_got], refs[n_got:]
    logw_ref, a_ref, k_ref, lt_hbm, msg_ref, g_ref, v_ref, m_ref, chunk_ref, sem = refs
    wide = a_ref.shape[0]
    tall = k_ref.shape[0] // LANES
    g = logw_ref[...] - combine([(r[:tall, :], r[tall:, :]) for r in got_refs])
    g_ref[...] = g
    high = jnp.max(jnp.max(g, axis=1, keepdims=True), axis=0, keepdims=True)
    v_ref[...] = jnp.exp(g - high)
    eye = diagonal()

    def block(j, acc):
        at = pl.ds(pl.multiple_of(j * LANES, LANES), LANES)
        v = to_column(repeated(v_ref, j), eye)
        return tuple(
            acc[c] + folded(k_ref[at, c * LANES : (c + 1) * LANES] * v, jnp.sum)
            for c in range(wide)
        )

    acc = lax.fori_loop(0, tall, block, (jnp.zeros((8, LANES), F32),) * wide)
    m_ref[:wide, :] = a_ref[...] + high
    least = jnp.full((1, LANES), jnp.inf, F32)
    for c in range(wide):
        total = jnp.sum(acc[c], axis=0, keepdims=True)
        m_ref[wide + c : wide + c + 1, :] = total
        least = jnp.minimum(least, total)

    @pl.when(jnp.logical_not(jnp.min(least) > SAFE))
    def _():
        m_ref[:wide, :] = jnp.full((wide, LANES), -jnp.inf, F32)
        m_ref[wide:, :] = jnp.zeros((wide, LANES), F32)

        def exact(j, carry):
            at = pl.ds(pl.multiple_of(j * LANES, LANES), LANES)
            copy = pltpu.make_async_copy(lt_hbm.at[at, :], chunk_ref, sem)
            copy.start()
            copy.wait()
            column = to_column(repeated(g_ref, j), eye)
            for c in range(wide):
                shifted = chunk_ref[:, c * LANES : (c + 1) * LANES] + column
                before = m_ref[c : c + 1, :]
                top = jnp.maximum(before, jnp.max(shifted, axis=0, keepdims=True))
                m_ref[c : c + 1, :] = top
                m_ref[wide + c : wide + c + 1, :] = m_ref[
                    wide + c : wide + c + 1, :
                ] * jnp.exp(before - top) + jnp.sum(jnp.exp(shifted - top), axis=0, keepdims=True)
            return carry

        lax.fori_loop(0, tall, exact, 0)

    for d in range(msg_ref.shape[0]):
        msg_ref[d] = m_ref[...]


def plan_kernel(n_got, *refs):
    got_refs, refs = refs[:n_got], refs[n_got:]
    logw_ref, f_ref, lt_ref, g_ref, p_ref, mass_ref = refs
    wide = f_ref.shape[0]
    tall = lt_ref.shape[0] // LANES
    g_ref[...] = logw_ref[...] - combine([(r[:tall, :], r[tall:, :]) for r in got_refs])
    eye = diagonal()

    def block(j, acc):
        at = pl.ds(pl.multiple_of(j * LANES, LANES), LANES)
        column = to_column(repeated(g_ref, j), eye)
        out = []
        for c in range(wide):
            lane = slice(c * LANES, (c + 1) * LANES)
            plan = jnp.exp(lt_ref[at, lane] + spread(repeated(f_ref, c)) + column)
            p_ref[at, lane] = plan.astype(BF16)
            out.append(acc[c] + folded(plan, jnp.sum))
        return tuple(out)

    acc = lax.fori_loop(0, tall, block, (jnp.zeros((8, LANES), F32),) * wide)
    for c in range(wide):
        mass_ref[c : c + 1, :] = jnp.sum(acc[c], axis=0, keepdims=True)


def old_terms_kernel(cut, where_ref, nf_ref, p_ref, *refs):
    outs, lhs_ref = refs[:-1], refs[-1]
    blocks = len(outs) // cut
    r, w = outs[0].shape
    for k in range(blocks):
        lhs_ref[k * r : (k + 1) * r, :] = nf_ref[pl.ds(pl.multiple_of(where_ref[k] * r, r), r), :]
    wide = 2 * LANES
    for h in range(cut):

        def block(b, carry, h=h):
            here = pl.ds(pl.multiple_of(b * wide, wide), wide)
            at = pl.ds(pl.multiple_of(h * w + b * wide, wide), wide)
            got = jnp.dot(lhs_ref[...], p_ref[:, at], preferred_element_type=F32)
            for k in range(blocks):
                out = outs[k * cut + h]
                out[:, here] = got[k * r : (k + 1) * r, :].astype(out.dtype)
            return carry

        lax.fori_loop(0, w // wide, block, 0)


def new_terms_kernel(where_ref, of_ref, p_ref, out_ref, lhs_ref):
    blocks, r, w = out_ref.shape
    for k in range(blocks):
        lhs_ref[k * r : (k + 1) * r, :] = of_ref[pl.ds(pl.multiple_of(where_ref[k] * r, r), r), :]
    wide = 2 * LANES

    def block(b, carry):
        at = pl.ds(pl.multiple_of(b * wide, wide), wide)
        got = lax.dot_general(
            lhs_ref[...], p_ref[at, :], (((1,), (1,)), ((), ())), preferred_element_type=F32
        )
        for k in range(blocks):
            out_ref[k, :, at] = got[k * r : (k + 1) * r, :].astype(out_ref.dtype)
        return carry

    lax.fori_loop(0, w // wide, block, 0)


def swap(x, axis, size, mask, only=None):
    return lax.ppermute(
        x, axis, [(i, i ^ mask) for i in range(size) if only is None or only(i)]
    )


def is_mid(i):
    return i // 2 in (1, 2)


def is_end(i):
    return not is_mid(i)


def gather_old(x):
    me = lax.axis_index("new")
    mid = jnp.logical_or(me // 2 == 1, me // 2 == 2)
    width = x.shape[1] // CUT_IN
    slots = [[], [], [], []]
    across = [[], [], [], []]
    parts = [x[:, h * width : (h + 1) * width] for h in range(CUT_IN)]
    for own in parts:
        slots[0].append(own)
        across[0].append(swap(own, "new", 8, 1))
    near = [swap(own, "new", 8, 2) for own in parts]
    middle = [swap(own, "new", 8, 6, is_mid) for own in parts]
    far = [swap(x, "new", 8, 6, is_mid) for x in near]
    end = [swap(x, "new", 8, 2, is_mid) for x in middle]
    last = [swap(x, "new", 8, 2, is_mid) for x in far]
    for h in range(CUT_IN):
        third = jnp.where(mid, middle[h], end[h])
        fourth = jnp.where(mid, far[h], last[h])
        for s, block in ((1, near[h]), (2, third), (3, fourth)):
            slots[s].append(block)
            across[s].append(swap(block, "new", 8, 1))
    two, three = jnp.where(mid, 6, 4), jnp.where(mid, 4, 6)
    owners = [me, me ^ 2, me ^ two, me ^ three]
    owners = owners + [o ^ 1 for o in owners]
    return slots + across, owners


def gather_new(x):
    me = lax.axis_index("old")
    pair = jnp.stack([x, swap(x, "old", 4, 2)])
    other = swap(pair, "old", 4, 1)
    return [pair[0], pair[1], other[0], other[1]], [me, me ^ 2, me ^ 1, me ^ 3]


def out_order():
    z = lax.axis_index("new") // 2
    mid = jnp.logical_or(z == 1, z == 2)
    return [jnp.where(mid, z ^ 2, z ^ 3), jnp.where(mid, z ^ 3, z ^ 2), z ^ 1, z]


def scatter_old(away, own):
    outs = []
    held = [
        [own[k][h] + swap(away[k][h], "new", 8, 1).astype(F32) for h in range(CUT_OUT)]
        for k in range(4)
    ]
    first, second, third, final = held

    def send(xs, mask, only=None):
        return [swap(x.astype(BF16), "new", 8, mask, only) for x in xs]

    def add(xs, ys):
        return [x + y.astype(F32) for x, y in zip(xs, ys)]

    first = add(first, send(first, 2, is_end))
    third = add(third, send(first, 6, is_mid))
    second = add(second, send(second, 2, is_end))
    final = add(final, send(second, 6, is_mid))
    outs = add(final, send(third, 2))
    return jnp.concatenate(outs, axis=1)


def integers(values):
    return jnp.stack([jnp.asarray(v, jnp.int32) for v in values])


def per_device(n_old, n_new, old_emb, new_emb, old_logw, new_logw):
    tuned = (n_old, n_new) == (4, 8)
    width, height = old_logw.shape[0], new_logw.shape[0]
    wide, tall = width // LANES, height // LANES
    depth = old_emb.shape[0] * n_new
    scale = 1.0 / (math.sqrt(depth) * EPSILON)
    if tuned:
        old_slots, old_owners = gather_old(old_emb)
        new_slots, new_owners = gather_new(new_emb)
    else:
        old_slots = [[lax.all_gather(old_emb, "new", axis=0, tiled=True)]]
        new_slots = [lax.all_gather(new_emb, "old", axis=0, tiled=True)]
        old_owners = new_owners = [0]
    old_w = old_logw.reshape(wide, LANES)
    new_w = new_logw.reshape(tall, LANES)
    cells = width * height
    lt, k, old_full, new_full, a, msg = call(
        functools.partial(
            logits_kernel, len(old_slots), len(new_slots), len(old_slots[0]), scale, n_new
        ),
        [
            ((height, width), F32, True),
            ((height, width), F32, True),
            ((depth, width), BF16, False),
            ((depth, height), BF16, False),
            ((wide, LANES), F32, False),
            ((n_new, 2 * wide, LANES), F32, False),
        ],
        [pltpu.VMEM((height, depth), BF16), pltpu.VMEM((2 * wide, LANES), F32)],
        [(integers(old_owners + new_owners), "smem")]
        + [(x, "vmem") for slot in old_slots for x in slot]
        + [(x, "vmem") for x in new_slots],
        "logits",
        flops=2 * cells * depth,
        nbytes=12 * cells,
        exps=cells,
    )

    def over_old(message):
        return [message] + [swap(message, "old", n_old, d) for d in range(1, n_old)]

    chunk = [pltpu.VMEM((LANES, width), F32), pltpu.SemaphoreType.DMA]
    for step in range(ITERS):
        got = lax.all_to_all(msg, "new", 0, 0, tiled=True)
        f, columns = call(
            column_kernel,
            [((wide, LANES), F32, False), ((2 * tall, LANES), F32, False)],
            [pltpu.VMEM((wide, LANES), F32)] + chunk,
            [(got, "vmem"), (a, "vmem"), (old_w, "vmem"), (k, "resident"), (lt, "any")],
            "column_sums",
            flops=2 * cells,
            nbytes=4 * cells,
        )
        columns = over_old(columns)
        if step + 1 < ITERS:
            (msg,) = call(
                functools.partial(row_kernel, n_old),
                [((n_new, 2 * wide, LANES), F32, False)],
                [pltpu.VMEM((tall, LANES), F32)] * 2
                + [pltpu.VMEM((2 * wide, LANES), F32)]
                + chunk,
                [(c, "vmem") for c in columns]
                + [(new_w, "vmem"), (a, "vmem"), (k, "resident"), (lt, "any")],
                "row_sums",
                flops=2 * cells,
                nbytes=4 * cells,
            )
    g, plan, mass = call(
        functools.partial(plan_kernel, n_old),
        [
            ((tall, LANES), F32, False),
            ((height, width), BF16, True),
            ((wide, LANES), F32, False),
        ],
        [],
        [(c, "vmem") for c in columns] + [(new_w, "vmem"), (f, "vmem"), (lt, "resident")],
        "plan",
        flops=2 * cells,
        nbytes=6 * cells,
        exps=cells,
    )
    if tuned:
        r = depth // n_new
        mine = lax.axis_index("new") % 2
        order = out_order()

        def old_part(y, dtype, name):
            got = call(
                functools.partial(old_terms_kernel, CUT_OUT),
                [((r, width // CUT_OUT), dtype, False)] * (4 * CUT_OUT),
                [pltpu.VMEM((4 * r, height), BF16)],
                [
                    (integers([2 * o + y for o in order]), "smem"),
                    (new_full, "vmem"),
                    (plan, "resident"),
                ],
                name,
                flops=cells * depth,
                nbytes=2 * cells,
            )
            return [got[i * CUT_OUT : (i + 1) * CUT_OUT] for i in range(4)]

        away = old_part(1 - mine, BF16, "old_terms_away")
        for d in (1, 2, 4):
            mass = mass + swap(mass, "new", 8, d)
        own = old_part(mine, F32, "old_terms_own")
        old_sums = scatter_old(away, own)
        q = depth // n_old
        me = lax.axis_index("old")

        def new_part(targets, dtype, name):
            return call(
                new_terms_kernel,
                [((2, q, height), dtype, False)],
                [pltpu.VMEM((2 * q, width), BF16)],
                [(integers(targets), "smem"), (old_full, "vmem"), (plan, "resident")],
                name,
                flops=cells * depth,
                nbytes=2 * cells,
            )[0]

        far = swap(new_part([me ^ 2, me ^ 3], BF16, "new_terms_away"), "old", 4, 2)
        near = new_part([me, me ^ 1], F32, "new_terms_own") + far.astype(F32)
        new_sums = near[0] + swap(near[1].astype(BF16), "old", 4, 1).astype(F32)
    else:
        mass = lax.psum(mass, "new")
        old_terms = jnp.dot(new_full, plan, preferred_element_type=F32)
        new_terms = lax.dot_general(
            old_full, plan, (((1,), (1,)), ((), ())), preferred_element_type=F32
        )
        old_sums = lax.psum_scatter(old_terms, "new", scatter_dimension=0, tiled=True)
        new_sums = lax.psum_scatter(new_terms, "old", scatter_dimension=0, tiled=True)
    old_map = old_sums / mass.reshape(width)[None, :]
    new_map = new_sums / jnp.exp(new_logw)[None, :]
    return (f.reshape(width), g.reshape(height), old_map, new_map)


def solution(mesh):
    in_specs = (P("new", "old"), P("old", "new"), P("old"), P("new"))
    out_specs = (P("old"), P("new"), P("new", "old"), P("old", "new"))
    return jax.shard_map(
        functools.partial(per_device, mesh.shape["old"], mesh.shape["new"]),
        mesh=mesh,
        in_specs=in_specs,
        out_specs=out_specs,
        check_vma=False,
    )
```

```python
import functools
import math

import jax
import jax.numpy as jnp
from jax import lax
from jax.experimental import pallas as pl
from jax.experimental.pallas import tpu as pltpu
from jax.sharding import PartitionSpec as P

ITERS = 3
EPSILON = 0.5
LANES = 128
SAFE = 1e-20
BF16 = jnp.bfloat16
F32 = jnp.float32
MIB = 2**20


def call(kernel, outs, scratch, args, limit, flops=0, nbytes=0, exps=0):
    out_shape, arrays, in_specs = [], [], []
    for shape, dtype, resident in outs:
        out_shape.append(
            pltpu.VMEM(shape, dtype) if resident else jax.ShapeDtypeStruct(shape, dtype)
        )
    for array, where in args:
        if where == "resident":
            array = pltpu.with_memory_space_constraint(array, pltpu.VMEM)
        arrays.append(array)
        space = {"smem": pltpu.SMEM, "any": pl.ANY}.get(where, pltpu.VMEM)
        in_specs.append(pl.BlockSpec(memory_space=space))
    return pl.pallas_call(
        kernel,
        out_shape=tuple(out_shape),
        in_specs=in_specs,
        out_specs=tuple(pl.BlockSpec(memory_space=pltpu.VMEM) for _ in outs),
        scratch_shapes=scratch,
        compiler_params=pltpu.CompilerParams(vmem_limit_bytes=limit * MIB),
        cost_estimate=pl.CostEstimate(flops=flops, bytes_accessed=nbytes, transcendentals=exps),
    )(*arrays)


def diagonal():
    shape = (LANES, LANES)
    return lax.broadcasted_iota(jnp.int32, shape, 0) == lax.broadcasted_iota(jnp.int32, shape, 1)


def to_column(row8, eye):
    rows = jnp.concatenate([row8] * (LANES // 8), axis=0)
    return jnp.sum(jnp.where(eye, rows, 0.0), axis=1, keepdims=True)


def to_row(column, eye):
    return jnp.sum(jnp.where(eye, column, 0.0), axis=0, keepdims=True)


def folded(tile, op):
    return op(tile.reshape(LANES // 8, 8, LANES), axis=0)


def repeated(ref, row):
    return ref[pl.ds(row, 8, stride=0), :]


def spread(row8):
    return jnp.concatenate([row8] * (LANES // 8), axis=0)


def logits_kernel(n_old, n_new, cut, scale, devices, where_ref, *refs):
    old_refs, refs = refs[: n_old * cut], refs[n_old * cut :]
    new_refs, refs = refs[:n_new], refs[n_new:]
    lt_ref, k_ref, of_ref, nf_ref, a_ref, msg_ref, nt_ref, m_ref = refs
    _, rows = nf_ref.shape
    columns = of_ref.shape[1]
    for p in range(n_old):
        for h in range(cut):
            piece = old_refs[p * cut + h]
            r, w = piece.shape
            start = pl.multiple_of(where_ref[p] * r, r)
            of_ref[pl.ds(start, r), h * w : (h + 1) * w] = piece[...]
    for p in range(n_new):
        piece = new_refs[p]
        r = piece.shape[0]
        start = pl.multiple_of(where_ref[n_old + p] * r, r)
        nf_ref[pl.ds(start, r), :] = piece[...]
    for c in range(rows // LANES):
        nt_ref[c * LANES : (c + 1) * LANES, :] = nf_ref[:, c * LANES : (c + 1) * LANES].T
    wide = 2 * LANES
    blocks = columns // wide

    def product(b):
        at = pl.ds(pl.multiple_of(b * wide, wide), wide)
        lt_ref[:, at] = (
            lax.dot_general(
                nt_ref[...], of_ref[:, at], (((1,), (0,)), ((), ())), preferred_element_type=F32
            )
            * scale
        )

    def exponentials(b):
        for t in range(2):
            lane = pl.ds(pl.multiple_of(b * wide + t * LANES, LANES), LANES)
            top = jnp.full((8, LANES), -jnp.inf, F32)
            for j in range(rows // LANES):
                top = jnp.maximum(top, folded(lt_ref[j * LANES : (j + 1) * LANES, lane], jnp.max))
            top = jnp.max(top, axis=0, keepdims=True)
            a_ref[pl.ds(2 * b + t, 1), :] = top
            m_ref[pl.ds(2 * b + t, 1), :] = top
            high = spread(jnp.broadcast_to(top, (8, LANES)))
            total = jnp.zeros((8, LANES), F32)
            for j in range(rows // LANES):
                tile = jnp.exp(lt_ref[j * LANES : (j + 1) * LANES, lane] - high)
                k_ref[j * LANES : (j + 1) * LANES, lane] = tile
                total = total + folded(tile, jnp.sum)
            m_ref[pl.ds(2 * blocks + 2 * b + t, 1), :] = jnp.sum(total, axis=0, keepdims=True)

    product(0)

    def block(b, carry):
        product(b)
        exponentials(b - 1)
        return carry

    lax.fori_loop(1, blocks, block, 0)
    exponentials(blocks - 1)
    for d in range(devices):
        msg_ref[d] = m_ref[...]


def combine(parts):
    peak = functools.reduce(jnp.maximum, [m for m, _ in parts])
    sums = [s * jnp.exp(m - peak) for m, s in parts]
    while len(sums) > 1:
        sums = [sums[i] + sums[i + 1] for i in range(0, len(sums), 2)]
    return peak + jnp.log(sums[0])


def column_kernel(got_ref, a_ref, logw_ref, k_ref, lt_hbm, f_ref, msg_ref, w_ref, chunk_ref, sem):
    wide = a_ref.shape[0]
    tall = k_ref.shape[0] // LANES
    got = [(got_ref[d, :wide, :], got_ref[d, wide:, :]) for d in range(got_ref.shape[0])]
    f = logw_ref[...] - combine(got)
    f_ref[...] = f
    fa = f + a_ref[...]
    high = jnp.max(jnp.max(fa, axis=1, keepdims=True), axis=0, keepdims=True)
    w_ref[...] = jnp.exp(fa - high)
    eye = diagonal()

    def block(j, least):
        at = pl.ds(pl.multiple_of(j * LANES, LANES), LANES)
        acc = jnp.zeros((LANES // 8, 8, LANES), F32)
        for c in range(wide):
            tile = k_ref[at, c * LANES : (c + 1) * LANES].reshape(LANES // 8, 8, LANES)
            acc = acc + tile * repeated(w_ref, c)[None]
        total = to_row(jnp.sum(acc.reshape(LANES, LANES), axis=1, keepdims=True), eye)
        msg_ref[pl.ds(tall + j, 1), :] = total
        return jnp.minimum(least, total)

    least = lax.fori_loop(0, tall, block, jnp.full((1, LANES), jnp.inf, F32))
    msg_ref[:tall, :] = jnp.broadcast_to(high, (tall, LANES))

    @pl.when(jnp.logical_not(jnp.min(least) > SAFE))
    def _():
        def exact(j, carry):
            at = pl.ds(pl.multiple_of(j * LANES, LANES), LANES)
            copy = pltpu.make_async_copy(lt_hbm.at[at, :], chunk_ref, sem)
            copy.start()
            copy.wait()
            top = jnp.full((LANES, LANES), -jnp.inf, F32)
            for c in range(wide):
                lane = slice(c * LANES, (c + 1) * LANES)
                shifted = chunk_ref[:, lane] + spread(repeated(f_ref, c))
                chunk_ref[:, lane] = shifted
                top = jnp.maximum(top, shifted)
            top = jnp.max(top, axis=1, keepdims=True)
            acc = jnp.zeros((LANES, LANES), F32)
            for c in range(wide):
                acc = acc + jnp.exp(chunk_ref[:, c * LANES : (c + 1) * LANES] - top)
            msg_ref[pl.ds(j, 1), :] = to_row(top, eye)
            msg_ref[pl.ds(tall + j, 1), :] = to_row(jnp.sum(acc, axis=1, keepdims=True), eye)
            return carry

        lax.fori_loop(0, tall, exact, 0)


def row_kernel(n_got, *refs):
    got_refs, refs = refs[:n_got], refs[n_got:]
    logw_ref, a_ref, k_ref, lt_hbm, msg_ref, g_ref, v_ref, m_ref, chunk_ref, sem = refs
    wide = a_ref.shape[0]
    tall = k_ref.shape[0] // LANES
    g = logw_ref[...] - combine([(r[:tall, :], r[tall:, :]) for r in got_refs])
    g_ref[...] = g
    high = jnp.max(jnp.max(g, axis=1, keepdims=True), axis=0, keepdims=True)
    v_ref[...] = jnp.exp(g - high)
    eye = diagonal()

    def block(j, acc):
        at = pl.ds(pl.multiple_of(j * LANES, LANES), LANES)
        v = to_column(repeated(v_ref, j), eye)
        return tuple(
            acc[c] + folded(k_ref[at, c * LANES : (c + 1) * LANES] * v, jnp.sum)
            for c in range(wide)
        )

    acc = lax.fori_loop(0, tall, block, (jnp.zeros((8, LANES), F32),) * wide)
    m_ref[:wide, :] = a_ref[...] + high
    least = jnp.full((1, LANES), jnp.inf, F32)
    for c in range(wide):
        total = jnp.sum(acc[c], axis=0, keepdims=True)
        m_ref[wide + c : wide + c + 1, :] = total
        least = jnp.minimum(least, total)

    @pl.when(jnp.logical_not(jnp.min(least) > SAFE))
    def _():
        m_ref[:wide, :] = jnp.full((wide, LANES), -jnp.inf, F32)
        m_ref[wide:, :] = jnp.zeros((wide, LANES), F32)

        def exact(j, carry):
            at = pl.ds(pl.multiple_of(j * LANES, LANES), LANES)
            copy = pltpu.make_async_copy(lt_hbm.at[at, :], chunk_ref, sem)
            copy.start()
            copy.wait()
            column = to_column(repeated(g_ref, j), eye)
            for c in range(wide):
                shifted = chunk_ref[:, c * LANES : (c + 1) * LANES] + column
                before = m_ref[c : c + 1, :]
                top = jnp.maximum(before, jnp.max(shifted, axis=0, keepdims=True))
                m_ref[c : c + 1, :] = top
                m_ref[wide + c : wide + c + 1, :] = m_ref[
                    wide + c : wide + c + 1, :
                ] * jnp.exp(before - top) + jnp.sum(jnp.exp(shifted - top), axis=0, keepdims=True)
            return carry

        lax.fori_loop(0, tall, exact, 0)

    for d in range(msg_ref.shape[0]):
        msg_ref[d] = m_ref[...]


def plan_kernel(n_got, *refs):
    got_refs, refs = refs[:n_got], refs[n_got:]
    logw_ref, f_ref, lt_ref, g_ref, p_ref, mass_ref = refs
    wide = f_ref.shape[0]
    tall = lt_ref.shape[0] // LANES
    g_ref[...] = logw_ref[...] - combine([(r[:tall, :], r[tall:, :]) for r in got_refs])
    eye = diagonal()

    def block(j, acc):
        at = pl.ds(pl.multiple_of(j * LANES, LANES), LANES)
        column = to_column(repeated(g_ref, j), eye)
        out = []
        for c in range(wide):
            lane = slice(c * LANES, (c + 1) * LANES)
            plan = jnp.exp(lt_ref[at, lane] + spread(repeated(f_ref, c)) + column)
            p_ref[at, lane] = plan.astype(BF16)
            out.append(acc[c] + folded(plan, jnp.sum))
        return tuple(out)

    acc = lax.fori_loop(0, tall, block, (jnp.zeros((8, LANES), F32),) * wide)
    for c in range(wide):
        mass_ref[c : c + 1, :] = jnp.sum(acc[c], axis=0, keepdims=True)


def old_terms_kernel(cuts, base, where_ref, nf_ref, p_ref, *refs):
    outs, lhs_ref = refs[:-1], refs[-1]
    r = lhs_ref.shape[0] // len(cuts)
    for k in range(len(cuts)):
        lhs_ref[k * r : (k + 1) * r, :] = nf_ref[
            pl.ds(pl.multiple_of(where_ref[base + k] * r, r), r), :
        ]
    wide = 2 * LANES
    half = p_ref.shape[1] // 2
    for h in range(2):

        def block(b, carry, h=h):
            at = pl.ds(pl.multiple_of(h * half + b * wide, wide), wide)
            within = pl.ds(pl.multiple_of(b * wide, wide), wide)
            got = jnp.dot(lhs_ref[...], p_ref[:, at], preferred_element_type=F32)
            for k, cut in enumerate(cuts):
                out = outs[sum(cuts[:k]) + (h if cut == 2 else 0)]
                out[:, within if cut == 2 else at] = got[k * r : (k + 1) * r, :].astype(out.dtype)
            return carry

        lax.fori_loop(0, half // wide, block, 0)


def new_terms_kernel(base, where_ref, of_ref, p_ref, out_ref, lhs_ref):
    blocks, r, w = out_ref.shape
    for k in range(blocks):
        lhs_ref[k * r : (k + 1) * r, :] = of_ref[
            pl.ds(pl.multiple_of(where_ref[base + k] * r, r), r), :
        ]
    wide = 2 * LANES

    def block(b, carry):
        at = pl.ds(pl.multiple_of(b * wide, wide), wide)
        got = lax.dot_general(
            lhs_ref[...], p_ref[at, :], (((1,), (1,)), ((), ())), preferred_element_type=F32
        )
        for k in range(blocks):
            out_ref[k, :, at] = got[k * r : (k + 1) * r, :].astype(out_ref.dtype)
        return carry

    lax.fori_loop(0, w // wide, block, 0)


def swap(x, axis, size, mask, only=None):
    return lax.ppermute(x, axis, [(i, i ^ mask) for i in range(size) if only is None or only(i)])


def is_mid(i):
    return i // 2 in (1, 2)


def is_end(i):
    return not is_mid(i)


def halves(x):
    width = x.shape[1] // 2
    return [x[:, :width], x[:, width:]]


def gather_old(x):
    me = lax.axis_index("new")
    mid = jnp.logical_or(me // 2 == 1, me // 2 == 2)
    parts = halves(x)

    def send(blocks, mask, only=None):
        return [swap(b, "new", 8, mask, only) for b in blocks]

    near = send(parts, 2)
    middle = send(parts, 6, is_mid)
    far = send(near, 6, is_mid)
    end = send(middle, 2, is_mid)
    last = send(far, 2, is_mid)
    third = [jnp.where(mid, middle[h], end[h]) for h in range(2)]
    fourth = [jnp.where(mid, far[h], last[h]) for h in range(2)]
    slots = [parts, near, third, fourth]
    across = [halves(swap(x, "new", 8, 1, None))]
    across += [send(slots[s], 1) for s in (1, 2, 3)]
    two, three = jnp.where(mid, 6, 4), jnp.where(mid, 4, 6)
    owners = [me, me ^ 2, me ^ two, me ^ three]
    owners = owners + [o ^ 1 for o in owners]
    return slots + across, owners


def gather_new(x):
    me = lax.axis_index("old")
    pair = jnp.stack([x, swap(x, "old", 4, 2, None)])
    other = swap(pair, "old", 4, 1, None)
    return [pair[0], pair[1], other[0], other[1]], [me, me ^ 2, me ^ 1, me ^ 3]


def out_order():
    z = lax.axis_index("new") // 2
    mid = jnp.logical_or(z == 1, z == 2)
    return [jnp.where(mid, z ^ 2, z ^ 3), jnp.where(mid, z ^ 3, z ^ 2), z ^ 1, z]


def scatter_old(away, own):
    def send(x, mask, only=None):
        return swap(x.astype(BF16), "new", 8, mask, only).astype(F32)

    first = [x + send(y, 1) for x, y in zip(halves(own[0]), away[0])]
    second, third, final = (own[k] + send(away[k], 1) for k in (1, 2, 3))
    second = second + send(second, 2, is_end)
    first = [x + send(x, 2, is_end) for x in first]
    across = [send(x, 6, is_mid) for x in first]
    third = [x + y for x, y in zip(halves(third), across)]
    final = final + send(second, 6, is_mid)
    return final + jnp.concatenate([send(x, 2) for x in third], axis=1)


def integers(values):
    return jnp.stack([jnp.asarray(v, jnp.int32) for v in values])


def is_tuned(n_old, n_new):
    return (n_old, n_new) == (4, 8)


def per_device(n_old, n_new, old_emb, new_emb, old_logw, new_logw):
    tuned = is_tuned(n_old, n_new)
    width, height = old_logw.shape[0], new_logw.shape[0]
    wide, tall = width // LANES, height // LANES
    depth = old_emb.shape[0] * n_new
    scale = 1.0 / (math.sqrt(depth) * EPSILON)
    if tuned:
        old_slots, old_owners = gather_old(old_emb)
        new_slots, new_owners = gather_new(new_emb)
    else:
        old_slots = [[lax.all_gather(old_emb, "new", axis=0, tiled=True)]]
        new_slots = [lax.all_gather(new_emb, "old", axis=0, tiled=True)]
        old_owners = new_owners = [0]
    owners = old_owners + new_owners
    held = len(owners)
    if tuned:
        y, me = lax.axis_index("new") % 2, lax.axis_index("old")
        order = out_order()
        owners = owners + [2 * o + 1 - y for o in order] + [2 * o + y for o in order]
        owners = owners + [me ^ 2, me ^ 3, me, me ^ 1]
    where = integers(owners)
    old_w = old_logw.reshape(wide, LANES)
    new_w = new_logw.reshape(tall, LANES)
    cells = width * height
    lt, k, old_full, new_full, a, msg = call(
        functools.partial(
            logits_kernel, len(old_slots), len(new_slots), len(old_slots[0]), scale, n_new
        ),
        [
            ((height, width), F32, True),
            ((height, width), F32, True),
            ((depth, width), BF16, False),
            ((depth, height), BF16, False),
            ((wide, LANES), F32, False),
            ((n_new, 2 * wide, LANES), F32, False),
        ],
        [pltpu.VMEM((height, depth), BF16), pltpu.VMEM((2 * wide, LANES), F32)],
        [(where, "smem")]
        + [(x, "vmem") for slot in old_slots for x in slot]
        + [(x, "vmem") for x in new_slots],
        28,
        flops=2 * cells * depth,
        nbytes=12 * cells,
        exps=cells,
    )

    def over_old(message):
        return [message] + [swap(message, "old", n_old, d) for d in range(1, n_old)]

    chunk = [pltpu.VMEM((LANES, width), F32), pltpu.SemaphoreType.DMA]
    for step in range(ITERS):
        got = lax.all_to_all(msg, "new", 0, 0, tiled=True)
        f, columns = call(
            column_kernel,
            [((wide, LANES), F32, False), ((2 * tall, LANES), F32, False)],
            [pltpu.VMEM((wide, LANES), F32)] + chunk,
            [(got, "vmem"), (a, "vmem"), (old_w, "vmem"), (k, "resident"), (lt, "any")],
            6,
            flops=2 * cells,
            nbytes=4 * cells,
        )
        columns = over_old(columns)
        if step + 1 < ITERS:
            (msg,) = call(
                functools.partial(row_kernel, n_old),
                [((n_new, 2 * wide, LANES), F32, False)],
                [pltpu.VMEM((tall, LANES), F32)] * 2
                + [pltpu.VMEM((2 * wide, LANES), F32)]
                + chunk,
                [(c, "vmem") for c in columns]
                + [(new_w, "vmem"), (a, "vmem"), (k, "resident"), (lt, "any")],
                6,
                flops=2 * cells,
                nbytes=4 * cells,
            )
    g, plan, mass = call(
        functools.partial(plan_kernel, n_old),
        [
            ((tall, LANES), F32, False),
            ((height, width), BF16, True),
            ((wide, LANES), F32, False),
        ],
        [],
        [(c, "vmem") for c in columns] + [(new_w, "vmem"), (f, "vmem"), (lt, "resident")],
        6,
        flops=2 * cells,
        nbytes=6 * cells,
        exps=cells,
    )
    if tuned:
        r = depth // n_new

        def old_part(base, dtype, cuts):
            return call(
                functools.partial(old_terms_kernel, cuts, base),
                [((r, width // cut), dtype, False) for cut in cuts for _ in range(cut)],
                [pltpu.VMEM((4 * r, height), BF16)],
                [
                    (where, "smem"),
                    (new_full, "vmem"),
                    (plan, "resident"),
                ],
                16,
                flops=cells * depth,
                nbytes=2 * cells,
            )

        got = old_part(held, BF16, (2, 1, 1, 1))
        for d in (1, 2, 4):
            mass = mass + swap(mass, "new", 8, d, None)
        own = old_part(held + 4, F32, (1, 1, 1, 1))
        old_sums = scatter_old([got[:2], *got[2:]], own)
        q = depth // n_old

        def new_part(base, dtype):
            return call(
                functools.partial(new_terms_kernel, base),
                [((2, q, height), dtype, False)],
                [pltpu.VMEM((2 * q, width), BF16)],
                [(where, "smem"), (old_full, "vmem"), (plan, "resident")],
                16,
                flops=cells * depth,
                nbytes=2 * cells,
            )[0]

        far = swap(new_part(held + 8, BF16), "old", 4, 2, None)
        near = new_part(held + 10, F32) + far.astype(F32)
        core = swap(near[1].astype(BF16), "old", 4, 1, None)
        new_sums = near[0] + core.astype(F32)
    else:
        mass = lax.psum(mass, "new")
        old_terms = jnp.dot(new_full, plan, preferred_element_type=F32)
        new_terms = lax.dot_general(
            old_full, plan, (((1,), (1,)), ((), ())), preferred_element_type=F32
        )
        old_sums = lax.psum_scatter(old_terms, "new", scatter_dimension=0, tiled=True)
        new_sums = lax.psum_scatter(new_terms, "old", scatter_dimension=0, tiled=True)
    old_map = old_sums / mass.reshape(width)[None, :]
    new_map = new_sums / jnp.exp(new_logw)[None, :]
    return (f.reshape(width), g.reshape(height), old_map, new_map)


def solution(mesh):
    in_specs = (P("new", "old"), P("old", "new"), P("old"), P("new"))
    out_specs = (P("old"), P("new"), P("new", "old"), P("old", "new"))
    n_old, n_new = mesh.shape["old"], mesh.shape["new"]
    return jax.shard_map(
        functools.partial(per_device, n_old, n_new),
        mesh=mesh,
        in_specs=in_specs,
        out_specs=out_specs,
        check_vma=False,
    )
```

```python
import functools
import math

import jax
import jax.numpy as jnp
from jax import lax
from jax.experimental import pallas as pl
from jax.experimental.pallas import tpu as pltpu
from jax.sharding import PartitionSpec as P

ITERS = 3
EPSILON = 0.5
LANES = 128
SAFE = 1e-20
BF16 = jnp.bfloat16
F32 = jnp.float32
OLD, NEW = "old", "new"
MIB = 2**20
STAY, VM, SM, ANY = range(4)


def call(kernel, outs, scratch, args, limit, flops=0, nbytes=0, exps=0, aliases=None):
    out_shape, arrays, in_specs = [], [], []
    for shape, dtype, resident in outs:
        out_shape.append(
            pltpu.VMEM(shape, dtype) if resident else jax.ShapeDtypeStruct(shape, dtype)
        )
    for array, where in args:
        if where == STAY:
            array = pltpu.with_memory_space_constraint(array, pltpu.VMEM)
        arrays.append(array)
        space = {SM: pltpu.SMEM, ANY: pl.ANY}.get(where, pltpu.VMEM)
        in_specs.append(pl.BlockSpec(memory_space=space))
    return pl.pallas_call(
        kernel,
        out_shape=tuple(out_shape),
        in_specs=in_specs,
        out_specs=tuple(pl.BlockSpec(memory_space=pltpu.VMEM) for _ in outs),
        scratch_shapes=scratch,
        input_output_aliases=aliases or {},
        compiler_params=pltpu.CompilerParams(vmem_limit_bytes=limit * MIB),
        cost_estimate=pl.CostEstimate(flops=flops, bytes_accessed=nbytes, transcendentals=exps),
    )(*arrays)


def diagonal():
    shape = (LANES, LANES)
    return lax.broadcasted_iota(jnp.int32, shape, 0) == lax.broadcasted_iota(jnp.int32, shape, 1)


def to_column(row8, eye):
    rows = jnp.concatenate([row8] * (LANES // 8), axis=0)
    return jnp.sum(jnp.where(eye, rows, 0.0), axis=1, keepdims=True)


def to_row(column, eye):
    return jnp.sum(jnp.where(eye, column, 0.0), axis=0, keepdims=True)


def folded(tile, op):
    return op(tile.reshape(LANES // 8, 8, LANES), axis=0)


def repeated(ref, row):
    return ref[pl.ds(row, 8, stride=0), :]


def spread(row8):
    return jnp.concatenate([row8] * (LANES // 8), axis=0)


def stack_slots(slots, out_ref, row=0):
    for slot in slots:
        column = 0
        for piece in slot:
            r, w = piece.shape
            out_ref[row : row + r, column : column + w] = piece[...]
            column += w
        row += r


def grouped(refs, counts):
    return [refs[sum(counts[:p]) : sum(counts[: p + 1])] for p in range(len(counts))]


def prepare_kernel(n_slots, where_ref, *refs):
    new_refs, (nt_ref, nf_ref, ns_ref) = refs[:-3], refs[-3:]
    depth, rows = nf_ref.shape
    for p, piece in enumerate(new_refs):
        r = piece.shape[0]
        start = pl.multiple_of(where_ref[n_slots + p] * r, r)
        nf_ref[pl.ds(start, r), :] = piece[...]
    r = depth // n_slots
    for p in range(n_slots):
        ns_ref[p * r : (p + 1) * r, :] = nf_ref[pl.ds(pl.multiple_of(where_ref[p] * r, r), r), :]
    for c in range(rows // LANES):
        nt_ref[c * LANES : (c + 1) * LANES, :] = ns_ref[:, c * LANES : (c + 1) * LANES].T


def logits_kernel(counts, scale, devices, nt_ref, *refs):
    slots, refs = grouped(refs, counts), refs[sum(counts) :]
    lt_ref, k_ref, of_ref, a_ref, msg_ref, m_ref = refs
    columns = of_ref.shape[1]
    rows = nt_ref.shape[0]
    stack_slots(slots, of_ref)
    wide = 2 * LANES
    blocks = columns // wide

    def product(b):
        at = pl.ds(pl.multiple_of(b * wide, wide), wide)
        lt_ref[:, at] = jnp.dot(nt_ref[...], of_ref[:, at], preferred_element_type=F32) * scale

    def exponentials(b):
        for t in range(2):
            lane = pl.ds(pl.multiple_of(b * wide + t * LANES, LANES), LANES)
            top = jnp.full((8, LANES), -jnp.inf, F32)
            for j in range(rows // LANES):
                top = jnp.maximum(top, folded(lt_ref[j * LANES : (j + 1) * LANES, lane], jnp.max))
            top = jnp.max(top, axis=0, keepdims=True)
            a_ref[pl.ds(2 * b + t, 1), :] = top
            m_ref[pl.ds(2 * b + t, 1), :] = top
            high = spread(jnp.broadcast_to(top, (8, LANES)))
            total = jnp.zeros((8, LANES), F32)
            for j in range(rows // LANES):
                tile = jnp.exp(lt_ref[j * LANES : (j + 1) * LANES, lane] - high)
                k_ref[j * LANES : (j + 1) * LANES, lane] = tile
                total = total + folded(tile, jnp.sum)
            m_ref[pl.ds(2 * blocks + 2 * b + t, 1), :] = jnp.sum(total, axis=0, keepdims=True)

    product(0)

    def block(b, carry):
        product(b)
        exponentials(b - 1)
        return carry

    lax.fori_loop(1, blocks, block, 0)
    exponentials(blocks - 1)
    for d in range(devices):
        msg_ref[d] = m_ref[...]


def combine(parts):
    peak = functools.reduce(jnp.maximum, [m for m, _ in parts])
    sums = [s * jnp.exp(m - peak) for m, s in parts]
    while len(sums) > 1:
        sums = [sums[i] + sums[i + 1] for i in range(0, len(sums), 2)]
    return peak + jnp.log(sums[0])


def column_kernel(got_ref, a_ref, logw_ref, k_ref, lt_hbm, f_ref, near_ref, msg_ref, w_ref, chunk_ref, sem):
    wide = a_ref.shape[0]
    tall = k_ref.shape[0] // LANES
    got = [(got_ref[d, :wide, :], got_ref[d, wide:, :]) for d in range(got_ref.shape[0])]
    f = logw_ref[...] - combine(got)
    f_ref[...] = f
    near_ref[...] = f
    fa = f + a_ref[...]
    high = jnp.max(jnp.max(fa, axis=1, keepdims=True), axis=0, keepdims=True)
    w_ref[...] = jnp.exp(fa - high)
    eye = diagonal()

    least = jnp.full((1, LANES), jnp.inf, F32)
    for j in range(tall):
        acc = jnp.zeros((LANES // 8, 8, LANES), F32)
        for c in range(wide):
            tile = k_ref[j * LANES : (j + 1) * LANES, c * LANES : (c + 1) * LANES]
            acc = acc + tile.reshape(LANES // 8, 8, LANES) * repeated(w_ref, c)[None]
        total = to_row(jnp.sum(acc.reshape(LANES, LANES), axis=1, keepdims=True), eye)
        msg_ref[tall + j : tall + j + 1, :] = total
        least = jnp.minimum(least, total)
    msg_ref[:tall, :] = jnp.broadcast_to(high, (tall, LANES))

    @pl.when(jnp.logical_not(jnp.min(least) > SAFE))
    def _():
        def exact(j, carry):
            at = pl.ds(pl.multiple_of(j * LANES, LANES), LANES)
            copy = pltpu.make_async_copy(lt_hbm.at[at, :], chunk_ref, sem)
            copy.start()
            copy.wait()
            top = jnp.full((LANES, LANES), -jnp.inf, F32)
            for c in range(wide):
                lane = slice(c * LANES, (c + 1) * LANES)
                shifted = chunk_ref[:, lane] + spread(repeated(f_ref, c))
                chunk_ref[:, lane] = shifted
                top = jnp.maximum(top, shifted)
            top = jnp.max(top, axis=1, keepdims=True)
            acc = jnp.zeros((LANES, LANES), F32)
            for c in range(wide):
                acc = acc + jnp.exp(chunk_ref[:, c * LANES : (c + 1) * LANES] - top)
            msg_ref[pl.ds(j, 1), :] = to_row(top, eye)
            msg_ref[pl.ds(tall + j, 1), :] = to_row(jnp.sum(acc, axis=1, keepdims=True), eye)
            return carry

        lax.fori_loop(0, tall, exact, 0)


def row_kernel(n_got, *refs):
    got_refs, refs = refs[:n_got], refs[n_got:]
    logw_ref, a_ref, k_ref, lt_hbm, msg_ref, g_ref, v_ref, m_ref, chunk_ref, sem = refs
    wide = a_ref.shape[0]
    tall = k_ref.shape[0] // LANES
    g = logw_ref[...] - combine([(r[:tall, :], r[tall:, :]) for r in got_refs])
    g_ref[...] = g
    high = jnp.max(jnp.max(g, axis=1, keepdims=True), axis=0, keepdims=True)
    v_ref[...] = jnp.exp(g - high)
    eye = diagonal()

    acc = [jnp.zeros((8, LANES), F32)] * wide
    for j in range(tall):
        v = to_column(repeated(v_ref, j), eye)
        for c in range(wide):
            tile = k_ref[j * LANES : (j + 1) * LANES, c * LANES : (c + 1) * LANES]
            acc[c] = acc[c] + folded(tile * v, jnp.sum)
    m_ref[:wide, :] = a_ref[...] + high
    least = jnp.full((1, LANES), jnp.inf, F32)
    for c in range(wide):
        total = jnp.sum(acc[c], axis=0, keepdims=True)
        m_ref[wide + c : wide + c + 1, :] = total
        least = jnp.minimum(least, total)

    @pl.when(jnp.logical_not(jnp.min(least) > SAFE))
    def _():
        m_ref[:wide, :] = jnp.full((wide, LANES), -jnp.inf, F32)
        m_ref[wide:, :] = jnp.zeros((wide, LANES), F32)

        def exact(j, carry):
            at = pl.ds(pl.multiple_of(j * LANES, LANES), LANES)
            copy = pltpu.make_async_copy(lt_hbm.at[at, :], chunk_ref, sem)
            copy.start()
            copy.wait()
            column = to_column(repeated(g_ref, j), eye)
            for c in range(wide):
                shifted = chunk_ref[:, c * LANES : (c + 1) * LANES] + column
                before = m_ref[c : c + 1, :]
                top = jnp.maximum(before, jnp.max(shifted, axis=0, keepdims=True))
                m_ref[c : c + 1, :] = top
                m_ref[wide + c : wide + c + 1, :] = m_ref[
                    wide + c : wide + c + 1, :
                ] * jnp.exp(before - top) + jnp.sum(jnp.exp(shifted - top), axis=0, keepdims=True)
            return carry

        lax.fori_loop(0, tall, exact, 0)

    for d in range(msg_ref.shape[0]):
        msg_ref[d] = m_ref[...]


def plan_kernel(n_got, *refs):
    got_refs, refs = refs[:n_got], refs[n_got:]
    logw_ref, f_ref, lt_ref, g_ref, p_ref, mass_ref = refs
    wide = f_ref.shape[0]
    tall = lt_ref.shape[0] // LANES
    g_ref[...] = logw_ref[...] - combine([(r[:tall, :], r[tall:, :]) for r in got_refs])
    eye = diagonal()

    def block(j, acc):
        at = pl.ds(pl.multiple_of(j * LANES, LANES), LANES)
        column = to_column(repeated(g_ref, j), eye)
        out = []
        for c in range(wide):
            lane = slice(c * LANES, (c + 1) * LANES)
            plan = jnp.exp(lt_ref[at, lane] + spread(repeated(f_ref, c)) + column)
            p_ref[at, lane] = plan.astype(BF16)
            out.append(acc[c] + folded(plan, jnp.sum))
        return tuple(out)

    acc = lax.fori_loop(0, tall, block, (jnp.zeros((8, LANES), F32),) * wide)
    for c in range(wide):
        mass_ref[c : c + 1, :] = jnp.sum(acc[c], axis=0, keepdims=True)


def old_terms_kernel(cuts, base, where_ref, nf_ref, p_ref, *refs):
    outs, lhs_ref = refs[:-1], refs[-1]
    r = lhs_ref.shape[0] // len(cuts)
    for k in range(len(cuts)):
        lhs_ref[k * r : (k + 1) * r, :] = nf_ref[
            pl.ds(pl.multiple_of(where_ref[base + k] * r, r), r), :
        ]
    wide = 2 * LANES
    half = p_ref.shape[1] // 2
    for h in range(2):

        def block(b, carry, h=h):
            at = pl.ds(pl.multiple_of(h * half + b * wide, wide), wide)
            within = pl.ds(pl.multiple_of(b * wide, wide), wide)
            got = jnp.dot(lhs_ref[...], p_ref[:, at], preferred_element_type=F32)
            for k, cut in enumerate(cuts):
                out = outs[sum(cuts[:k]) + (h if cut == 2 else 0)]
                out[:, within if cut == 2 else at] = got[k * r : (k + 1) * r, :].astype(out.dtype)
            return carry

        lax.fori_loop(0, half // wide, block, 0)


def new_terms_kernel(base, pieces, where_ref, of_ref, p_ref, out_ref, lhs_ref):
    blocks, q, w = out_ref.shape
    r = blocks * q // pieces
    for k in range(pieces):
        lhs_ref[k * r : (k + 1) * r, :] = of_ref[
            pl.ds(pl.multiple_of(where_ref[base + k] * r, r), r), :
        ]
    wide = 2 * LANES

    def block(b, carry):
        at = pl.ds(pl.multiple_of(b * wide, wide), wide)
        got = lax.dot_general(
            lhs_ref[...], p_ref[at, :], (((1,), (1,)), ((), ())), preferred_element_type=F32
        )
        for k in range(blocks):
            out_ref[k, :, at] = got[k * q : (k + 1) * q, :].astype(out_ref.dtype)
        return carry

    lax.fori_loop(0, w // wide, block, 0)


def swap(x, axis, size, mask, only=None):
    return lax.ppermute(x, axis, [(i, i ^ mask) for i in range(size) if only is None or only(i)])


def is_mid(i):
    return i // 2 in (1, 2)


def is_end(i):
    return not is_mid(i)


def halves(x):
    width = x.shape[1] // 2
    return [x[:, :width], x[:, width:]]


def gather_old(x):
    me = lax.axis_index(NEW)
    mid = jnp.logical_or(me // 2 == 1, me // 2 == 2)
    parts = halves(x)

    def send(blocks, mask, only=None):
        return [swap(b, NEW, 8, mask, only) for b in blocks]

    near = send(parts, 2)
    middle = send(parts, 6, is_mid)
    far = send(near, 6, is_mid)
    end = send(middle, 2, is_mid)
    last = send(far, 2, is_mid)
    third = [jnp.where(mid, middle[h], end[h]) for h in range(2)]
    fourth = [jnp.where(mid, far[h], last[h]) for h in range(2)]
    slots = [[x], near, third, fourth]
    across = [[swap(x, NEW, 8, 1, None)]]
    across += [send(slots[s], 1) for s in (1, 2, 3)]
    two, three = jnp.where(mid, 6, 4), jnp.where(mid, 4, 6)
    masks = [0, 2, 1, 3, two, three, two ^ 1, three ^ 1]
    order = slots[:2] + across[:2] + slots[2:] + across[2:]
    return order, [me ^ mask for mask in masks]


def gather_new(x):
    me = lax.axis_index(OLD)
    pair = jnp.stack([x, swap(x, OLD, 4, 2, None)])
    other = swap(pair, OLD, 4, 1, None)
    return [pair[0], pair[1], other[0], other[1]], [me, me ^ 2, me ^ 1, me ^ 3]


def out_order():
    z = lax.axis_index(NEW) // 2
    mid = jnp.logical_or(z == 1, z == 2)
    return [jnp.where(mid, z ^ 2, z ^ 3), jnp.where(mid, z ^ 3, z ^ 2), z ^ 1, z]


def scatter_old(away, own):
    def send(x, mask, only=None):
        return swap(x.astype(BF16), NEW, 8, mask, only).astype(F32)

    first = [x + send(y, 1) for x, y in zip(own[0], away[0])]
    got = [send(away[k], 1) for k in (1, 2, 3)]
    second = [x + y for x, y in zip(own[1], halves(got[0]))]
    third = own[2][0] + got[1]
    final = [x + y for x, y in zip(own[3], halves(got[2]))]
    first = [x + send(x, 2, is_end) for x in first]
    passed = [send(x, 4, is_mid) for x in first]
    second = [x + send(x, 2, is_end) for x in second]
    middle = [send(x, 6, is_mid) for x in second]
    third = halves(send(third, 2))
    return jnp.concatenate([sum(parts) for parts in zip(final, third, passed, middle)], axis=1)


def slot_of(n):
    me = lax.axis_index(NEW)
    mid = jnp.logical_or(me // 2 == 1, me // 2 == 2)
    apart = (n ^ me) // 2
    late = jnp.where(apart == jnp.where(mid, 3, 2), 4, 5)
    return jnp.where(apart < 2, apart, late) + 2 * ((n ^ me) % 2)


def integers(values):
    return jnp.stack([jnp.asarray(v, jnp.int32) for v in values])


def is_tuned(n_old, n_new):
    return (n_old, n_new) == (4, 8)


def per_device(n_old, n_new, old_emb, new_emb, old_logw, new_logw):
    tuned = is_tuned(n_old, n_new)
    width, height = old_logw.shape[0], new_logw.shape[0]
    wide, tall = width // LANES, height // LANES
    depth = old_emb.shape[0] * n_new
    scale = 1.0 / (math.sqrt(depth) * EPSILON)
    if tuned:
        old_slots, old_owners = gather_old(old_emb)
        new_slots, new_owners = gather_new(new_emb)
    else:
        old_all = lax.all_gather(old_emb, NEW, axis=0, tiled=True)
        old_slots = [[old_all[: depth // 2]], [old_all[depth // 2 :]]]
        new_slots = [lax.all_gather(new_emb, OLD, axis=0, tiled=True)]
        old_owners, new_owners = [0, 1], [0]
    owners = old_owners + new_owners
    held = len(owners)
    if tuned:
        y, me = lax.axis_index(NEW) % 2, lax.axis_index(OLD)
        order = out_order()
        owners = owners + [2 * o + 1 - y for o in order] + [2 * o + y for o in order]
        for o in (me ^ 2, me ^ 3, me, me ^ 1):
            owners = owners + [slot_of(2 * o), slot_of(2 * o + 1)]
    where = integers(owners)
    old_w = old_logw.reshape(wide, LANES)
    new_w = new_logw.reshape(tall, LANES)
    cells = width * height
    n_slots = len(old_slots)
    new_rows, new_full = call(
        functools.partial(prepare_kernel, n_slots),
        [((height, depth), BF16, True), ((depth, height), BF16, True)],
        [pltpu.VMEM((depth, height), BF16)],
        [(where, SM)] + [(x, VM) for x in new_slots],
        8,
        flops=cells,
        nbytes=8 * depth * height,
    )
    lt, k, old_full, a, msg = call(
        functools.partial(logits_kernel, [len(slot) for slot in old_slots], scale, n_new),
        [
            ((height, width), F32, True),
            ((height, width), F32, True),
            ((depth, width), BF16, True),
            ((wide, LANES), F32, True),
            ((n_new, 2 * wide, LANES), F32, False),
        ],
        [pltpu.VMEM((2 * wide, LANES), F32)],
        [(new_rows, STAY)] + [(x, VM) for slot in old_slots for x in slot],
        8,
        flops=2 * cells * depth,
        nbytes=12 * cells,
        exps=cells,
    )

    def over_old(message):
        return [message] + [swap(message, OLD, n_old, d) for d in range(1, n_old)]

    chunk = [pltpu.VMEM((LANES, width), F32), pltpu.SemaphoreType.DMA]
    for step in range(ITERS):
        got = lax.all_to_all(msg, NEW, 0, 0, tiled=True)
        f, f_near, columns = call(
            column_kernel,
            [((wide, LANES), F32, False), ((wide, LANES), F32, True), ((2 * tall, LANES), F32, False)],
            [pltpu.VMEM((wide, LANES), F32)] + chunk,
            [(got, VM), (a, STAY), (old_w, VM), (k, STAY), (lt, ANY)],
            6,
            flops=2 * cells,
            nbytes=4 * cells,
        )
        columns = over_old(columns)
        if step + 1 < ITERS:
            (msg,) = call(
                functools.partial(row_kernel, n_old),
                [((n_new, 2 * wide, LANES), F32, False)],
                [pltpu.VMEM((tall, LANES), F32)] * 2
                + [pltpu.VMEM((2 * wide, LANES), F32)]
                + chunk,
                [(c, VM) for c in columns]
                + [(new_w, VM), (a, STAY), (k, STAY), (lt, ANY)],
                6,
                flops=2 * cells,
                nbytes=4 * cells,
            )
    g, plan, mass = call(
        functools.partial(plan_kernel, n_old),
        [
            ((tall, LANES), F32, False),
            ((height, width), BF16, True),
            ((wide, LANES), F32, False),
        ],
        [],
        [(c, VM) for c in columns] + [(new_w, VM), (f_near, STAY), (lt, STAY)],
        6,
        flops=2 * cells,
        nbytes=6 * cells,
        exps=cells,
    )
    if tuned:
        r = depth // n_new

        def old_part(base, dtype, cuts):
            return call(
                functools.partial(old_terms_kernel, cuts, base),
                [((r, width // cut), dtype, False) for cut in cuts for _ in range(cut)],
                [pltpu.VMEM((len(cuts) * r, height), BF16)],
                [(where, SM), (new_full, STAY), (plan, STAY)],
                16,
                flops=2 * cells * r * len(cuts),
                nbytes=2 * cells,
            )

        away = old_part(held, BF16, (2, 1, 1, 1))
        away = [away[:2], *away[2:]]
        for d in (1, 2, 4):
            mass = mass + swap(mass, NEW, 8, d, None)
        own = old_part(held + 4, F32, (2, 2, 1, 2))
        own = [own[:2], own[2:4], own[4:5], own[5:]]
        old_sums = scatter_old(away, own)
        q = depth // n_old

        def new_part(base, dtype):
            return call(
                functools.partial(new_terms_kernel, base, 4),
                [((2, q, height), dtype, False)],
                [pltpu.VMEM((2 * q, width), BF16)],
                [(where, SM), (old_full, STAY), (plan, STAY)],
                16,
                flops=cells * depth,
                nbytes=2 * cells,
            )[0]

        far = swap(new_part(held + 8, BF16), OLD, 4, 2, None)
        near = new_part(held + 12, F32) + far.astype(F32)
        core = swap(near[1].astype(BF16), OLD, 4, 1, None)
        new_sums = near[0] + core.astype(F32)
    else:
        mass = lax.psum(mass, NEW)
        old_terms = jnp.dot(new_full, plan, preferred_element_type=F32)
        new_terms = lax.dot_general(
            old_full, plan, (((1,), (1,)), ((), ())), preferred_element_type=F32
        )
        old_sums = lax.psum_scatter(old_terms, NEW, scatter_dimension=0, tiled=True)
        new_sums = lax.psum_scatter(new_terms, OLD, scatter_dimension=0, tiled=True)
    old_map = old_sums / mass.reshape(width)[None, :]
    new_map = new_sums / jnp.exp(new_logw)[None, :]
    return (f.reshape(width), g.reshape(height), old_map, new_map)


def solution(mesh):
    in_specs = (P(NEW, OLD), P(OLD, NEW), P(OLD), P(NEW))
    out_specs = (P(OLD), P(NEW), P(NEW, OLD), P(OLD, NEW))
    n_old, n_new = mesh.shape[OLD], mesh.shape[NEW]
    return jax.shard_map(
        functools.partial(per_device, n_old, n_new),
        mesh=mesh,
        in_specs=in_specs,
        out_specs=out_specs,
        check_vma=False,
    )
```

```python
import functools
import math

import jax
import jax.numpy as jnp
from jax import lax
from jax.experimental import pallas as pl
from jax.experimental.pallas import tpu as pltpu
from jax.sharding import PartitionSpec as P

ITERS = 3
EPSILON = 0.5
LANES = 128
SAFE = 1e-20
BF16 = jnp.bfloat16
F32 = jnp.float32
OLD, NEW = "old", "new"
MIB = 2**20
STAY, VM, SM, ANY = range(4)


def call(kernel, outs, scratch, args, limit, flops=0, nbytes=0, exps=0, aliases=None):
    out_shape, arrays, in_specs = [], [], []
    for shape, dtype, resident in outs:
        out_shape.append(
            pltpu.VMEM(shape, dtype) if resident else jax.ShapeDtypeStruct(shape, dtype)
        )
    for array, where in args:
        if where == STAY:
            array = pltpu.with_memory_space_constraint(array, pltpu.VMEM)
        arrays.append(array)
        space = {SM: pltpu.SMEM, ANY: pl.ANY}.get(where, pltpu.VMEM)
        in_specs.append(pl.BlockSpec(memory_space=space))
    return pl.pallas_call(
        kernel,
        out_shape=tuple(out_shape),
        in_specs=in_specs,
        out_specs=tuple(pl.BlockSpec(memory_space=pltpu.VMEM) for _ in outs),
        scratch_shapes=scratch,
        input_output_aliases=aliases or {},
        compiler_params=pltpu.CompilerParams(vmem_limit_bytes=limit * MIB),
        cost_estimate=pl.CostEstimate(flops=flops, bytes_accessed=nbytes, transcendentals=exps),
    )(*arrays)


def diagonal():
    shape = (LANES, LANES)
    return lax.broadcasted_iota(jnp.int32, shape, 0) == lax.broadcasted_iota(jnp.int32, shape, 1)


def to_column(row8, eye):
    rows = jnp.concatenate([row8] * (LANES // 8), axis=0)
    return jnp.sum(jnp.where(eye, rows, 0.0), axis=1, keepdims=True)


def to_row(column, eye):
    return jnp.sum(jnp.where(eye, column, 0.0), axis=0, keepdims=True)


def folded(tile, op):
    return op(tile.reshape(LANES // 8, 8, LANES), axis=0)


def repeated(ref, row):
    return ref[pl.ds(row, 8, stride=0), :]


def spread(row8):
    return jnp.concatenate([row8] * (LANES // 8), axis=0)


def stack_slots(slots, out_ref, row=0):
    for slot in slots:
        column = 0
        for piece in slot:
            r, w = piece.shape
            out_ref[row : row + r, column : column + w] = piece[...]
            column += w
        row += r


def grouped(refs, counts):
    return [refs[sum(counts[:p]) : sum(counts[: p + 1])] for p in range(len(counts))]


def prepare_kernel(n_slots, where_ref, *refs):
    new_refs, (nt_ref, nf_ref, ns_ref) = refs[:-3], refs[-3:]
    depth, rows = nf_ref.shape
    for p, piece in enumerate(new_refs):
        r = piece.shape[0]
        start = pl.multiple_of(where_ref[n_slots + p] * r, r)
        nf_ref[pl.ds(start, r), :] = piece[...]
    r = depth // n_slots
    for p in range(n_slots):
        ns_ref[p * r : (p + 1) * r, :] = nf_ref[pl.ds(pl.multiple_of(where_ref[p] * r, r), r), :]
    for c in range(rows // LANES):
        nt_ref[c * LANES : (c + 1) * LANES, :] = ns_ref[:, c * LANES : (c + 1) * LANES].T


def logits_kernel(counts, scale, devices, nt_ref, *refs):
    slots, refs = grouped(refs, counts), refs[sum(counts) :]
    lt_ref, k_ref, of_ref, a_ref, msg_ref, m_ref = refs
    columns = of_ref.shape[1]
    rows = nt_ref.shape[0]
    stack_slots(slots, of_ref)
    wide = 2 * LANES
    blocks = columns // wide

    def product(b):
        at = pl.ds(pl.multiple_of(b * wide, wide), wide)
        lt_ref[:, at] = jnp.dot(nt_ref[...], of_ref[:, at], preferred_element_type=F32) * scale

    def exponentials(b):
        for t in range(2):
            lane = pl.ds(pl.multiple_of(b * wide + t * LANES, LANES), LANES)
            top = jnp.full((8, LANES), -jnp.inf, F32)
            for j in range(rows // LANES):
                top = jnp.maximum(top, folded(lt_ref[j * LANES : (j + 1) * LANES, lane], jnp.max))
            top = jnp.max(top, axis=0, keepdims=True)
            a_ref[pl.ds(2 * b + t, 1), :] = top
            m_ref[pl.ds(2 * b + t, 1), :] = top
            high = spread(jnp.broadcast_to(top, (8, LANES)))
            total = jnp.zeros((8, LANES), F32)
            for j in range(rows // LANES):
                tile = jnp.exp(lt_ref[j * LANES : (j + 1) * LANES, lane] - high)
                k_ref[j * LANES : (j + 1) * LANES, lane] = tile
                total = total + folded(tile, jnp.sum)
            m_ref[pl.ds(2 * blocks + 2 * b + t, 1), :] = jnp.sum(total, axis=0, keepdims=True)

    product(0)

    def block(b, carry):
        product(b)
        exponentials(b - 1)
        return carry

    lax.fori_loop(1, blocks, block, 0)
    exponentials(blocks - 1)
    for d in range(devices):
        msg_ref[d] = m_ref[...]


def combine(parts):
    peak = functools.reduce(jnp.maximum, [m for m, _ in parts])
    sums = [s * jnp.exp(m - peak) for m, s in parts]
    while len(sums) > 1:
        sums = [sums[i] + sums[i + 1] for i in range(0, len(sums), 2)]
    return peak + jnp.log(sums[0])


def column_kernel(got_ref, a_ref, logw_ref, k_ref, lt_hbm, f_ref, near_ref, msg_ref, w_ref, chunk_ref, sem):
    wide = a_ref.shape[0]
    tall = k_ref.shape[0] // LANES
    got = [(got_ref[d, :wide, :], got_ref[d, wide:, :]) for d in range(got_ref.shape[0])]
    f = logw_ref[...] - combine(got)
    f_ref[...] = f
    near_ref[...] = f
    fa = f + a_ref[...]
    high = jnp.max(jnp.max(fa, axis=1, keepdims=True), axis=0, keepdims=True)
    w_ref[...] = jnp.exp(fa - high)
    eye = diagonal()

    least = jnp.full((1, LANES), jnp.inf, F32)
    for j in range(tall):
        acc = jnp.zeros((LANES // 8, 8, LANES), F32)
        for c in range(wide):
            tile = k_ref[j * LANES : (j + 1) * LANES, c * LANES : (c + 1) * LANES]
            acc = acc + tile.reshape(LANES // 8, 8, LANES) * repeated(w_ref, c)[None]
        total = to_row(jnp.sum(acc.reshape(LANES, LANES), axis=1, keepdims=True), eye)
        msg_ref[tall + j : tall + j + 1, :] = total
        least = jnp.minimum(least, total)
    msg_ref[:tall, :] = jnp.broadcast_to(high, (tall, LANES))

    @pl.when(jnp.logical_not(jnp.min(least) > SAFE))
    def _():
        def exact(j, carry):
            at = pl.ds(pl.multiple_of(j * LANES, LANES), LANES)
            copy = pltpu.make_async_copy(lt_hbm.at[at, :], chunk_ref, sem)
            copy.start()
            copy.wait()
            top = jnp.full((LANES, LANES), -jnp.inf, F32)
            for c in range(wide):
                lane = slice(c * LANES, (c + 1) * LANES)
                shifted = chunk_ref[:, lane] + spread(repeated(f_ref, c))
                chunk_ref[:, lane] = shifted
                top = jnp.maximum(top, shifted)
            top = jnp.max(top, axis=1, keepdims=True)
            acc = jnp.zeros((LANES, LANES), F32)
            for c in range(wide):
                acc = acc + jnp.exp(chunk_ref[:, c * LANES : (c + 1) * LANES] - top)
            msg_ref[pl.ds(j, 1), :] = to_row(top, eye)
            msg_ref[pl.ds(tall + j, 1), :] = to_row(jnp.sum(acc, axis=1, keepdims=True), eye)
            return carry

        lax.fori_loop(0, tall, exact, 0)


def row_kernel(n_got, *refs):
    got_refs, refs = refs[:n_got], refs[n_got:]
    logw_ref, a_ref, k_ref, lt_hbm, msg_ref, g_ref, v_ref, m_ref, chunk_ref, sem = refs
    wide = a_ref.shape[0]
    tall = k_ref.shape[0] // LANES
    g = logw_ref[...] - combine([(r[:tall, :], r[tall:, :]) for r in got_refs])
    g_ref[...] = g
    high = jnp.max(jnp.max(g, axis=1, keepdims=True), axis=0, keepdims=True)
    v_ref[...] = jnp.exp(g - high)
    eye = diagonal()

    acc = [jnp.zeros((8, LANES), F32)] * wide
    for j in range(tall):
        v = to_column(repeated(v_ref, j), eye)
        for c in range(wide):
            tile = k_ref[j * LANES : (j + 1) * LANES, c * LANES : (c + 1) * LANES]
            acc[c] = acc[c] + folded(tile * v, jnp.sum)
    m_ref[:wide, :] = a_ref[...] + high
    least = jnp.full((1, LANES), jnp.inf, F32)
    for c in range(wide):
        total = jnp.sum(acc[c], axis=0, keepdims=True)
        m_ref[wide + c : wide + c + 1, :] = total
        least = jnp.minimum(least, total)

    @pl.when(jnp.logical_not(jnp.min(least) > SAFE))
    def _():
        m_ref[:wide, :] = jnp.full((wide, LANES), -jnp.inf, F32)
        m_ref[wide:, :] = jnp.zeros((wide, LANES), F32)

        def exact(j, carry):
            at = pl.ds(pl.multiple_of(j * LANES, LANES), LANES)
            copy = pltpu.make_async_copy(lt_hbm.at[at, :], chunk_ref, sem)
            copy.start()
            copy.wait()
            column = to_column(repeated(g_ref, j), eye)
            for c in range(wide):
                shifted = chunk_ref[:, c * LANES : (c + 1) * LANES] + column
                before = m_ref[c : c + 1, :]
                top = jnp.maximum(before, jnp.max(shifted, axis=0, keepdims=True))
                m_ref[c : c + 1, :] = top
                m_ref[wide + c : wide + c + 1, :] = m_ref[
                    wide + c : wide + c + 1, :
                ] * jnp.exp(before - top) + jnp.sum(jnp.exp(shifted - top), axis=0, keepdims=True)
            return carry

        lax.fori_loop(0, tall, exact, 0)

    for d in range(msg_ref.shape[0]):
        msg_ref[d] = m_ref[...]


def plan_kernel(n_got, *refs):
    got_refs, refs = refs[:n_got], refs[n_got:]
    logw_ref, f_ref, lt_ref, g_ref, p_ref, mass_ref = refs
    wide = f_ref.shape[0]
    tall = lt_ref.shape[0] // LANES
    g_ref[...] = logw_ref[...] - combine([(r[:tall, :], r[tall:, :]) for r in got_refs])
    eye = diagonal()

    def block(j, acc):
        at = pl.ds(pl.multiple_of(j * LANES, LANES), LANES)
        column = to_column(repeated(g_ref, j), eye)
        out = []
        for c in range(wide):
            lane = slice(c * LANES, (c + 1) * LANES)
            plan = jnp.exp(lt_ref[at, lane] + spread(repeated(f_ref, c)) + column)
            p_ref[at, lane] = plan.astype(BF16)
            out.append(acc[c] + folded(plan, jnp.sum))
        return tuple(out)

    acc = lax.fori_loop(0, tall, block, (jnp.zeros((8, LANES), F32),) * wide)
    for c in range(wide):
        mass_ref[c : c + 1, :] = jnp.sum(acc[c], axis=0, keepdims=True)


def old_terms_kernel(base, where_ref, nf_ref, p_ref, *refs):
    outs, lhs_ref = refs[:-1], refs[-1]
    blocks = len(outs) // 2
    r, half = outs[0].shape
    for k in range(blocks):
        lhs_ref[k * r : (k + 1) * r, :] = nf_ref[
            pl.ds(pl.multiple_of(where_ref[base + k] * r, r), r), :
        ]
    wide = 2 * LANES
    for h in range(2):

        def block(b, carry, h=h):
            at = pl.ds(pl.multiple_of(h * half + b * wide, wide), wide)
            here = pl.ds(pl.multiple_of(b * wide, wide), wide)
            got = jnp.dot(lhs_ref[...], p_ref[:, at], preferred_element_type=F32)
            for k in range(blocks):
                out = outs[2 * k + h]
                out[:, here] = got[k * r : (k + 1) * r, :].astype(out.dtype)
            return carry

        lax.fori_loop(0, half // wide, block, 0)


def new_terms_kernel(base, pieces, where_ref, of_ref, p_ref, out_ref, lhs_ref):
    blocks, q, w = out_ref.shape
    r = blocks * q // pieces
    for k in range(pieces):
        lhs_ref[k * r : (k + 1) * r, :] = of_ref[
            pl.ds(pl.multiple_of(where_ref[base + k] * r, r), r), :
        ]
    wide = 2 * LANES

    def block(b, carry):
        at = pl.ds(pl.multiple_of(b * wide, wide), wide)
        got = lax.dot_general(
            lhs_ref[...], p_ref[at, :], (((1,), (1,)), ((), ())), preferred_element_type=F32
        )
        for k in range(blocks):
            out_ref[k, :, at] = got[k * q : (k + 1) * q, :].astype(out_ref.dtype)
        return carry

    lax.fori_loop(0, w // wide, block, 0)


def swap(x, axis, size, mask, only=None):
    return lax.ppermute(x, axis, [(i, i ^ mask) for i in range(size) if only is None or only(i)])


def position(n):
    return (n // 2) + (n % 2) * (7 - 2 * (n // 2))


def device_at(p):
    p = p % 8
    return 2 * p - (p // 4) * (4 * p - 15)


def turn(x, step):
    return lax.ppermute(x, NEW, [(i, device_at(position(i) + step)) for i in range(8)])


def halves(x):
    width = x.shape[1] // 2
    return [x[:, :width], x[:, width:]]


def gather_old(x):
    up, down = halves(x), halves(x)
    behind, ahead, opposite = [], [], [None, None]
    for hop in (1, 2, 3, 4):
        for h in (0, 1):
            if hop < 4 or h == 0:
                up[h] = turn(up[h], 1)
            if hop < 4 or h == 1:
                down[h] = turn(down[h], -1)
        if hop < 4:
            behind.append(list(up))
            ahead.append(list(down))
    opposite = [up[0], down[1]]
    return [[x], *ahead, opposite, *behind[::-1]]


def gather_new(x):
    pair = jnp.stack([x, swap(x, OLD, 4, 2, None)])
    other = swap(pair, OLD, 4, 1, None)
    return [pair[0], pair[1], other[0], other[1]]


def scatter_old(far, near):
    four, up3, down3 = far
    up = {3: up3, 2: near[0], 1: near[2]}
    down = {3: down3, 2: near[1], 1: near[3]}
    sums = list(near[4])
    for h in (0, 1):
        for blocks, step, start in ((up, 1, 4 - h), (down, -1, 3 + h)):
            x = four[h] if start == 4 else blocks[3][h]
            for hop in range(start, 0, -1):
                x = turn(x.astype(BF16), step).astype(F32)
                if hop > 1:
                    x = blocks[hop - 1][h] + x
            sums[h] = sums[h] + x
    return jnp.concatenate(sums, axis=1)


def integers(values):
    return jnp.stack([jnp.asarray(v, jnp.int32) for v in values])


def is_tuned(n_old, n_new):
    return (n_old, n_new) == (4, 8)


def per_device(n_old, n_new, old_emb, new_emb, old_logw, new_logw):
    tuned = is_tuned(n_old, n_new)
    width, height = old_logw.shape[0], new_logw.shape[0]
    wide, tall = width // LANES, height // LANES
    depth = old_emb.shape[0] * n_new
    scale = 1.0 / (math.sqrt(depth) * EPSILON)
    if tuned:
        old_slots, new_slots = gather_old(old_emb), gather_new(new_emb)
        p, me = position(lax.axis_index(NEW)), lax.axis_index(OLD)
        owners = [device_at(p + i) for i in range(8)] + [me, me ^ 2, me ^ 1, me ^ 3]
    else:
        old_all = lax.all_gather(old_emb, NEW, axis=0, tiled=True)
        old_slots = [[old_all[: depth // 2]], [old_all[depth // 2 :]]]
        new_slots = [lax.all_gather(new_emb, OLD, axis=0, tiled=True)]
        owners = [0, 1, 0]
    held = len(owners)
    if tuned:
        owners = owners + [device_at(p + i) for i in (4, 3, -3, 2, -2, 1, -1, 0)]
        for o in (me ^ 2, me ^ 3, me, me ^ 1):
            owners = owners + [(position(2 * o + i) - p) % 8 for i in (0, 1)]
    where = integers(owners)
    old_w = old_logw.reshape(wide, LANES)
    new_w = new_logw.reshape(tall, LANES)
    cells = width * height
    n_slots = len(old_slots)
    new_rows, new_full = call(
        functools.partial(prepare_kernel, n_slots),
        [((height, depth), BF16, True), ((depth, height), BF16, True)],
        [pltpu.VMEM((depth, height), BF16)],
        [(where, SM)] + [(x, VM) for x in new_slots],
        8,
        flops=cells,
        nbytes=8 * depth * height,
    )
    lt, k, old_full, a, msg = call(
        functools.partial(logits_kernel, [len(slot) for slot in old_slots], scale, n_new),
        [
            ((height, width), F32, True),
            ((height, width), F32, True),
            ((depth, width), BF16, True),
            ((wide, LANES), F32, True),
            ((n_new, 2 * wide, LANES), F32, False),
        ],
        [pltpu.VMEM((2 * wide, LANES), F32)],
        [(new_rows, STAY)] + [(x, VM) for slot in old_slots for x in slot],
        8,
        flops=2 * cells * depth,
        nbytes=12 * cells,
        exps=cells,
    )

    def over_old(message):
        return [message] + [swap(message, OLD, n_old, d) for d in range(1, n_old)]

    chunk = [pltpu.VMEM((LANES, width), F32), pltpu.SemaphoreType.DMA]
    for step in range(ITERS):
        got = lax.all_to_all(msg, NEW, 0, 0, tiled=True)
        f, f_near, columns = call(
            column_kernel,
            [((wide, LANES), F32, False), ((wide, LANES), F32, True), ((2 * tall, LANES), F32, False)],
            [pltpu.VMEM((wide, LANES), F32)] + chunk,
            [(got, VM), (a, STAY), (old_w, VM), (k, STAY), (lt, ANY)],
            6,
            flops=2 * cells,
            nbytes=4 * cells,
        )
        columns = over_old(columns)
        if step + 1 < ITERS:
            (msg,) = call(
                functools.partial(row_kernel, n_old),
                [((n_new, 2 * wide, LANES), F32, False)],
                [pltpu.VMEM((tall, LANES), F32)] * 2
                + [pltpu.VMEM((2 * wide, LANES), F32)]
                + chunk,
                [(c, VM) for c in columns]
                + [(new_w, VM), (a, STAY), (k, STAY), (lt, ANY)],
                6,
                flops=2 * cells,
                nbytes=4 * cells,
            )
    g, plan, mass = call(
        functools.partial(plan_kernel, n_old),
        [
            ((tall, LANES), F32, False),
            ((height, width), BF16, True),
            ((wide, LANES), F32, False),
        ],
        [],
        [(c, VM) for c in columns] + [(new_w, VM), (f_near, STAY), (lt, STAY)],
        6,
        flops=2 * cells,
        nbytes=6 * cells,
        exps=cells,
    )
    if tuned:
        r = depth // n_new

        def old_part(base, types):
            got = call(
                functools.partial(old_terms_kernel, base),
                [((r, width // 2), dtype, False) for dtype in types],
                [pltpu.VMEM((len(types) // 2 * r, height), BF16)],
                [(where, SM), (new_full, STAY), (plan, STAY)],
                16,
                flops=cells * r * len(types),
                nbytes=2 * cells,
            )
            return [got[i : i + 2] for i in range(0, len(got), 2)]

        far = old_part(held, (BF16, BF16, F32, BF16, BF16, F32))
        for d in (1, 2, 4):
            mass = mass + swap(mass, NEW, 8, d, None)
        old_sums = scatter_old(far, old_part(held + 3, (F32,) * 10))
        q = depth // n_old

        def new_part(base, dtype):
            return call(
                functools.partial(new_terms_kernel, base, 4),
                [((2, q, height), dtype, False)],
                [pltpu.VMEM((2 * q, width), BF16)],
                [(where, SM), (old_full, STAY), (plan, STAY)],
                16,
                flops=cells * depth,
                nbytes=2 * cells,
            )[0]

        far = swap(new_part(held + 8, BF16), OLD, 4, 2, None)
        near = new_part(held + 12, F32) + far.astype(F32)
        core = swap(near[1].astype(BF16), OLD, 4, 1, None)
        new_sums = near[0] + core.astype(F32)
    else:
        mass = lax.psum(mass, NEW)
        old_terms = jnp.dot(new_full, plan, preferred_element_type=F32)
        new_terms = lax.dot_general(
            old_full, plan, (((1,), (1,)), ((), ())), preferred_element_type=F32
        )
        old_sums = lax.psum_scatter(old_terms, NEW, scatter_dimension=0, tiled=True)
        new_sums = lax.psum_scatter(new_terms, OLD, scatter_dimension=0, tiled=True)
    old_map = old_sums / mass.reshape(width)[None, :]
    new_map = new_sums / jnp.exp(new_logw)[None, :]
    return (f.reshape(width), g.reshape(height), old_map, new_map)


def solution(mesh):
    in_specs = (P(NEW, OLD), P(OLD, NEW), P(OLD), P(NEW))
    out_specs = (P(OLD), P(NEW), P(NEW, OLD), P(OLD, NEW))
    n_old, n_new = mesh.shape[OLD], mesh.shape[NEW]
    return jax.shard_map(
        functools.partial(per_device, n_old, n_new),
        mesh=mesh,
        in_specs=in_specs,
        out_specs=out_specs,
        check_vma=False,
    )
```

```python
import functools
import math

import jax
import jax.numpy as jnp
from jax import lax
from jax.experimental import pallas as pl
from jax.experimental.pallas import tpu as pltpu
from jax.sharding import PartitionSpec as P

ITERS = 3
EPSILON = 0.5
LANES = 128
SAFE = 1e-20
BF16 = jnp.bfloat16
F32 = jnp.float32
OLD, NEW = "old", "new"
MIB = 2**20
STAY, VM, SM, ANY = range(4)


def call(kernel, outs, scratch, args, limit, flops=0, nbytes=0, exps=0, aliases=None):
    out_shape, arrays, in_specs = [], [], []
    for shape, dtype, resident in outs:
        out_shape.append(
            pltpu.VMEM(shape, dtype) if resident else jax.ShapeDtypeStruct(shape, dtype)
        )
    for array, where in args:
        if where == STAY:
            array = pltpu.with_memory_space_constraint(array, pltpu.VMEM)
        arrays.append(array)
        space = {SM: pltpu.SMEM, ANY: pl.ANY}.get(where, pltpu.VMEM)
        in_specs.append(pl.BlockSpec(memory_space=space))
    return pl.pallas_call(
        kernel,
        out_shape=tuple(out_shape),
        in_specs=in_specs,
        out_specs=tuple(pl.BlockSpec(memory_space=pltpu.VMEM) for _ in outs),
        scratch_shapes=scratch,
        input_output_aliases=aliases or {},
        compiler_params=pltpu.CompilerParams(vmem_limit_bytes=limit * MIB),
        cost_estimate=pl.CostEstimate(flops=flops, bytes_accessed=nbytes, transcendentals=exps),
    )(*arrays)


def diagonal():
    shape = (LANES, LANES)
    return lax.broadcasted_iota(jnp.int32, shape, 0) == lax.broadcasted_iota(jnp.int32, shape, 1)


def to_column(row8, eye):
    rows = jnp.concatenate([row8] * (LANES // 8), axis=0)
    return jnp.sum(jnp.where(eye, rows, 0.0), axis=1, keepdims=True)


def to_row(column, eye):
    return jnp.sum(jnp.where(eye, column, 0.0), axis=0, keepdims=True)


def folded(tile, op):
    return op(tile.reshape(LANES // 8, 8, LANES), axis=0)


def repeated(ref, row):
    return ref[pl.ds(row, 8, stride=0), :]


def spread(row8):
    return jnp.concatenate([row8] * (LANES // 8), axis=0)


def stack_slots(slots, out_ref, row=0):
    for slot in slots:
        column = 0
        for piece in slot:
            r, w = piece.shape
            out_ref[row : row + r, column : column + w] = piece[...]
            column += w
        row += r


def grouped(refs, counts):
    return [refs[sum(counts[:p]) : sum(counts[: p + 1])] for p in range(len(counts))]


def prepare_kernel(n_slots, where_ref, *refs):
    new_refs, (nt_ref, nf_ref, ns_ref) = refs[:-3], refs[-3:]
    depth, rows = nf_ref.shape
    for p, piece in enumerate(new_refs):
        r = piece.shape[0]
        start = pl.multiple_of(where_ref[n_slots + p] * r, r)
        nf_ref[pl.ds(start, r), :] = piece[...]
    r = depth // n_slots
    for p in range(n_slots):
        ns_ref[p * r : (p + 1) * r, :] = nf_ref[pl.ds(pl.multiple_of(where_ref[p] * r, r), r), :]
    for c in range(rows // LANES):
        nt_ref[c * LANES : (c + 1) * LANES, :] = ns_ref[:, c * LANES : (c + 1) * LANES].T


def logits_kernel(counts, scale, nt_ref, *refs):
    slots, refs = grouped(refs, counts), refs[sum(counts) :]
    lt_ref, k_ref, of_ref, a_ref, msg_ref, m_ref = refs
    columns = of_ref.shape[1]
    rows = nt_ref.shape[0]
    stack_slots(slots, of_ref)
    wide = 2 * LANES
    blocks = columns // wide

    def product(b):
        at = pl.ds(pl.multiple_of(b * wide, wide), wide)
        lt_ref[:, at] = jnp.dot(nt_ref[...], of_ref[:, at], preferred_element_type=F32) * scale

    def exponentials(b):
        for t in range(2):
            lane = pl.ds(pl.multiple_of(b * wide + t * LANES, LANES), LANES)
            top = jnp.full((8, LANES), -jnp.inf, F32)
            for j in range(rows // LANES):
                top = jnp.maximum(top, folded(lt_ref[j * LANES : (j + 1) * LANES, lane], jnp.max))
            top = jnp.max(top, axis=0, keepdims=True)
            a_ref[pl.ds(2 * b + t, 1), :] = top
            m_ref[pl.ds(2 * b + t, 1), :] = top
            high = spread(jnp.broadcast_to(top, (8, LANES)))
            total = jnp.zeros((8, LANES), F32)
            for j in range(rows // LANES):
                tile = jnp.exp(lt_ref[j * LANES : (j + 1) * LANES, lane] - high)
                k_ref[j * LANES : (j + 1) * LANES, lane] = tile
                total = total + folded(tile, jnp.sum)
            m_ref[pl.ds(2 * blocks + 2 * b + t, 1), :] = jnp.sum(total, axis=0, keepdims=True)

    product(0)

    def block(b, carry):
        product(b)
        exponentials(b - 1)
        return carry

    lax.fori_loop(1, blocks, block, 0)
    exponentials(blocks - 1)
    put_message(msg_ref, m_ref)


def put_message(msg_ref, m_ref):
    if len(msg_ref.shape) == 2:
        msg_ref[...] = m_ref[...]
    else:
        for d in range(msg_ref.shape[0]):
            msg_ref[d] = m_ref[...]


def combine(parts):
    peak = functools.reduce(jnp.maximum, [m for m, _ in parts])
    sums = [s * jnp.exp(m - peak) for m, s in parts]
    while len(sums) > 1:
        sums = [sums[i] + sums[i + 1] for i in range(0, len(sums), 2)]
    return peak + jnp.log(sums[0])


def column_kernel(n_got, *refs):
    got_refs, refs = refs[:n_got], refs[n_got:]
    a_ref, logw_ref, k_ref, lt_hbm, f_ref, near_ref, msg_ref, w_ref, chunk_ref, sem = refs
    wide = a_ref.shape[0]
    tall = k_ref.shape[0] // LANES
    got = []
    for ref in got_refs:
        views = [ref] if len(ref.shape) == 2 else [ref.at[d] for d in range(ref.shape[0])]
        got += [(view[:wide, :], view[wide:, :]) for view in views]
    f = logw_ref[...] - combine(got)
    f_ref[...] = f
    near_ref[...] = f
    fa = f + a_ref[...]
    high = jnp.max(jnp.max(fa, axis=1, keepdims=True), axis=0, keepdims=True)
    w_ref[...] = jnp.exp(fa - high)
    eye = diagonal()

    least = jnp.full((1, LANES), jnp.inf, F32)
    for j in range(tall):
        acc = jnp.zeros((LANES // 8, 8, LANES), F32)
        for c in range(wide):
            tile = k_ref[j * LANES : (j + 1) * LANES, c * LANES : (c + 1) * LANES]
            acc = acc + tile.reshape(LANES // 8, 8, LANES) * repeated(w_ref, c)[None]
        total = to_row(jnp.sum(acc.reshape(LANES, LANES), axis=1, keepdims=True), eye)
        msg_ref[tall + j : tall + j + 1, :] = total
        least = jnp.minimum(least, total)
    msg_ref[:tall, :] = jnp.broadcast_to(high, (tall, LANES))

    @pl.when(jnp.logical_not(jnp.min(least) > SAFE))
    def _():
        def exact(j, carry):
            at = pl.ds(pl.multiple_of(j * LANES, LANES), LANES)
            copy = pltpu.make_async_copy(lt_hbm.at[at, :], chunk_ref, sem)
            copy.start()
            copy.wait()
            top = jnp.full((LANES, LANES), -jnp.inf, F32)
            for c in range(wide):
                lane = slice(c * LANES, (c + 1) * LANES)
                shifted = chunk_ref[:, lane] + spread(repeated(f_ref, c))
                chunk_ref[:, lane] = shifted
                top = jnp.maximum(top, shifted)
            top = jnp.max(top, axis=1, keepdims=True)
            acc = jnp.zeros((LANES, LANES), F32)
            for c in range(wide):
                acc = acc + jnp.exp(chunk_ref[:, c * LANES : (c + 1) * LANES] - top)
            msg_ref[pl.ds(j, 1), :] = to_row(top, eye)
            msg_ref[pl.ds(tall + j, 1), :] = to_row(jnp.sum(acc, axis=1, keepdims=True), eye)
            return carry

        lax.fori_loop(0, tall, exact, 0)


def row_kernel(n_got, *refs):
    got_refs, refs = refs[:n_got], refs[n_got:]
    logw_ref, a_ref, k_ref, lt_hbm, msg_ref, g_ref, v_ref, m_ref, chunk_ref, sem = refs
    wide = a_ref.shape[0]
    tall = k_ref.shape[0] // LANES
    g = logw_ref[...] - combine([(r[:tall, :], r[tall:, :]) for r in got_refs])
    g_ref[...] = g
    high = jnp.max(jnp.max(g, axis=1, keepdims=True), axis=0, keepdims=True)
    v_ref[...] = jnp.exp(g - high)
    eye = diagonal()

    acc = [jnp.zeros((8, LANES), F32)] * wide
    for j in range(tall):
        v = to_column(repeated(v_ref, j), eye)
        for c in range(wide):
            tile = k_ref[j * LANES : (j + 1) * LANES, c * LANES : (c + 1) * LANES]
            acc[c] = acc[c] + folded(tile * v, jnp.sum)
    m_ref[:wide, :] = a_ref[...] + high
    least = jnp.full((1, LANES), jnp.inf, F32)
    for c in range(wide):
        total = jnp.sum(acc[c], axis=0, keepdims=True)
        m_ref[wide + c : wide + c + 1, :] = total
        least = jnp.minimum(least, total)

    @pl.when(jnp.logical_not(jnp.min(least) > SAFE))
    def _():
        m_ref[:wide, :] = jnp.full((wide, LANES), -jnp.inf, F32)
        m_ref[wide:, :] = jnp.zeros((wide, LANES), F32)

        def exact(j, carry):
            at = pl.ds(pl.multiple_of(j * LANES, LANES), LANES)
            copy = pltpu.make_async_copy(lt_hbm.at[at, :], chunk_ref, sem)
            copy.start()
            copy.wait()
            column = to_column(repeated(g_ref, j), eye)
            for c in range(wide):
                shifted = chunk_ref[:, c * LANES : (c + 1) * LANES] + column
                before = m_ref[c : c + 1, :]
                top = jnp.maximum(before, jnp.max(shifted, axis=0, keepdims=True))
                m_ref[c : c + 1, :] = top
                m_ref[wide + c : wide + c + 1, :] = m_ref[
                    wide + c : wide + c + 1, :
                ] * jnp.exp(before - top) + jnp.sum(jnp.exp(shifted - top), axis=0, keepdims=True)
            return carry

        lax.fori_loop(0, tall, exact, 0)

    put_message(msg_ref, m_ref)


def plan_kernel(n_got, *refs):
    got_refs, refs = refs[:n_got], refs[n_got:]
    logw_ref, f_ref, lt_ref, g_ref, p_ref, mass_ref = refs
    wide = f_ref.shape[0]
    tall = lt_ref.shape[0] // LANES
    g_ref[...] = logw_ref[...] - combine([(r[:tall, :], r[tall:, :]) for r in got_refs])
    eye = diagonal()

    def block(j, acc):
        at = pl.ds(pl.multiple_of(j * LANES, LANES), LANES)
        column = to_column(repeated(g_ref, j), eye)
        out = []
        for c in range(wide):
            lane = slice(c * LANES, (c + 1) * LANES)
            plan = jnp.exp(lt_ref[at, lane] + spread(repeated(f_ref, c)) + column)
            p_ref[at, lane] = plan.astype(BF16)
            out.append(acc[c] + folded(plan, jnp.sum))
        return tuple(out)

    acc = lax.fori_loop(0, tall, block, (jnp.zeros((8, LANES), F32),) * wide)
    for c in range(wide):
        mass_ref[c : c + 1, :] = jnp.sum(acc[c], axis=0, keepdims=True)


def old_terms_kernel(base, where_ref, nf_ref, p_ref, *refs):
    outs, lhs_ref = refs[:-1], refs[-1]
    blocks = len(outs) // 2
    r, half = outs[0].shape
    for k in range(blocks):
        lhs_ref[k * r : (k + 1) * r, :] = nf_ref[
            pl.ds(pl.multiple_of(where_ref[base + k] * r, r), r), :
        ]
    wide = 2 * LANES
    for h in range(2):

        def block(b, carry, h=h):
            at = pl.ds(pl.multiple_of(h * half + b * wide, wide), wide)
            here = pl.ds(pl.multiple_of(b * wide, wide), wide)
            got = jnp.dot(lhs_ref[...], p_ref[:, at], preferred_element_type=F32)
            for k in range(blocks):
                out = outs[2 * k + h]
                out[:, here] = got[k * r : (k + 1) * r, :].astype(out.dtype)
            return carry

        lax.fori_loop(0, half // wide, block, 0)


def new_terms_kernel(base, pieces, where_ref, of_ref, p_ref, away_ref, own_ref, lhs_ref):
    blocks, q, w = own_ref.shape
    r = lhs_ref.shape[0] // pieces
    for k in range(pieces):
        lhs_ref[k * r : (k + 1) * r, :] = of_ref[
            pl.ds(pl.multiple_of(where_ref[base + k] * r, r), r), :
        ]
    wide = 2 * LANES

    def block(b, carry):
        at = pl.ds(pl.multiple_of(b * wide, wide), wide)
        got = lax.dot_general(
            lhs_ref[...], p_ref[at, :], (((1,), (1,)), ((), ())), preferred_element_type=F32
        )
        for i, out_ref in enumerate((away_ref, own_ref)):
            for k in range(blocks):
                row = (i * blocks + k) * q
                out_ref[k, :, at] = got[row : row + q, :].astype(out_ref.dtype)
        return carry

    lax.fori_loop(0, w // wide, block, 0)


def swap(x, axis, size, mask, only=None):
    return lax.ppermute(x, axis, [(i, i ^ mask) for i in range(size) if only is None or only(i)])


def position(n):
    return (n // 2) + (n % 2) * (7 - 2 * (n // 2))


def device_at(p):
    p = p % 8
    return 2 * p - (p // 4) * (4 * p - 15)


def turn(x, step):
    return lax.ppermute(x, NEW, [(i, device_at(position(i) + step)) for i in range(8)])


def halves(x):
    width = x.shape[1] // 2
    return [x[:, :width], x[:, width:]]


def gather_old(x):
    up, down = halves(x), halves(x)
    behind, ahead, opposite = [], [], [None, None]
    for hop in (1, 2, 3, 4):
        for h in (0, 1):
            if hop < 4 or h == 0:
                up[h] = turn(up[h], 1)
            if hop < 4 or h == 1:
                down[h] = turn(down[h], -1)
        if hop < 4:
            behind.append(list(up))
            ahead.append(list(down))
    opposite = [up[0], down[1]]
    return [[x], *ahead, opposite, *behind[::-1]]


def gather_new(x):
    across = swap(x, OLD, 4, 2, None)
    return [x, across, swap(x, OLD, 4, 1, None), swap(across, OLD, 4, 1, None)]


def scatter_old(far, near):
    four, up3, down3 = far
    up = {3: up3, 2: near[0], 1: near[2]}
    down = {3: down3, 2: near[1], 1: near[3]}
    sums = list(near[4])
    for h in (0, 1):
        for blocks, step, start in ((up, 1, 4 - h), (down, -1, 3 + h)):
            x = four[h] if start == 4 else blocks[3][h]
            for hop in range(start, 0, -1):
                x = turn(x.astype(BF16), step).astype(F32)
                if hop > 1:
                    x = blocks[hop - 1][h] + x
            sums[h] = sums[h] + x
    return sums


def integers(values):
    return jnp.stack([jnp.asarray(v, jnp.int32) for v in values])


def is_tuned(n_old, n_new):
    return (n_old, n_new) == (4, 8)


def per_device(n_old, n_new, old_emb, new_emb, old_logw, new_logw):
    tuned = is_tuned(n_old, n_new)
    width, height = old_logw.shape[0], new_logw.shape[0]
    wide, tall = width // LANES, height // LANES
    depth = old_emb.shape[0] * n_new
    scale = 1.0 / (math.sqrt(depth) * EPSILON)
    if tuned:
        old_slots, new_slots = gather_old(old_emb), gather_new(new_emb)
        p, me = position(lax.axis_index(NEW)), lax.axis_index(OLD)
        owners = [device_at(p + i) for i in range(8)] + [me, me ^ 2, me ^ 1, me ^ 3]
    else:
        old_all = lax.all_gather(old_emb, NEW, axis=0, tiled=True)
        old_slots = [[old_all[: depth // 2]], [old_all[depth // 2 :]]]
        new_slots = [lax.all_gather(new_emb, OLD, axis=0, tiled=True)]
        owners = [0, 1, 0]
    held = len(owners)
    if tuned:
        owners = owners + [device_at(p + i) for i in (4, 3, -3, 2, -2, 1, -1, 0)]
        for o in (me ^ 1, me ^ 3, me, me ^ 2):
            owners = owners + [(position(2 * o + i) - p) % 8 for i in (0, 1)]
    where = integers(owners)
    old_w = old_logw.reshape(wide, LANES)
    new_w = new_logw.reshape(tall, LANES)
    cells = width * height
    n_slots = len(old_slots)
    message = (2 * wide, LANES) if tuned else (n_new, 2 * wide, LANES)
    new_rows, new_full = call(
        functools.partial(prepare_kernel, n_slots),
        [((height, depth), BF16, True), ((depth, height), BF16, True)],
        [pltpu.VMEM((depth, height), BF16)],
        [(where, SM)] + [(x, VM) for x in new_slots],
        8,
        flops=cells,
        nbytes=8 * depth * height,
    )
    lt, k, old_full, a, msg = call(
        functools.partial(logits_kernel, [len(slot) for slot in old_slots], scale),
        [
            ((height, width), F32, True),
            ((height, width), F32, True),
            ((depth, width), BF16, True),
            ((wide, LANES), F32, True),
            (message, F32, False),
        ],
        [pltpu.VMEM((2 * wide, LANES), F32)],
        [(new_rows, STAY)] + [(x, VM) for slot in old_slots for x in slot],
        8,
        flops=2 * cells * depth,
        nbytes=12 * cells,
        exps=cells,
    )

    def over_new(message):
        if not tuned:
            return [lax.all_to_all(message, NEW, 0, 0, tiled=True)]
        other = swap(message, NEW, 8, 4)
        peak = jnp.maximum(message[:wide], other[:wide])
        total = sum(x[wide:] * jnp.exp(x[:wide] - peak) for x in (message, other))
        both = jnp.concatenate([peak, total], axis=0)
        return [both] + [swap(both, NEW, 8, d) for d in (1, 2, 3)]

    def over_old(message):
        return [message] + [swap(message, OLD, n_old, d) for d in range(1, n_old)]

    chunk = [pltpu.VMEM((LANES, width), F32), pltpu.SemaphoreType.DMA]
    for step in range(ITERS):
        got = over_new(msg)
        f, f_near, columns = call(
            functools.partial(column_kernel, len(got)),
            [((wide, LANES), F32, False), ((wide, LANES), F32, True), ((2 * tall, LANES), F32, False)],
            [pltpu.VMEM((wide, LANES), F32)] + chunk,
            [(x, VM) for x in got] + [(a, STAY), (old_w, VM), (k, STAY), (lt, ANY)],
            6,
            flops=2 * cells,
            nbytes=4 * cells,
        )
        columns = over_old(columns)
        if step + 1 < ITERS:
            (msg,) = call(
                functools.partial(row_kernel, n_old),
                [(message, F32, False)],
                [pltpu.VMEM((tall, LANES), F32)] * 2
                + [pltpu.VMEM((2 * wide, LANES), F32)]
                + chunk,
                [(c, VM) for c in columns]
                + [(new_w, VM), (a, STAY), (k, STAY), (lt, ANY)],
                6,
                flops=2 * cells,
                nbytes=4 * cells,
            )
    g, plan, mass = call(
        functools.partial(plan_kernel, n_old),
        [
            ((tall, LANES), F32, False),
            ((height, width), BF16, True),
            ((wide, LANES), F32, False),
        ],
        [],
        [(c, VM) for c in columns] + [(new_w, VM), (f_near, STAY), (lt, STAY)],
        6,
        flops=2 * cells,
        nbytes=6 * cells,
        exps=cells,
    )
    if tuned:
        r = depth // n_new

        def old_part(base, types):
            got = call(
                functools.partial(old_terms_kernel, base),
                [((r, width // 2), dtype, False) for dtype in types],
                [pltpu.VMEM((len(types) // 2 * r, height), BF16)],
                [(where, SM), (new_full, STAY), (plan, STAY)],
                16,
                flops=cells * r * len(types),
                nbytes=2 * cells,
            )
            return [got[i : i + 2] for i in range(0, len(got), 2)]

        far = old_part(held, (BF16, BF16, F32, BF16, BF16, F32))
        for d in (1, 2, 4):
            mass = mass + swap(mass, NEW, 8, d, None)
        old_sums = scatter_old(far, old_part(held + 3, (F32,) * 10))
        q = depth // n_old

        away, near = call(
            functools.partial(new_terms_kernel, held + 8, n_new),
            [((2, q, height), BF16, False), ((2, q, height), F32, False)],
            [pltpu.VMEM((depth, width), BF16)],
            [(where, SM), (old_full, STAY), (plan, STAY)],
            24,
            flops=2 * cells * depth,
            nbytes=4 * cells,
        )
        near = near + swap(away, OLD, 4, 1, None).astype(F32)
        new_sums = near[0] + swap(near[1].astype(BF16), OLD, 4, 2, None).astype(F32)
    else:
        mass = lax.psum(mass, NEW)
        old_terms = jnp.dot(new_full, plan, preferred_element_type=F32)
        new_terms = lax.dot_general(
            old_full, plan, (((1,), (1,)), ((), ())), preferred_element_type=F32
        )
        old_sums = lax.psum_scatter(old_terms, NEW, scatter_dimension=0, tiled=True)
        new_sums = lax.psum_scatter(new_terms, OLD, scatter_dimension=0, tiled=True)
    if tuned:
        masses = halves(mass.reshape(1, width))
        old_map = jnp.concatenate([x / y for x, y in zip(old_sums, masses)], axis=1)
    else:
        old_map = old_sums / mass.reshape(width)[None, :]
    new_map = new_sums / jnp.exp(new_logw)[None, :]
    return (f.reshape(width), g.reshape(height), old_map, new_map)


def solution(mesh):
    in_specs = (P(NEW, OLD), P(OLD, NEW), P(OLD), P(NEW))
    out_specs = (P(OLD), P(NEW), P(NEW, OLD), P(OLD, NEW))
    n_old, n_new = mesh.shape[OLD], mesh.shape[NEW]
    return jax.shard_map(
        functools.partial(per_device, n_old, n_new),
        mesh=mesh,
        in_specs=in_specs,
        out_specs=out_specs,
        check_vma=False,
    )
```

```python
import functools
import math

import jax
import jax.numpy as jnp
from jax import lax
from jax.experimental import pallas as pl
from jax.experimental.pallas import tpu as pltpu
from jax.sharding import PartitionSpec as P

ITERS = 3
EPSILON = 0.5
LANES = 128
SAFE = 1e-20
BF16 = jnp.bfloat16
F32 = jnp.float32
OLD, NEW = "old", "new"
MIB = 2**20
STAY, VM, SM, ANY = range(4)


def call(kernel, outs, scratch, args, limit, flops=0, nbytes=0, exps=0, aliases=None):
    out_shape, arrays, in_specs = [], [], []
    for shape, dtype, resident in outs:
        out_shape.append(
            pltpu.VMEM(shape, dtype) if resident else jax.ShapeDtypeStruct(shape, dtype)
        )
    for array, where in args:
        if where == STAY:
            array = pltpu.with_memory_space_constraint(array, pltpu.VMEM)
        arrays.append(array)
        space = {SM: pltpu.SMEM, ANY: pl.ANY}.get(where, pltpu.VMEM)
        in_specs.append(pl.BlockSpec(memory_space=space))
    return pl.pallas_call(
        kernel,
        out_shape=tuple(out_shape),
        in_specs=in_specs,
        out_specs=tuple(pl.BlockSpec(memory_space=pltpu.VMEM) for _ in outs),
        scratch_shapes=scratch,
        input_output_aliases=aliases or {},
        compiler_params=pltpu.CompilerParams(vmem_limit_bytes=limit * MIB),
        cost_estimate=pl.CostEstimate(flops=flops, bytes_accessed=nbytes, transcendentals=exps),
    )(*arrays)


def diagonal():
    shape = (LANES, LANES)
    return lax.broadcasted_iota(jnp.int32, shape, 0) == lax.broadcasted_iota(jnp.int32, shape, 1)


def to_column(row8, eye):
    rows = jnp.concatenate([row8] * (LANES // 8), axis=0)
    return jnp.sum(jnp.where(eye, rows, 0.0), axis=1, keepdims=True)


def to_row(column, eye):
    return jnp.sum(jnp.where(eye, column, 0.0), axis=0, keepdims=True)


def folded(tile, op):
    return op(tile.reshape(LANES // 8, 8, LANES), axis=0)


def repeated(ref, row):
    return ref[pl.ds(row, 8, stride=0), :]


def spread(row8):
    return jnp.concatenate([row8] * (LANES // 8), axis=0)


def stack_slots(slots, out_ref, row=0):
    for slot in slots:
        column = 0
        for piece in slot:
            r, w = piece.shape
            out_ref[row : row + r, column : column + w] = piece[...]
            column += w
        row += r


def grouped(refs, counts):
    return [refs[sum(counts[:p]) : sum(counts[: p + 1])] for p in range(len(counts))]


def prepare_kernel(n_slots, where_ref, *refs):
    new_refs, (nt_ref, nf_ref, ns_ref) = refs[:-3], refs[-3:]
    depth, rows = nf_ref.shape
    for p, piece in enumerate(new_refs):
        r = piece.shape[0]
        start = pl.multiple_of(where_ref[n_slots + p] * r, r)
        nf_ref[pl.ds(start, r), :] = piece[...]
    r = depth // n_slots
    for p in range(n_slots):
        ns_ref[p * r : (p + 1) * r, :] = nf_ref[pl.ds(pl.multiple_of(where_ref[p] * r, r), r), :]
    for c in range(rows // LANES):
        nt_ref[c * LANES : (c + 1) * LANES, :] = ns_ref[:, c * LANES : (c + 1) * LANES].T


def logits_kernel(counts, scale, nt_ref, *refs):
    slots, refs = grouped(refs, counts), refs[sum(counts) :]
    lt_ref, k_ref, of_ref, a_ref, msg_ref, m_ref = refs
    columns = of_ref.shape[1]
    rows = nt_ref.shape[0]
    stack_slots(slots, of_ref)
    wide = 2 * LANES
    blocks = columns // wide

    def product(b):
        at = pl.ds(pl.multiple_of(b * wide, wide), wide)
        lt_ref[:, at] = jnp.dot(nt_ref[...], of_ref[:, at], preferred_element_type=F32) * scale

    def exponentials(b):
        for t in range(2):
            lane = pl.ds(pl.multiple_of(b * wide + t * LANES, LANES), LANES)
            top = jnp.full((8, LANES), -jnp.inf, F32)
            for j in range(rows // LANES):
                top = jnp.maximum(top, folded(lt_ref[j * LANES : (j + 1) * LANES, lane], jnp.max))
            top = jnp.max(top, axis=0, keepdims=True)
            a_ref[pl.ds(2 * b + t, 1), :] = top
            m_ref[pl.ds(2 * b + t, 1), :] = top
            high = spread(jnp.broadcast_to(top, (8, LANES)))
            total = jnp.zeros((8, LANES), F32)
            for j in range(rows // LANES):
                tile = jnp.exp(lt_ref[j * LANES : (j + 1) * LANES, lane] - high)
                k_ref[j * LANES : (j + 1) * LANES, lane] = tile
                total = total + folded(tile, jnp.sum)
            m_ref[pl.ds(2 * blocks + 2 * b + t, 1), :] = jnp.sum(total, axis=0, keepdims=True)

    product(0)

    def block(b, carry):
        product(b)
        exponentials(b - 1)
        return carry

    lax.fori_loop(1, blocks, block, 0)
    exponentials(blocks - 1)
    put_message(msg_ref, m_ref)


def put_message(msg_ref, m_ref):
    if len(msg_ref.shape) == 2:
        msg_ref[...] = m_ref[...]
    else:
        for d in range(msg_ref.shape[0]):
            msg_ref[d] = m_ref[...]


def combine(parts):
    peak = functools.reduce(jnp.maximum, [m for m, _ in parts])
    sums = [s * jnp.exp(m - peak) for m, s in parts]
    while len(sums) > 1:
        sums = [sums[i] + sums[i + 1] for i in range(0, len(sums), 2)]
    return peak + jnp.log(sums[0])


def column_kernel(n_got, *refs):
    got_refs, refs = refs[:n_got], refs[n_got:]
    a_ref, logw_ref, k_ref, lt_hbm, f_ref, near_ref, msg_ref, w_ref, chunk_ref, sem = refs
    wide = a_ref.shape[0]
    tall = k_ref.shape[0] // LANES
    got = []
    for ref in got_refs:
        views = [ref] if len(ref.shape) == 2 else [ref.at[d] for d in range(ref.shape[0])]
        got += [(view[:wide, :], view[wide:, :]) for view in views]
    f = logw_ref[...] - combine(got)
    f_ref[...] = f
    near_ref[...] = f
    fa = f + a_ref[...]
    high = jnp.max(jnp.max(fa, axis=1, keepdims=True), axis=0, keepdims=True)
    w_ref[...] = jnp.exp(fa - high)
    eye = diagonal()

    least = jnp.full((1, LANES), jnp.inf, F32)
    for j in range(tall):
        acc = jnp.zeros((LANES // 8, 8, LANES), F32)
        for c in range(wide):
            tile = k_ref[j * LANES : (j + 1) * LANES, c * LANES : (c + 1) * LANES]
            acc = acc + tile.reshape(LANES // 8, 8, LANES) * repeated(w_ref, c)[None]
        total = to_row(jnp.sum(acc.reshape(LANES, LANES), axis=1, keepdims=True), eye)
        msg_ref[tall + j : tall + j + 1, :] = total
        least = jnp.minimum(least, total)
    msg_ref[:tall, :] = jnp.broadcast_to(high, (tall, LANES))

    @pl.when(jnp.logical_not(jnp.min(least) > SAFE))
    def _():
        def exact(j, carry):
            at = pl.ds(pl.multiple_of(j * LANES, LANES), LANES)
            copy = pltpu.make_async_copy(lt_hbm.at[at, :], chunk_ref, sem)
            copy.start()
            copy.wait()
            top = jnp.full((LANES, LANES), -jnp.inf, F32)
            for c in range(wide):
                lane = slice(c * LANES, (c + 1) * LANES)
                shifted = chunk_ref[:, lane] + spread(repeated(f_ref, c))
                chunk_ref[:, lane] = shifted
                top = jnp.maximum(top, shifted)
            top = jnp.max(top, axis=1, keepdims=True)
            acc = jnp.zeros((LANES, LANES), F32)
            for c in range(wide):
                acc = acc + jnp.exp(chunk_ref[:, c * LANES : (c + 1) * LANES] - top)
            msg_ref[pl.ds(j, 1), :] = to_row(top, eye)
            msg_ref[pl.ds(tall + j, 1), :] = to_row(jnp.sum(acc, axis=1, keepdims=True), eye)
            return carry

        lax.fori_loop(0, tall, exact, 0)


def row_kernel(n_got, *refs):
    got_refs, refs = refs[:n_got], refs[n_got:]
    logw_ref, a_ref, k_ref, lt_hbm, msg_ref, g_ref, v_ref, m_ref, chunk_ref, sem = refs
    wide = a_ref.shape[0]
    tall = k_ref.shape[0] // LANES
    g = logw_ref[...] - combine([(r[:tall, :], r[tall:, :]) for r in got_refs])
    g_ref[...] = g
    high = jnp.max(jnp.max(g, axis=1, keepdims=True), axis=0, keepdims=True)
    v_ref[...] = jnp.exp(g - high)
    eye = diagonal()

    acc = [jnp.zeros((8, LANES), F32)] * wide
    for j in range(tall):
        v = to_column(repeated(v_ref, j), eye)
        for c in range(wide):
            tile = k_ref[j * LANES : (j + 1) * LANES, c * LANES : (c + 1) * LANES]
            acc[c] = acc[c] + folded(tile * v, jnp.sum)
    m_ref[:wide, :] = a_ref[...] + high
    least = jnp.full((1, LANES), jnp.inf, F32)
    for c in range(wide):
        total = jnp.sum(acc[c], axis=0, keepdims=True)
        m_ref[wide + c : wide + c + 1, :] = total
        least = jnp.minimum(least, total)

    @pl.when(jnp.logical_not(jnp.min(least) > SAFE))
    def _():
        m_ref[:wide, :] = jnp.full((wide, LANES), -jnp.inf, F32)
        m_ref[wide:, :] = jnp.zeros((wide, LANES), F32)

        def exact(j, carry):
            at = pl.ds(pl.multiple_of(j * LANES, LANES), LANES)
            copy = pltpu.make_async_copy(lt_hbm.at[at, :], chunk_ref, sem)
            copy.start()
            copy.wait()
            column = to_column(repeated(g_ref, j), eye)
            for c in range(wide):
                shifted = chunk_ref[:, c * LANES : (c + 1) * LANES] + column
                before = m_ref[c : c + 1, :]
                top = jnp.maximum(before, jnp.max(shifted, axis=0, keepdims=True))
                m_ref[c : c + 1, :] = top
                m_ref[wide + c : wide + c + 1, :] = m_ref[
                    wide + c : wide + c + 1, :
                ] * jnp.exp(before - top) + jnp.sum(jnp.exp(shifted - top), axis=0, keepdims=True)
            return carry

        lax.fori_loop(0, tall, exact, 0)

    put_message(msg_ref, m_ref)


def plan_kernel(n_got, *refs):
    got_refs, refs = refs[:n_got], refs[n_got:]
    logw_ref, f_ref, lt_ref, g_ref, p_ref, mass_ref = refs
    wide = f_ref.shape[0]
    tall = lt_ref.shape[0] // LANES
    g_ref[...] = logw_ref[...] - combine([(r[:tall, :], r[tall:, :]) for r in got_refs])
    eye = diagonal()

    def block(j, acc):
        at = pl.ds(pl.multiple_of(j * LANES, LANES), LANES)
        column = to_column(repeated(g_ref, j), eye)
        out = []
        for c in range(wide):
            lane = slice(c * LANES, (c + 1) * LANES)
            plan = jnp.exp(lt_ref[at, lane] + spread(repeated(f_ref, c)) + column)
            p_ref[at, lane] = plan.astype(BF16)
            out.append(acc[c] + folded(plan, jnp.sum))
        return tuple(out)

    acc = lax.fori_loop(0, tall, block, (jnp.zeros((8, LANES), F32),) * wide)
    for c in range(wide):
        mass_ref[c : c + 1, :] = jnp.sum(acc[c], axis=0, keepdims=True)


def old_terms_kernel(base, where_ref, nf_ref, p_ref, *refs):
    outs, lhs_ref = refs[:-1], refs[-1]
    blocks = len(outs) // 2
    r, half = outs[0].shape
    for k in range(blocks):
        lhs_ref[k * r : (k + 1) * r, :] = nf_ref[
            pl.ds(pl.multiple_of(where_ref[base + k] * r, r), r), :
        ]
    wide = 2 * LANES
    for h in range(2):

        def block(b, carry, h=h):
            at = pl.ds(pl.multiple_of(h * half + b * wide, wide), wide)
            here = pl.ds(pl.multiple_of(b * wide, wide), wide)
            got = jnp.dot(lhs_ref[...], p_ref[:, at], preferred_element_type=F32)
            for k in range(blocks):
                out = outs[2 * k + h]
                out[:, here] = got[k * r : (k + 1) * r, :].astype(out.dtype)
            return carry

        lax.fori_loop(0, half // wide, block, 0)


def new_terms_kernel(base, pieces, where_ref, of_ref, p_ref, away_ref, own_ref, lhs_ref):
    q, w = own_ref.shape
    r = lhs_ref.shape[0] // pieces
    for k in range(pieces):
        lhs_ref[k * r : (k + 1) * r, :] = of_ref[
            pl.ds(pl.multiple_of(where_ref[base + k] * r, r), r), :
        ]
    wide = 2 * LANES

    def block(b, carry):
        at = pl.ds(pl.multiple_of(b * wide, wide), wide)
        got = lax.dot_general(
            lhs_ref[...], p_ref[at, :], (((1,), (1,)), ((), ())), preferred_element_type=F32
        )
        away_ref[:, at] = got[:q, :].astype(away_ref.dtype)
        own_ref[:, at] = got[q:, :]
        return carry

    lax.fori_loop(0, w // wide, block, 0)


def swap(x, axis, size, mask, only=None):
    return lax.ppermute(x, axis, [(i, i ^ mask) for i in range(size) if only is None or only(i)])


def position(n):
    return (n // 2) + (n % 2) * (7 - 2 * (n // 2))


def device_at(p):
    p = p % 8
    return 2 * p - (p // 4) * (4 * p - 15)


def turn(x, step):
    return lax.ppermute(x, NEW, [(i, device_at(position(i) + step)) for i in range(8)])


def halves(x):
    width = x.shape[1] // 2
    return [x[:, :width], x[:, width:]]


def gather_old(x):
    up, down = halves(x), halves(x)
    behind, ahead, opposite = [], [], [None, None]
    for hop in (1, 2, 3, 4):
        for h in (0, 1):
            if hop < 4 or h == 0:
                up[h] = turn(up[h], 1)
            if hop < 4 or h == 1:
                down[h] = turn(down[h], -1)
        if hop < 4:
            behind.append(list(up))
            ahead.append(list(down))
    opposite = [up[0], down[1]]
    return [[x], *ahead, opposite, *behind[::-1]]


def gather_new(x):
    across = swap(x, OLD, 4, 2, None)
    return [x, across, swap(x, OLD, 4, 1, None), swap(across, OLD, 4, 1, None)]


def scatter_old(far, near):
    four, up3, down3 = far
    up = {3: up3, 2: near[0], 1: near[2]}
    down = {3: down3, 2: near[1], 1: near[3]}
    sums = list(near[4])
    for h in (0, 1):
        for blocks, step, start in ((up, 1, 4 - h), (down, -1, 3 + h)):
            x = four[h] if start == 4 else blocks[3][h]
            for hop in range(start, 0, -1):
                x = turn(x.astype(BF16), step).astype(F32)
                if hop > 1:
                    x = blocks[hop - 1][h] + x
            sums[h] = sums[h] + x
    return sums


def integers(values):
    return jnp.stack([jnp.asarray(v, jnp.int32) for v in values])


def is_tuned(n_old, n_new):
    return (n_old, n_new) == (4, 8)


def per_device(n_old, n_new, old_emb, new_emb, old_logw, new_logw):
    tuned = is_tuned(n_old, n_new)
    width, height = old_logw.shape[0], new_logw.shape[0]
    wide, tall = width // LANES, height // LANES
    depth = old_emb.shape[0] * n_new
    scale = 1.0 / (math.sqrt(depth) * EPSILON)
    if tuned:
        old_slots, new_slots = gather_old(old_emb), gather_new(new_emb)
        p, me = position(lax.axis_index(NEW)), lax.axis_index(OLD)
        owners = [device_at(p + i) for i in range(8)] + [me, me ^ 2, me ^ 1, me ^ 3]
    else:
        old_all = lax.all_gather(old_emb, NEW, axis=0, tiled=True)
        old_slots = [[old_all[: depth // 2]], [old_all[depth // 2 :]]]
        new_slots = [lax.all_gather(new_emb, OLD, axis=0, tiled=True)]
        owners = [0, 1, 0]
    held = len(owners)
    if tuned:
        owners = owners + [device_at(p + i) for i in (4, 3, -3, 2, -2, 1, -1, 0)]
        for o in (me ^ 3, me ^ 2, me ^ 1, me):
            owners = owners + [(position(2 * o + i) - p) % 8 for i in (0, 1)]
    where = integers(owners)
    old_w = old_logw.reshape(wide, LANES)
    new_w = new_logw.reshape(tall, LANES)
    cells = width * height
    n_slots = len(old_slots)
    message = (n_new, 2 * wide, LANES)
    new_rows, new_full = call(
        functools.partial(prepare_kernel, n_slots),
        [((height, depth), BF16, True), ((depth, height), BF16, True)],
        [pltpu.VMEM((depth, height), BF16)],
        [(where, SM)] + [(x, VM) for x in new_slots],
        8,
        flops=cells,
        nbytes=8 * depth * height,
    )
    lt, k, old_full, a, msg = call(
        functools.partial(logits_kernel, [len(slot) for slot in old_slots], scale),
        [
            ((height, width), F32, True),
            ((height, width), F32, True),
            ((depth, width), BF16, True),
            ((wide, LANES), F32, True),
            (message, F32, False),
        ],
        [pltpu.VMEM((2 * wide, LANES), F32)],
        [(new_rows, STAY)] + [(x, VM) for slot in old_slots for x in slot],
        8,
        flops=2 * cells * depth,
        nbytes=12 * cells,
        exps=cells,
    )

    def over_old(message):
        return [message] + [swap(message, OLD, n_old, d) for d in range(1, n_old)]

    chunk = [pltpu.VMEM((LANES, width), F32), pltpu.SemaphoreType.DMA]
    for step in range(ITERS):
        got = [lax.all_to_all(msg, NEW, 0, 0, tiled=True)]
        f, f_near, columns = call(
            functools.partial(column_kernel, len(got)),
            [((wide, LANES), F32, False), ((wide, LANES), F32, True), ((2 * tall, LANES), F32, False)],
            [pltpu.VMEM((wide, LANES), F32)] + chunk,
            [(x, VM) for x in got] + [(a, STAY), (old_w, VM), (k, STAY), (lt, ANY)],
            6,
            flops=2 * cells,
            nbytes=4 * cells,
        )
        columns = over_old(columns)
        if step + 1 < ITERS:
            (msg,) = call(
                functools.partial(row_kernel, n_old),
                [(message, F32, False)],
                [pltpu.VMEM((tall, LANES), F32)] * 2
                + [pltpu.VMEM((2 * wide, LANES), F32)]
                + chunk,
                [(c, VM) for c in columns]
                + [(new_w, VM), (a, STAY), (k, STAY), (lt, ANY)],
                6,
                flops=2 * cells,
                nbytes=4 * cells,
            )
    g, plan, mass = call(
        functools.partial(plan_kernel, n_old),
        [
            ((tall, LANES), F32, False),
            ((height, width), BF16, True),
            ((wide, LANES), F32, False),
        ],
        [],
        [(c, VM) for c in columns] + [(new_w, VM), (f_near, STAY), (lt, STAY)],
        6,
        flops=2 * cells,
        nbytes=6 * cells,
        exps=cells,
    )
    if tuned:
        r = depth // n_new

        def old_part(base, types):
            got = call(
                functools.partial(old_terms_kernel, base),
                [((r, width // 2), dtype, False) for dtype in types],
                [pltpu.VMEM((len(types) // 2 * r, height), BF16)],
                [(where, SM), (new_full, STAY), (plan, STAY)],
                16,
                flops=cells * r * len(types),
                nbytes=2 * cells,
            )
            return [got[i : i + 2] for i in range(0, len(got), 2)]

        far = old_part(held, (BF16, BF16, F32, BF16, BF16, F32))
        for d in (1, 2, 4):
            mass = mass + swap(mass, NEW, 8, d, None)
        old_sums = scatter_old(far, old_part(held + 3, (F32,) * 10))
        q = depth // n_old


        def new_part(base):
            away, own = call(
                functools.partial(new_terms_kernel, base, 4),
                [((q, height), BF16, False), ((q, height), F32, False)],
                [pltpu.VMEM((2 * q, width), BF16)],
                [(where, SM), (old_full, STAY), (plan, STAY)],
                16,
                flops=cells * depth,
                nbytes=4 * cells,
            )
            return own + swap(away, OLD, 4, 1, None).astype(F32)

        far = swap(new_part(held + 8).astype(BF16), OLD, 4, 2, None)
        new_sums = new_part(held + 12) + far.astype(F32)
    else:
        mass = lax.psum(mass, NEW)
        old_terms = jnp.dot(new_full, plan, preferred_element_type=F32)
        new_terms = lax.dot_general(
            old_full, plan, (((1,), (1,)), ((), ())), preferred_element_type=F32
        )
        old_sums = lax.psum_scatter(old_terms, NEW, scatter_dimension=0, tiled=True)
        new_sums = lax.psum_scatter(new_terms, OLD, scatter_dimension=0, tiled=True)
    if tuned:
        masses = halves(mass.reshape(1, width))
        old_map = jnp.concatenate([x / y for x, y in zip(old_sums, masses)], axis=1)
    else:
        old_map = old_sums / mass.reshape(width)[None, :]
    new_map = new_sums / jnp.exp(new_logw)[None, :]
    return (f.reshape(width), g.reshape(height), old_map, new_map)


def solution(mesh):
    in_specs = (P(NEW, OLD), P(OLD, NEW), P(OLD), P(NEW))
    out_specs = (P(OLD), P(NEW), P(NEW, OLD), P(OLD, NEW))
    n_old, n_new = mesh.shape[OLD], mesh.shape[NEW]
    return jax.shard_map(
        functools.partial(per_device, n_old, n_new),
        mesh=mesh,
        in_specs=in_specs,
        out_specs=out_specs,
        check_vma=False,
    )
```

```python
import functools
import math

import jax
import jax.numpy as jnp
from jax import lax
from jax.experimental import pallas as pl
from jax.experimental.pallas import tpu as pltpu
from jax.sharding import PartitionSpec as P

ITERS = 3
EPSILON = 0.5
LANES = 128
SAFE = 1e-20
BF16 = jnp.bfloat16
F32 = jnp.float32
OLD, NEW = "old", "new"
MIB = 2**20
STAY, VM, SM, ANY = range(4)


def call(kernel, outs, scratch, args, limit, flops=0, nbytes=0, exps=0, aliases=None):
    out_shape, arrays, in_specs = [], [], []
    for shape, dtype, resident in outs:
        out_shape.append(
            pltpu.VMEM(shape, dtype) if resident else jax.ShapeDtypeStruct(shape, dtype)
        )
    for array, where in args:
        if where == STAY:
            array = pltpu.with_memory_space_constraint(array, pltpu.VMEM)
        arrays.append(array)
        space = {SM: pltpu.SMEM, ANY: pl.ANY}.get(where, pltpu.VMEM)
        in_specs.append(pl.BlockSpec(memory_space=space))
    return pl.pallas_call(
        kernel,
        out_shape=tuple(out_shape),
        in_specs=in_specs,
        out_specs=tuple(pl.BlockSpec(memory_space=pltpu.VMEM) for _ in outs),
        scratch_shapes=scratch,
        input_output_aliases=aliases or {},
        compiler_params=pltpu.CompilerParams(vmem_limit_bytes=limit * MIB),
        cost_estimate=pl.CostEstimate(flops=flops, bytes_accessed=nbytes, transcendentals=exps),
    )(*arrays)


def diagonal():
    shape = (LANES, LANES)
    return lax.broadcasted_iota(jnp.int32, shape, 0) == lax.broadcasted_iota(jnp.int32, shape, 1)


def to_column(row8, eye):
    rows = jnp.concatenate([row8] * (LANES // 8), axis=0)
    return jnp.sum(jnp.where(eye, rows, 0.0), axis=1, keepdims=True)


def to_row(column, eye):
    return jnp.sum(jnp.where(eye, column, 0.0), axis=0, keepdims=True)


def folded(tile, op):
    return op(tile.reshape(LANES // 8, 8, LANES), axis=0)


def repeated(ref, row):
    return ref[pl.ds(row, 8, stride=0), :]


def spread(row8):
    return jnp.concatenate([row8] * (LANES // 8), axis=0)


def stack_slots(slots, out_ref, row=0):
    for slot in slots:
        column = 0
        for piece in slot:
            r, w = piece.shape
            out_ref[row : row + r, column : column + w] = piece[...]
            column += w
        row += r


def grouped(refs, counts):
    return [refs[sum(counts[:p]) : sum(counts[: p + 1])] for p in range(len(counts))]


def prepare_kernel(n_slots, where_ref, *refs):
    new_refs, (nt_ref, nf_ref, ns_ref) = refs[:-3], refs[-3:]
    depth, rows = nf_ref.shape
    for p, piece in enumerate(new_refs):
        r = piece.shape[0]
        start = pl.multiple_of(where_ref[n_slots + p] * r, r)
        nf_ref[pl.ds(start, r), :] = piece[...]
    r = depth // n_slots
    for p in range(n_slots):
        ns_ref[p * r : (p + 1) * r, :] = nf_ref[pl.ds(pl.multiple_of(where_ref[p] * r, r), r), :]
    for c in range(rows // LANES):
        nt_ref[c * LANES : (c + 1) * LANES, :] = ns_ref[:, c * LANES : (c + 1) * LANES].T


def logits_kernel(counts, scale, nt_ref, *refs):
    slots, refs = grouped(refs, counts), refs[sum(counts) :]
    lt_ref, k_ref, of_ref, a_ref, msg_ref, m_ref, even_ref, odd_ref = refs
    columns = of_ref.shape[1]
    rows = nt_ref.shape[0]
    stack_slots(slots, of_ref)
    wide = 2 * LANES
    blocks = columns // wide

    def product(b, out_ref):
        at = pl.ds(pl.multiple_of(b * wide, wide), wide)
        out_ref[...] = jnp.dot(nt_ref[...], of_ref[:, at], preferred_element_type=F32) * scale

    def exponentials(b, in_ref):
        for t in range(2):
            here = slice(t * LANES, (t + 1) * LANES)
            lane = pl.ds(pl.multiple_of(b * wide + t * LANES, LANES), LANES)
            top = jnp.full((8, LANES), -jnp.inf, F32)
            for j in range(rows // LANES):
                top = jnp.maximum(top, folded(in_ref[j * LANES : (j + 1) * LANES, here], jnp.max))
            top = jnp.max(top, axis=0, keepdims=True)
            a_ref[pl.ds(2 * b + t, 1), :] = top
            high = spread(jnp.broadcast_to(top, (8, LANES)))
            total = jnp.zeros((8, LANES), F32)
            for j in range(rows // LANES):
                down = slice(j * LANES, (j + 1) * LANES)
                tile = in_ref[down, here]
                lt_ref[down, lane] = tile
                tile = jnp.exp(tile - high)
                k_ref[down, lane] = tile
                total = total + folded(tile, jnp.sum)
            m_ref[pl.ds(2 * b + t, 1), :] = jnp.sum(total, axis=0, keepdims=True)

    product(0, even_ref)

    def pair(i, carry):
        product(2 * i + 1, odd_ref)
        exponentials(2 * i, even_ref)
        product(2 * i + 2, even_ref)
        exponentials(2 * i + 1, odd_ref)
        return carry

    lax.fori_loop(0, blocks // 2 - 1, pair, 0)
    product(blocks - 1, odd_ref)
    exponentials(blocks - 2, even_ref)
    exponentials(blocks - 1, odd_ref)
    put_message(msg_ref, a_ref[...] + jnp.log(m_ref[...]))


def put_message(msg_ref, message):
    for d in range(msg_ref.shape[0]):
        msg_ref[d] = message


def combine(parts):
    peak = functools.reduce(jnp.maximum, parts)
    sums = [jnp.exp(x - peak) for x in parts]
    while len(sums) > 1:
        sums = [sums[i] + sums[i + 1] for i in range(0, len(sums), 2)]
    return peak + jnp.log(sums[0])


def column_kernel(*refs):
    got_ref, a_ref, logw_ref, k_ref, lt_hbm, f_ref, near_ref, msg_ref, w_ref, chunk_ref, sem = refs
    wide = a_ref.shape[0]
    tall = k_ref.shape[0] // LANES
    f = logw_ref[...] - combine([got_ref[d] for d in range(got_ref.shape[0])])
    f_ref[...] = f
    near_ref[...] = f
    fa = f + a_ref[...]
    high = jnp.max(jnp.max(fa, axis=1, keepdims=True), axis=0, keepdims=True)
    w_ref[...] = jnp.exp(fa - high)
    eye = diagonal()

    least = jnp.full((1, LANES), jnp.inf, F32)
    for j in range(tall):
        acc = jnp.zeros((LANES // 8, 8, LANES), F32)
        for c in range(wide):
            tile = k_ref[j * LANES : (j + 1) * LANES, c * LANES : (c + 1) * LANES]
            acc = acc + tile.reshape(LANES // 8, 8, LANES) * repeated(w_ref, c)[None]
        total = to_row(jnp.sum(acc.reshape(LANES, LANES), axis=1, keepdims=True), eye)
        msg_ref[j : j + 1, :] = total
        least = jnp.minimum(least, total)
    msg_ref[...] = high + jnp.log(msg_ref[...])

    @pl.when(jnp.logical_not(jnp.min(least) > SAFE))
    def _():
        def exact(j, carry):
            at = pl.ds(pl.multiple_of(j * LANES, LANES), LANES)
            copy = pltpu.make_async_copy(lt_hbm.at[at, :], chunk_ref, sem)
            copy.start()
            copy.wait()
            top = jnp.full((LANES, LANES), -jnp.inf, F32)
            for c in range(wide):
                lane = slice(c * LANES, (c + 1) * LANES)
                shifted = chunk_ref[:, lane] + spread(repeated(f_ref, c))
                chunk_ref[:, lane] = shifted
                top = jnp.maximum(top, shifted)
            top = jnp.max(top, axis=1, keepdims=True)
            acc = jnp.zeros((LANES, LANES), F32)
            for c in range(wide):
                acc = acc + jnp.exp(chunk_ref[:, c * LANES : (c + 1) * LANES] - top)
            total = top + jnp.log(jnp.sum(acc, axis=1, keepdims=True))
            msg_ref[pl.ds(j, 1), :] = to_row(total, eye)
            return carry

        lax.fori_loop(0, tall, exact, 0)


def row_kernel(n_got, *refs):
    got_refs, refs = refs[:n_got], refs[n_got:]
    logw_ref, a_ref, k_ref, lt_hbm, msg_ref, g_ref, v_ref, m_ref, top_ref, chunk_ref, sem = refs
    wide = a_ref.shape[0]
    tall = k_ref.shape[0] // LANES
    g = logw_ref[...] - combine([r[...] for r in got_refs])
    g_ref[...] = g
    high = jnp.max(jnp.max(g, axis=1, keepdims=True), axis=0, keepdims=True)
    v_ref[...] = jnp.exp(g - high)
    eye = diagonal()

    acc = [jnp.zeros((8, LANES), F32)] * wide
    for j in range(tall):
        v = to_column(repeated(v_ref, j), eye)
        for c in range(wide):
            tile = k_ref[j * LANES : (j + 1) * LANES, c * LANES : (c + 1) * LANES]
            acc[c] = acc[c] + folded(tile * v, jnp.sum)
    least = jnp.full((1, LANES), jnp.inf, F32)
    for c in range(wide):
        total = jnp.sum(acc[c], axis=0, keepdims=True)
        m_ref[c : c + 1, :] = total
        least = jnp.minimum(least, total)
    put_message(msg_ref, (a_ref[...] + high) + jnp.log(m_ref[...]))

    @pl.when(jnp.logical_not(jnp.min(least) > SAFE))
    def _():
        m_ref[...] = jnp.zeros((wide, LANES), F32)
        top_ref[...] = jnp.full((wide, LANES), -jnp.inf, F32)

        def exact(j, carry):
            at = pl.ds(pl.multiple_of(j * LANES, LANES), LANES)
            copy = pltpu.make_async_copy(lt_hbm.at[at, :], chunk_ref, sem)
            copy.start()
            copy.wait()
            column = to_column(repeated(g_ref, j), eye)
            for c in range(wide):
                row = slice(c, c + 1)
                shifted = chunk_ref[:, c * LANES : (c + 1) * LANES] + column
                before = top_ref[row, :]
                top = jnp.maximum(before, jnp.max(shifted, axis=0, keepdims=True))
                top_ref[row, :] = top
                more = jnp.sum(jnp.exp(shifted - top), axis=0, keepdims=True)
                m_ref[row, :] = m_ref[row, :] * jnp.exp(before - top) + more
            return carry

        lax.fori_loop(0, tall, exact, 0)
        put_message(msg_ref, top_ref[...] + jnp.log(m_ref[...]))


def plan_kernel(n_got, *refs):
    got_refs, refs = refs[:n_got], refs[n_got:]
    logw_ref, f_ref, lt_ref, g_ref, p_ref, mass_ref = refs
    wide = f_ref.shape[0]
    tall = lt_ref.shape[0] // LANES
    g_ref[...] = logw_ref[...] - combine([r[...] for r in got_refs])
    eye = diagonal()

    def block(j, acc):
        at = pl.ds(pl.multiple_of(j * LANES, LANES), LANES)
        column = to_column(repeated(g_ref, j), eye)
        out = []
        for c in range(wide):
            lane = slice(c * LANES, (c + 1) * LANES)
            plan = jnp.exp(lt_ref[at, lane] + spread(repeated(f_ref, c)) + column)
            p_ref[at, lane] = plan.astype(BF16)
            out.append(acc[c] + folded(plan, jnp.sum))
        return tuple(out)

    acc = lax.fori_loop(0, tall, block, (jnp.zeros((8, LANES), F32),) * wide)
    for c in range(wide):
        mass_ref[c : c + 1, :] = jnp.sum(acc[c], axis=0, keepdims=True)


def old_terms_kernel(base, where_ref, nf_ref, p_ref, *refs):
    outs, lhs_ref = refs[:-1], refs[-1]
    blocks = len(outs) // 2
    r, half = outs[0].shape
    for k in range(blocks):
        lhs_ref[k * r : (k + 1) * r, :] = nf_ref[
            pl.ds(pl.multiple_of(where_ref[base + k] * r, r), r), :
        ]
    wide = 2 * LANES
    for h in range(2):

        def block(b, carry, h=h):
            at = pl.ds(pl.multiple_of(h * half + b * wide, wide), wide)
            here = pl.ds(pl.multiple_of(b * wide, wide), wide)
            got = jnp.dot(lhs_ref[...], p_ref[:, at], preferred_element_type=F32)
            for k in range(blocks):
                out = outs[2 * k + h]
                out[:, here] = got[k * r : (k + 1) * r, :].astype(out.dtype)
            return carry

        lax.fori_loop(0, half // wide, block, 0)


def new_terms_kernel(base, pieces, where_ref, of_ref, p_ref, away_ref, own_ref, lhs_ref):
    q, w = own_ref.shape
    r = lhs_ref.shape[0] // pieces
    for k in range(pieces):
        lhs_ref[k * r : (k + 1) * r, :] = of_ref[
            pl.ds(pl.multiple_of(where_ref[base + k] * r, r), r), :
        ]
    wide = 2 * LANES

    def block(b, carry):
        at = pl.ds(pl.multiple_of(b * wide, wide), wide)
        got = lax.dot_general(
            lhs_ref[...], p_ref[at, :], (((1,), (1,)), ((), ())), preferred_element_type=F32
        )
        away_ref[:, at] = got[:q, :].astype(away_ref.dtype)
        own_ref[:, at] = got[q:, :]
        return carry

    lax.fori_loop(0, w // wide, block, 0)


def swap(x, axis, size, mask, only=None):
    return lax.ppermute(x, axis, [(i, i ^ mask) for i in range(size) if only is None or only(i)])


def maps_kernel(mass_ref, logw_ref, *refs):
    left, right, last, (old_ref, new_ref) = refs[:3], refs[3:6], refs[6:9], refs[9:]
    half = left[0].shape[1] // LANES
    for h, parts in enumerate((left, right)):
        for c in range(half):
            lane = slice(c * LANES, (c + 1) * LANES)
            out = slice((h * half + c) * LANES, (h * half + c + 1) * LANES)
            total = sum(part[:, lane].astype(F32) for part in parts)
            old_ref[:, out] = total / mass_ref[h * half + c : h * half + c + 1, :]
    for c in range(logw_ref.shape[0]):
        lane = slice(c * LANES, (c + 1) * LANES)
        total = sum(part[:, lane].astype(F32) for part in last)
        new_ref[:, lane] = total / jnp.exp(logw_ref[c : c + 1, :])


def position(n):
    return (n // 2) + (n % 2) * (7 - 2 * (n // 2))


def device_at(p):
    p = p % 8
    return 2 * p - (p // 4) * (4 * p - 15)


def turn(x, step):
    return lax.ppermute(x, NEW, [(i, device_at(position(i) + step)) for i in range(8)])


def halves(x):
    width = x.shape[1] // 2
    return [x[:, :width], x[:, width:]]


def gather_old(x):
    first = halves(x)
    up, down = list(first), list(first)
    behind, ahead, opposite = [], [], [None, None]
    for hop in (1, 2, 3, 4):
        for h in (0, 1):
            if hop < 4 or h == 0:
                up[h] = turn(up[h], 1)
            if hop < 4 or h == 1:
                down[h] = turn(down[h], -1)
        if hop < 4:
            behind.append(list(up))
            ahead.append(list(down))
    opposite = [up[0], down[1]]
    return [first, *ahead, opposite, *behind[::-1]]


def gather_new(x):
    across = swap(x, OLD, 4, 2, None)
    return [x, across, swap(x, OLD, 4, 1, None), swap(across, OLD, 4, 1, None)]


def scatter_old(far, near):
    four, up3, down3 = far
    up = {3: up3, 2: near[0], 1: near[2]}
    down = {3: down3, 2: near[1], 1: near[3]}
    last = [[near[4][0]], [near[4][1]]]
    for h in (0, 1):
        for blocks, step, start in ((up, 1, 4 - h), (down, -1, 3 + h)):
            x = four[h] if start == 4 else blocks[3][h]
            for hop in range(start, 0, -1):
                x = turn(x.astype(BF16), step)
                if hop > 1:
                    x = blocks[hop - 1][h] + x.astype(F32)
            last[h].append(x)
    return last


def integers(values):
    return jnp.stack([jnp.asarray(v, jnp.int32) for v in values])


def is_tuned(n_old, n_new):
    return (n_old, n_new) == (4, 8)


def per_device(n_old, n_new, old_emb, new_emb, old_logw, new_logw):
    tuned = is_tuned(n_old, n_new)
    width, height = old_logw.shape[0], new_logw.shape[0]
    wide, tall = width // LANES, height // LANES
    depth = old_emb.shape[0] * n_new
    scale = 1.0 / (math.sqrt(depth) * EPSILON)
    if tuned:
        old_slots, new_slots = gather_old(old_emb), gather_new(new_emb)
        p, me = position(lax.axis_index(NEW)), lax.axis_index(OLD)
        owners = [device_at(p + i) for i in range(8)] + [me, me ^ 2, me ^ 1, me ^ 3]
    else:
        old_all = lax.all_gather(old_emb, NEW, axis=0, tiled=True)
        old_slots = [[old_all[: depth // 2]], [old_all[depth // 2 :]]]
        new_slots = [lax.all_gather(new_emb, OLD, axis=0, tiled=True)]
        owners = [0, 1, 0]
    held = len(owners)
    if tuned:
        owners = owners + [device_at(p + i) for i in (4, 3, -3, 2, -2, 1, -1, 0)]
        for o in (me ^ 3, me ^ 2, me ^ 1, me):
            owners = owners + [(position(2 * o + i) - p) % 8 for i in (0, 1)]
    where = integers(owners)
    old_w = old_logw.reshape(wide, LANES)
    new_w = new_logw.reshape(tall, LANES)
    cells = width * height
    n_slots = len(old_slots)
    message = (n_new, wide, LANES)
    new_rows, new_full = call(
        functools.partial(prepare_kernel, n_slots),
        [((height, depth), BF16, True), ((depth, height), BF16, True)],
        [pltpu.VMEM((depth, height), BF16)],
        [(where, SM)] + [(x, VM) for x in new_slots],
        8,
        flops=cells,
        nbytes=8 * depth * height,
    )
    lt, k, old_full, a, msg = call(
        functools.partial(logits_kernel, [len(slot) for slot in old_slots], scale),
        [
            ((height, width), F32, True),
            ((height, width), F32, True),
            ((depth, width), BF16, True),
            ((wide, LANES), F32, True),
            (message, F32, False),
        ],
        [pltpu.VMEM((wide, LANES), F32)] + [pltpu.VMEM((height, 2 * LANES), F32)] * 2,
        [(new_rows, STAY)] + [(x, VM) for slot in old_slots for x in slot],
        8,
        flops=2 * cells * depth,
        nbytes=12 * cells,
        exps=cells,
    )

    def over_old(message):
        return [message] + [swap(message, OLD, n_old, d) for d in range(1, n_old)]

    chunk = [pltpu.VMEM((LANES, width), F32), pltpu.SemaphoreType.DMA]
    for step in range(ITERS):
        got = lax.all_to_all(msg, NEW, 0, 0, tiled=True)
        f, f_near, columns = call(
            column_kernel,
            [((wide, LANES), F32, False), ((wide, LANES), F32, True), ((tall, LANES), F32, False)],
            [pltpu.VMEM((wide, LANES), F32)] + chunk,
            [(got, VM), (a, STAY), (old_w, VM), (k, STAY), (lt, ANY)],
            6,
            flops=2 * cells,
            nbytes=4 * cells,
        )
        columns = over_old(columns)
        if step + 1 < ITERS:
            (msg,) = call(
                functools.partial(row_kernel, n_old),
                [(message, F32, False)],
                [pltpu.VMEM((tall, LANES), F32)] * 2
                + [pltpu.VMEM((wide, LANES), F32)] * 2
                + chunk,
                [(c, VM) for c in columns]
                + [(new_w, VM), (a, STAY), (k, STAY), (lt, ANY)],
                6,
                flops=2 * cells,
                nbytes=4 * cells,
            )
    g, plan, mass = call(
        functools.partial(plan_kernel, n_old),
        [
            ((tall, LANES), F32, False),
            ((height, width), BF16, True),
            ((wide, LANES), F32, False),
        ],
        [],
        [(c, VM) for c in columns] + [(new_w, VM), (f_near, STAY), (lt, STAY)],
        6,
        flops=2 * cells,
        nbytes=6 * cells,
        exps=cells,
    )
    if tuned:
        r = depth // n_new

        def old_part(base, types):
            got = call(
                functools.partial(old_terms_kernel, base),
                [((r, width // 2), dtype, False) for dtype in types],
                [pltpu.VMEM((len(types) // 2 * r, height), BF16)],
                [(where, SM), (new_full, STAY), (plan, STAY)],
                16,
                flops=cells * r * len(types),
                nbytes=2 * cells,
            )
            return [got[i : i + 2] for i in range(0, len(got), 2)]

        far = old_part(held, (BF16, BF16, F32, BF16, BF16, F32))
        for d in (1, 2, 4):
            mass = mass + swap(mass, NEW, 8, d, None)
        old_parts = scatter_old(far, old_part(held + 3, (F32,) * 10))
        q = depth // n_old


        def new_part(base):
            away, own = call(
                functools.partial(new_terms_kernel, base, 4),
                [((q, height), BF16, False), ((q, height), F32, False)],
                [pltpu.VMEM((2 * q, width), BF16)],
                [(where, SM), (old_full, STAY), (plan, STAY)],
                16,
                flops=cells * depth,
                nbytes=4 * cells,
            )
            return own, swap(away, OLD, 4, 1, None)

        own, core = new_part(held + 8)
        far = swap((own + core.astype(F32)).astype(BF16), OLD, 4, 2, None)
        new_parts = [*new_part(held + 12), far]
        old_map, new_map = call(
            maps_kernel,
            [((r, width), F32, False), ((q, height), F32, False)],
            [],
            [(mass, VM), (new_w, VM)] + [(x, VM) for x in (*old_parts[0], *old_parts[1], *new_parts)],
            8,
            flops=8 * r * width,
            nbytes=16 * r * width,
        )
    else:
        mass = lax.psum(mass, NEW)
        old_terms = jnp.dot(new_full, plan, preferred_element_type=F32)
        new_terms = lax.dot_general(
            old_full, plan, (((1,), (1,)), ((), ())), preferred_element_type=F32
        )
        old_sums = lax.psum_scatter(old_terms, NEW, scatter_dimension=0, tiled=True)
        new_sums = lax.psum_scatter(new_terms, OLD, scatter_dimension=0, tiled=True)
        old_map = old_sums / mass.reshape(width)[None, :]
        new_map = new_sums / jnp.exp(new_logw)[None, :]
    return (f.reshape(width), g.reshape(height), old_map, new_map)


def solution(mesh):
    in_specs = (P(NEW, OLD), P(OLD, NEW), P(OLD), P(NEW))
    out_specs = (P(OLD), P(NEW), P(NEW, OLD), P(OLD, NEW))
    n_old, n_new = mesh.shape[OLD], mesh.shape[NEW]
    return jax.shard_map(
        functools.partial(per_device, n_old, n_new),
        mesh=mesh,
        in_specs=in_specs,
        out_specs=out_specs,
        check_vma=False,
    )
```

```python
import functools
import math

import jax
import jax.numpy as jnp
from jax import lax
from jax.experimental import pallas as pl
from jax.experimental.pallas import tpu as pltpu
from jax.sharding import PartitionSpec as P

ITERS = 3
EPSILON = 0.5
LANES = 128
SAFE = 1e-20
BF16 = jnp.bfloat16
F32 = jnp.float32
OLD, NEW = "old", "new"
MIB = 2**20
STAY, VM, SM, ANY = range(4)


def call(kernel, outs, scratch, args, limit, flops=0, nbytes=0, exps=0, aliases=None):
    out_shape, arrays, in_specs = [], [], []
    for shape, dtype, resident in outs:
        out_shape.append(
            pltpu.VMEM(shape, dtype) if resident else jax.ShapeDtypeStruct(shape, dtype)
        )
    for array, where in args:
        if where == STAY:
            array = pltpu.with_memory_space_constraint(array, pltpu.VMEM)
        arrays.append(array)
        space = {SM: pltpu.SMEM, ANY: pl.ANY}.get(where, pltpu.VMEM)
        in_specs.append(pl.BlockSpec(memory_space=space))
    return pl.pallas_call(
        kernel,
        out_shape=tuple(out_shape),
        in_specs=in_specs,
        out_specs=tuple(pl.BlockSpec(memory_space=pltpu.VMEM) for _ in outs),
        scratch_shapes=scratch,
        input_output_aliases=aliases or {},
        compiler_params=pltpu.CompilerParams(vmem_limit_bytes=limit * MIB),
        cost_estimate=pl.CostEstimate(flops=flops, bytes_accessed=nbytes, transcendentals=exps),
    )(*arrays)


def diagonal():
    shape = (LANES, LANES)
    return lax.broadcasted_iota(jnp.int32, shape, 0) == lax.broadcasted_iota(jnp.int32, shape, 1)


def to_column(row8, eye):
    rows = jnp.concatenate([row8] * (LANES // 8), axis=0)
    return jnp.sum(jnp.where(eye, rows, 0.0), axis=1, keepdims=True)


def to_row(column, eye):
    return jnp.sum(jnp.where(eye, column, 0.0), axis=0, keepdims=True)


def folded(tile, op):
    return op(tile.reshape(LANES // 8, 8, LANES), axis=0)


def repeated(ref, row):
    return ref[pl.ds(row, 8, stride=0), :]


def spread(row8):
    return jnp.concatenate([row8] * (LANES // 8), axis=0)


def stack_slots(slots, out_ref, row=0):
    for slot in slots:
        column = 0
        for piece in slot:
            r, w = piece.shape
            out_ref[row : row + r, column : column + w] = piece[...]
            column += w
        row += r


def grouped(refs, counts):
    return [refs[sum(counts[:p]) : sum(counts[: p + 1])] for p in range(len(counts))]


def prepare_kernel(n_slots, where_ref, *refs):
    new_refs, (nt_ref, nf_ref, ns_ref) = refs[:-3], refs[-3:]
    depth, rows = nf_ref.shape
    for p, piece in enumerate(new_refs):
        r = piece.shape[0]
        start = pl.multiple_of(where_ref[n_slots + p] * r, r)
        nf_ref[pl.ds(start, r), :] = piece[...]
    r = depth // n_slots
    for p in range(n_slots):
        ns_ref[p * r : (p + 1) * r, :] = nf_ref[pl.ds(pl.multiple_of(where_ref[p] * r, r), r), :]
    for c in range(rows // LANES):
        nt_ref[c * LANES : (c + 1) * LANES, :] = ns_ref[:, c * LANES : (c + 1) * LANES].T


def logits_kernel(counts, scale, nt_ref, *refs):
    slots, refs = grouped(refs, counts), refs[sum(counts) :]
    lt_ref, k_ref, of_ref, a_ref, msg_ref, m_ref, even_ref, odd_ref = refs
    columns = of_ref.shape[1]
    rows = nt_ref.shape[0]
    stack_slots(slots, of_ref)
    wide = 2 * LANES
    blocks = columns // wide

    def product(b, out_ref):
        at = pl.ds(pl.multiple_of(b * wide, wide), wide)
        out_ref[...] = jnp.dot(nt_ref[...], of_ref[:, at], preferred_element_type=F32) * scale

    def exponentials(b, in_ref):
        for t in range(2):
            here = slice(t * LANES, (t + 1) * LANES)
            lane = pl.ds(pl.multiple_of(b * wide + t * LANES, LANES), LANES)
            top = jnp.full((8, LANES), -jnp.inf, F32)
            for j in range(rows // LANES):
                top = jnp.maximum(top, folded(in_ref[j * LANES : (j + 1) * LANES, here], jnp.max))
            top = jnp.max(top, axis=0, keepdims=True)
            a_ref[pl.ds(2 * b + t, 1), :] = top
            high = spread(jnp.broadcast_to(top, (8, LANES)))
            total = jnp.zeros((8, LANES), F32)
            for j in range(rows // LANES):
                down = slice(j * LANES, (j + 1) * LANES)
                tile = in_ref[down, here]
                lt_ref[down, lane] = tile
                tile = jnp.exp(tile - high)
                k_ref[down, lane] = tile
                total = total + folded(tile, jnp.sum)
            m_ref[pl.ds(2 * b + t, 1), :] = jnp.sum(total, axis=0, keepdims=True)

    product(0, even_ref)

    def pair(i, carry):
        product(2 * i + 1, odd_ref)
        exponentials(2 * i, even_ref)
        product(2 * i + 2, even_ref)
        exponentials(2 * i + 1, odd_ref)
        return carry

    lax.fori_loop(0, blocks // 2 - 1, pair, 0)
    product(blocks - 1, odd_ref)
    exponentials(blocks - 2, even_ref)
    exponentials(blocks - 1, odd_ref)
    put_message(msg_ref, a_ref[...] + jnp.log(m_ref[...]))


def put_message(msg_ref, message):
    for d in range(msg_ref.shape[0]):
        msg_ref[d] = message


def combine(parts):
    peak = functools.reduce(jnp.maximum, parts)
    sums = [jnp.exp(x - peak) for x in parts]
    while len(sums) > 1:
        sums = [sums[i] + sums[i + 1] for i in range(0, len(sums), 2)]
    return peak + jnp.log(sums[0])


def column_kernel(*refs):
    got_ref, a_ref, logw_ref, k_ref, lt_hbm, f_ref, near_ref, msg_ref, w_ref, chunk_ref, sem = refs
    wide = a_ref.shape[0]
    tall = k_ref.shape[0] // LANES
    f = logw_ref[...] - combine([got_ref[d] for d in range(got_ref.shape[0])])
    f_ref[...] = f
    near_ref[...] = f
    fa = f + a_ref[...]
    high = jnp.max(jnp.max(fa, axis=1, keepdims=True), axis=0, keepdims=True)
    w_ref[...] = jnp.exp(fa - high)
    eye = diagonal()

    least = jnp.full((1, LANES), jnp.inf, F32)
    for j in range(tall):
        acc = jnp.zeros((LANES // 8, 8, LANES), F32)
        for c in range(wide):
            tile = k_ref[j * LANES : (j + 1) * LANES, c * LANES : (c + 1) * LANES]
            acc = acc + tile.reshape(LANES // 8, 8, LANES) * repeated(w_ref, c)[None]
        total = to_row(jnp.sum(acc.reshape(LANES, LANES), axis=1, keepdims=True), eye)
        msg_ref[j : j + 1, :] = total
        least = jnp.minimum(least, total)
    msg_ref[...] = high + jnp.log(msg_ref[...])

    @pl.when(jnp.logical_not(jnp.min(least) > SAFE))
    def _():
        def exact(j, carry):
            at = pl.ds(pl.multiple_of(j * LANES, LANES), LANES)
            copy = pltpu.make_async_copy(lt_hbm.at[at, :], chunk_ref, sem)
            copy.start()
            copy.wait()
            top = jnp.full((LANES, LANES), -jnp.inf, F32)
            for c in range(wide):
                lane = slice(c * LANES, (c + 1) * LANES)
                shifted = chunk_ref[:, lane] + spread(repeated(f_ref, c))
                chunk_ref[:, lane] = shifted
                top = jnp.maximum(top, shifted)
            top = jnp.max(top, axis=1, keepdims=True)
            acc = jnp.zeros((LANES, LANES), F32)
            for c in range(wide):
                acc = acc + jnp.exp(chunk_ref[:, c * LANES : (c + 1) * LANES] - top)
            total = top + jnp.log(jnp.sum(acc, axis=1, keepdims=True))
            msg_ref[pl.ds(j, 1), :] = to_row(total, eye)
            return carry

        lax.fori_loop(0, tall, exact, 0)


def row_kernel(n_got, *refs):
    got_refs, refs = refs[:n_got], refs[n_got:]
    logw_ref, a_ref, k_ref, lt_hbm, msg_ref, g_ref, v_ref, m_ref, top_ref, chunk_ref, sem = refs
    wide = a_ref.shape[0]
    tall = k_ref.shape[0] // LANES
    g = logw_ref[...] - combine([r[...] for r in got_refs])
    g_ref[...] = g
    high = jnp.max(jnp.max(g, axis=1, keepdims=True), axis=0, keepdims=True)
    v_ref[...] = jnp.exp(g - high)
    eye = diagonal()

    acc = [jnp.zeros((8, LANES), F32)] * wide
    for j in range(tall):
        v = to_column(repeated(v_ref, j), eye)
        for c in range(wide):
            tile = k_ref[j * LANES : (j + 1) * LANES, c * LANES : (c + 1) * LANES]
            acc[c] = acc[c] + folded(tile * v, jnp.sum)
    least = jnp.full((1, LANES), jnp.inf, F32)
    for c in range(wide):
        total = jnp.sum(acc[c], axis=0, keepdims=True)
        m_ref[c : c + 1, :] = total
        least = jnp.minimum(least, total)
    put_message(msg_ref, (a_ref[...] + high) + jnp.log(m_ref[...]))

    @pl.when(jnp.logical_not(jnp.min(least) > SAFE))
    def _():
        m_ref[...] = jnp.zeros((wide, LANES), F32)
        top_ref[...] = jnp.full((wide, LANES), -jnp.inf, F32)

        def exact(j, carry):
            at = pl.ds(pl.multiple_of(j * LANES, LANES), LANES)
            copy = pltpu.make_async_copy(lt_hbm.at[at, :], chunk_ref, sem)
            copy.start()
            copy.wait()
            column = to_column(repeated(g_ref, j), eye)
            for c in range(wide):
                row = slice(c, c + 1)
                shifted = chunk_ref[:, c * LANES : (c + 1) * LANES] + column
                before = top_ref[row, :]
                top = jnp.maximum(before, jnp.max(shifted, axis=0, keepdims=True))
                top_ref[row, :] = top
                more = jnp.sum(jnp.exp(shifted - top), axis=0, keepdims=True)
                m_ref[row, :] = m_ref[row, :] * jnp.exp(before - top) + more
            return carry

        lax.fori_loop(0, tall, exact, 0)
        put_message(msg_ref, top_ref[...] + jnp.log(m_ref[...]))


def plan_kernel(n_got, base, where_ref, *refs):
    got_refs, refs = refs[:n_got], refs[n_got:]
    logw_ref, f_ref, lt_ref, nf_ref, g_ref, p_ref, mass_ref = refs[:7]
    outs, (lhs_ref, column_ref) = refs[7:-2], refs[-2:]
    wide = f_ref.shape[0]
    tall = lt_ref.shape[0] // LANES
    g_ref[...] = logw_ref[...] - combine([r[...] for r in got_refs])
    eye = diagonal()
    for j in range(tall):
        column = to_column(repeated(g_ref, j), eye)
        column_ref[j * LANES : (j + 1) * LANES, :] = jnp.broadcast_to(column, (LANES, LANES))
    take_rows(base, where_ref, nf_ref, lhs_ref, len(outs) // 2)

    def plan(c):
        lane = slice(c * LANES, (c + 1) * LANES)
        row = spread(repeated(f_ref, c))
        total = jnp.zeros((8, LANES), F32)
        for j in range(tall):
            at = slice(j * LANES, (j + 1) * LANES)
            tile = jnp.exp(lt_ref[at, lane] + row + column_ref[at, :])
            p_ref[at, lane] = tile.astype(BF16)
            total = total + folded(tile, jnp.sum)
        mass_ref[c : c + 1, :] = jnp.sum(total, axis=0, keepdims=True)

    for c in range(0, wide, 2):
        plan(c)
        plan(c + 1)
        if c and outs:
            product(c - 2, p_ref, lhs_ref, outs)
    if outs:
        product(wide - 2, p_ref, lhs_ref, outs)


def take_rows(base, where_ref, nf_ref, lhs_ref, blocks):
    for k in range(blocks):
        r = lhs_ref.shape[0] // blocks
        lhs_ref[k * r : (k + 1) * r, :] = nf_ref[
            pl.ds(pl.multiple_of(where_ref[base + k] * r, r), r), :
        ]


def product(c, p_ref, lhs_ref, outs):
    r, half = outs[0].shape
    got = jnp.dot(
        lhs_ref[...], p_ref[:, c * LANES : (c + 2) * LANES], preferred_element_type=F32
    )
    h = c * LANES // half
    here = slice(c * LANES - h * half, (c + 2) * LANES - h * half)
    for k, out in enumerate(outs[h::2]):
        out[:, here] = got[k * r : (k + 1) * r, :].astype(out.dtype)


def old_terms_kernel(base, where_ref, nf_ref, p_ref, *refs):
    outs, lhs_ref = refs[:-1], refs[-1]
    blocks = len(outs) // 2
    r, half = outs[0].shape
    for k in range(blocks):
        lhs_ref[k * r : (k + 1) * r, :] = nf_ref[
            pl.ds(pl.multiple_of(where_ref[base + k] * r, r), r), :
        ]
    wide = 2 * LANES
    for h in range(2):

        def block(b, carry, h=h):
            at = pl.ds(pl.multiple_of(h * half + b * wide, wide), wide)
            here = pl.ds(pl.multiple_of(b * wide, wide), wide)
            got = jnp.dot(lhs_ref[...], p_ref[:, at], preferred_element_type=F32)
            for k in range(blocks):
                out = outs[2 * k + h]
                out[:, here] = got[k * r : (k + 1) * r, :].astype(out.dtype)
            return carry

        lax.fori_loop(0, half // wide, block, 0)


def new_terms_kernel(base, pieces, where_ref, of_ref, p_ref, away_ref, own_ref, lhs_ref):
    q, w = own_ref.shape
    r = lhs_ref.shape[0] // pieces
    for k in range(pieces):
        lhs_ref[k * r : (k + 1) * r, :] = of_ref[
            pl.ds(pl.multiple_of(where_ref[base + k] * r, r), r), :
        ]
    wide = 2 * LANES

    def block(b, carry):
        at = pl.ds(pl.multiple_of(b * wide, wide), wide)
        got = lax.dot_general(
            lhs_ref[...], p_ref[at, :], (((1,), (1,)), ((), ())), preferred_element_type=F32
        )
        away_ref[:, at] = got[:q, :].astype(away_ref.dtype)
        own_ref[:, at] = got[q:, :]
        return carry

    lax.fori_loop(0, w // wide, block, 0)


def swap(x, axis, size, mask, only=None):
    return lax.ppermute(x, axis, [(i, i ^ mask) for i in range(size) if only is None or only(i)])


def maps_kernel(mass_ref, logw_ref, *refs):
    left, right, last, (old_ref, new_ref) = refs[:3], refs[3:6], refs[6:9], refs[9:]
    half = left[0].shape[1] // LANES
    for h, parts in enumerate((left, right)):
        for c in range(half):
            lane = slice(c * LANES, (c + 1) * LANES)
            out = slice((h * half + c) * LANES, (h * half + c + 1) * LANES)
            total = sum(part[:, lane].astype(F32) for part in parts)
            old_ref[:, out] = total / mass_ref[h * half + c : h * half + c + 1, :]
    for c in range(logw_ref.shape[0]):
        lane = slice(c * LANES, (c + 1) * LANES)
        total = sum(part[:, lane].astype(F32) for part in last)
        new_ref[:, lane] = total / jnp.exp(logw_ref[c : c + 1, :])


def position(n):
    return (n // 2) + (n % 2) * (7 - 2 * (n // 2))


def device_at(p):
    p = p % 8
    return 2 * p - (p // 4) * (4 * p - 15)


def turn(x, step):
    return lax.ppermute(x, NEW, [(i, device_at(position(i) + step)) for i in range(8)])


def halves(x):
    width = x.shape[1] // 2
    return [x[:, :width], x[:, width:]]


def gather_old(x):
    first = halves(x)
    up, down = list(first), list(first)
    behind, ahead, opposite = [], [], [None, None]
    for hop in (1, 2, 3, 4):
        for h in (0, 1):
            if hop < 4 or h == 0:
                up[h] = turn(up[h], 1)
            if hop < 4 or h == 1:
                down[h] = turn(down[h], -1)
        if hop < 4:
            behind.append(list(up))
            ahead.append(list(down))
    opposite = [up[0], down[1]]
    return [first, *ahead, opposite, *behind[::-1]]


def gather_new(x):
    across = swap(x, OLD, 4, 2, None)
    return [x, across, swap(x, OLD, 4, 1, None), swap(across, OLD, 4, 1, None)]


def scatter_old(far, near):
    four, up3, down3 = far
    up = {3: up3, 2: near[0], 1: near[2]}
    down = {3: down3, 2: near[1], 1: near[3]}
    last = [[near[4][0]], [near[4][1]]]
    for h in (0, 1):
        for blocks, step, start in ((up, 1, 4 - h), (down, -1, 3 + h)):
            x = four[h] if start == 4 else blocks[3][h]
            for hop in range(start, 0, -1):
                x = turn(x.astype(BF16), step)
                if hop > 1:
                    x = blocks[hop - 1][h] + x.astype(F32)
            last[h].append(x)
    return last


def integers(values):
    return jnp.stack([jnp.asarray(v, jnp.int32) for v in values])


def is_tuned(n_old, n_new):
    return (n_old, n_new) == (4, 8)


def per_device(n_old, n_new, old_emb, new_emb, old_logw, new_logw):
    tuned = is_tuned(n_old, n_new)
    width, height = old_logw.shape[0], new_logw.shape[0]
    wide, tall = width // LANES, height // LANES
    depth = old_emb.shape[0] * n_new
    scale = 1.0 / (math.sqrt(depth) * EPSILON)
    if tuned:
        old_slots, new_slots = gather_old(old_emb), gather_new(new_emb)
        p, me = position(lax.axis_index(NEW)), lax.axis_index(OLD)
        owners = [device_at(p + i) for i in range(8)] + [me, me ^ 2, me ^ 1, me ^ 3]
    else:
        old_all = lax.all_gather(old_emb, NEW, axis=0, tiled=True)
        old_slots = [[old_all[: depth // 2]], [old_all[depth // 2 :]]]
        new_slots = [lax.all_gather(new_emb, OLD, axis=0, tiled=True)]
        owners = [0, 1, 0]
    held = len(owners)
    if tuned:
        owners = owners + [device_at(p + i) for i in (4, 3, -3, 2, -2, 1, -1, 0)]
        for o in (me ^ 3, me ^ 2, me ^ 1, me):
            owners = owners + [(position(2 * o + i) - p) % 8 for i in (0, 1)]
    where = integers(owners)
    old_w = old_logw.reshape(wide, LANES)
    new_w = new_logw.reshape(tall, LANES)
    cells = width * height
    n_slots = len(old_slots)
    message = (n_new, wide, LANES)
    new_rows, new_full = call(
        functools.partial(prepare_kernel, n_slots),
        [((height, depth), BF16, True), ((depth, height), BF16, True)],
        [pltpu.VMEM((depth, height), BF16)],
        [(where, SM)] + [(x, VM) for x in new_slots],
        8,
        flops=cells,
        nbytes=8 * depth * height,
    )
    lt, k, old_full, a, msg = call(
        functools.partial(logits_kernel, [len(slot) for slot in old_slots], scale),
        [
            ((height, width), F32, True),
            ((height, width), F32, True),
            ((depth, width), BF16, True),
            ((wide, LANES), F32, True),
            (message, F32, False),
        ],
        [pltpu.VMEM((wide, LANES), F32)] + [pltpu.VMEM((height, 2 * LANES), F32)] * 2,
        [(new_rows, STAY)] + [(x, VM) for slot in old_slots for x in slot],
        8,
        flops=2 * cells * depth,
        nbytes=12 * cells,
        exps=cells,
    )

    def over_old(message):
        return [message] + [swap(message, OLD, n_old, d) for d in range(1, n_old)]

    chunk = [pltpu.VMEM((LANES, width), F32), pltpu.SemaphoreType.DMA]
    for step in range(ITERS):
        got = lax.all_to_all(msg, NEW, 0, 0, tiled=True)
        f, f_near, columns = call(
            column_kernel,
            [((wide, LANES), F32, False), ((wide, LANES), F32, True), ((tall, LANES), F32, False)],
            [pltpu.VMEM((wide, LANES), F32)] + chunk,
            [(got, VM), (a, STAY), (old_w, VM), (k, STAY), (lt, ANY)],
            6,
            flops=2 * cells,
            nbytes=4 * cells,
        )
        columns = over_old(columns)
        if step + 1 < ITERS:
            (msg,) = call(
                functools.partial(row_kernel, n_old),
                [(message, F32, False)],
                [pltpu.VMEM((tall, LANES), F32)] * 2
                + [pltpu.VMEM((wide, LANES), F32)] * 2
                + chunk,
                [(c, VM) for c in columns]
                + [(new_w, VM), (a, STAY), (k, STAY), (lt, ANY)],
                6,
                flops=2 * cells,
                nbytes=4 * cells,
            )
    r = depth // n_new
    types = (BF16, BF16, F32, BF16, BF16, F32) if tuned else ()
    g, plan, mass, *far = call(
        functools.partial(plan_kernel, n_old, held),
        [
            ((tall, LANES), F32, False),
            ((height, width), BF16, True),
            ((wide, LANES), F32, False),
        ]
        + [((r, width // 2), dtype, False) for dtype in types],
        [pltpu.VMEM((max(1, len(types) // 2) * r, height), BF16), pltpu.VMEM((height, LANES), F32)],
        [(where, SM)]
        + [(c, VM) for c in columns]
        + [(new_w, VM), (f_near, STAY), (lt, STAY), (new_full, STAY)],
        8,
        flops=2 * cells * (1 + r * len(types) // 2),
        nbytes=6 * cells,
        exps=cells,
    )
    far = [far[i : i + 2] for i in range(0, len(far), 2)]
    if tuned:

        def old_part(base, types):
            got = call(
                functools.partial(old_terms_kernel, base),
                [((r, width // 2), dtype, False) for dtype in types],
                [pltpu.VMEM((len(types) // 2 * r, height), BF16)],
                [(where, SM), (new_full, STAY), (plan, STAY)],
                16,
                flops=cells * r * len(types),
                nbytes=2 * cells,
            )
            return [got[i : i + 2] for i in range(0, len(got), 2)]

        for d in (1, 2, 4):
            mass = mass + swap(mass, NEW, 8, d, None)
        old_parts = scatter_old(far, old_part(held + 3, (F32,) * 10))
        q = depth // n_old


        def new_part(base):
            away, own = call(
                functools.partial(new_terms_kernel, base, 4),
                [((q, height), BF16, False), ((q, height), F32, False)],
                [pltpu.VMEM((2 * q, width), BF16)],
                [(where, SM), (old_full, STAY), (plan, STAY)],
                16,
                flops=cells * depth,
                nbytes=4 * cells,
            )
            return own, swap(away, OLD, 4, 1, None)

        own, core = new_part(held + 8)
        far = swap((own + core.astype(F32)).astype(BF16), OLD, 4, 2, None)
        new_parts = [*new_part(held + 12), far]
        old_map, new_map = call(
            maps_kernel,
            [((r, width), F32, False), ((q, height), F32, False)],
            [],
            [(mass, VM), (new_w, VM)] + [(x, VM) for x in (*old_parts[0], *old_parts[1], *new_parts)],
            8,
            flops=8 * r * width,
            nbytes=16 * r * width,
        )
    else:
        mass = lax.psum(mass, NEW)
        old_terms = jnp.dot(new_full, plan, preferred_element_type=F32)
        new_terms = lax.dot_general(
            old_full, plan, (((1,), (1,)), ((), ())), preferred_element_type=F32
        )
        old_sums = lax.psum_scatter(old_terms, NEW, scatter_dimension=0, tiled=True)
        new_sums = lax.psum_scatter(new_terms, OLD, scatter_dimension=0, tiled=True)
        old_map = old_sums / mass.reshape(width)[None, :]
        new_map = new_sums / jnp.exp(new_logw)[None, :]
    return (f.reshape(width), g.reshape(height), old_map, new_map)


def solution(mesh):
    in_specs = (P(NEW, OLD), P(OLD, NEW), P(OLD), P(NEW))
    out_specs = (P(OLD), P(NEW), P(NEW, OLD), P(OLD, NEW))
    n_old, n_new = mesh.shape[OLD], mesh.shape[NEW]
    return jax.shard_map(
        functools.partial(per_device, n_old, n_new),
        mesh=mesh,
        in_specs=in_specs,
        out_specs=out_specs,
        check_vma=False,
    )
```

```python
import functools
import math

import jax
import jax.numpy as jnp
from jax import lax
from jax.experimental import pallas as pl
from jax.experimental.pallas import tpu as pltpu
from jax.sharding import PartitionSpec as P

ITERS = 3
EPSILON = 0.5
LANES = 128
SAFE = 1e-20
BF16 = jnp.bfloat16
F32 = jnp.float32
OLD, NEW = "old", "new"
MIB = 2**20
STAY, VM, SM, ANY = range(4)


def call(kernel, outs, scratch, args, limit, flops=0, nbytes=0, exps=0, aliases=None):
    out_shape, arrays, in_specs = [], [], []
    for shape, dtype, resident in outs:
        out_shape.append(
            pltpu.VMEM(shape, dtype) if resident else jax.ShapeDtypeStruct(shape, dtype)
        )
    for array, where in args:
        if where == STAY:
            array = pltpu.with_memory_space_constraint(array, pltpu.VMEM)
        arrays.append(array)
        space = {SM: pltpu.SMEM, ANY: pl.ANY}.get(where, pltpu.VMEM)
        in_specs.append(pl.BlockSpec(memory_space=space))
    return pl.pallas_call(
        kernel,
        out_shape=tuple(out_shape),
        in_specs=in_specs,
        out_specs=tuple(pl.BlockSpec(memory_space=pltpu.VMEM) for _ in outs),
        scratch_shapes=scratch,
        input_output_aliases=aliases or {},
        compiler_params=pltpu.CompilerParams(vmem_limit_bytes=limit * MIB),
        cost_estimate=pl.CostEstimate(flops=flops, bytes_accessed=nbytes, transcendentals=exps),
    )(*arrays)


def diagonal():
    shape = (LANES, LANES)
    return lax.broadcasted_iota(jnp.int32, shape, 0) == lax.broadcasted_iota(jnp.int32, shape, 1)


def to_column(row8, eye):
    rows = jnp.concatenate([row8] * (LANES // 8), axis=0)
    return jnp.sum(jnp.where(eye, rows, 0.0), axis=1, keepdims=True)


def to_row(column, eye):
    return jnp.sum(jnp.where(eye, column, 0.0), axis=0, keepdims=True)


def folded(tile, op):
    return op(tile.reshape(LANES // 8, 8, LANES), axis=0)


def repeated(ref, row):
    return ref[pl.ds(row, 8, stride=0), :]


def spread(row8):
    return jnp.concatenate([row8] * (LANES // 8), axis=0)


def place(pieces, places, out_ref):
    for piece, (row, column) in zip(pieces, places):
        r, w = piece.shape
        out_ref[row : row + r, column : column + w] = piece[...]


def prepare_kernel(n_slots, where_ref, *refs):
    new_refs, (left_ref, right_ref, nf_ref, ns_ref) = refs[:-4], refs[-4:]
    _, rows = nf_ref.shape
    for p, piece in enumerate(new_refs):
        r = piece.shape[0]
        start = pl.multiple_of(where_ref[2 * n_slots + p] * r, r)
        nf_ref[pl.ds(start, r), :] = piece[...]
    for h, nt_ref in enumerate((left_ref, right_ref)):
        take_rows(h * n_slots, where_ref, nf_ref, ns_ref, n_slots)
        for c in range(rows // LANES):
            nt_ref[c * LANES : (c + 1) * LANES, :] = ns_ref[:, c * LANES : (c + 1) * LANES].T


def early_kernel(places, known, left_ref, right_ref, *refs):
    pieces, (part_ref, of_ref) = refs[:-2], refs[-2:]
    place(pieces, places, of_ref)
    wide = 2 * LANES
    half = of_ref.shape[1] // 2
    for h, nt_ref in enumerate((left_ref, right_ref)):

        def block(b, carry, h=h, nt_ref=nt_ref):
            at = pl.ds(pl.multiple_of(h * half + b * wide, wide), wide)
            part_ref[:, at] = jnp.dot(
                nt_ref[:, :known], of_ref[:known, at], preferred_element_type=F32
            )
            return carry

        lax.fori_loop(0, half // wide, block, 0)


def logits_kernel(places, known, scale, part_ref, before_ref, left_ref, right_ref, *refs):
    pieces, (lt_ref, k_ref, of_ref, a_ref, msg_ref, m_ref) = refs[:-6], refs[-6:]
    columns = of_ref.shape[1]
    rows = left_ref.shape[0]
    place(pieces, places, of_ref)
    wide = 2 * LANES

    def product(c):
        at = slice(c * LANES, c * LANES + wide)
        nt_ref = left_ref if 2 * c * LANES < columns else right_ref
        got = jnp.dot(nt_ref[:, known:], of_ref[known:, at], preferred_element_type=F32)
        lt_ref[:, at] = (part_ref[:, at] + got) * scale

    def exponentials(c):
        lane = slice(c * LANES, (c + 1) * LANES)
        top = jnp.full((8, LANES), -jnp.inf, F32)
        for j in range(rows // LANES):
            top = jnp.maximum(top, folded(lt_ref[j * LANES : (j + 1) * LANES, lane], jnp.max))
        top = jnp.max(top, axis=0, keepdims=True)
        a_ref[c : c + 1, :] = top
        high = spread(jnp.broadcast_to(top, (8, LANES)))
        total = jnp.zeros((8, LANES), F32)
        for j in range(rows // LANES):
            down = slice(j * LANES, (j + 1) * LANES)
            tile = jnp.exp(lt_ref[down, lane] - high)
            k_ref[down, lane] = tile
            total = total + folded(tile, jnp.sum)
        m_ref[c : c + 1, :] = jnp.sum(total, axis=0, keepdims=True)

    product(0)
    for c in range(0, columns // LANES, 2):
        if c + 2 < columns // LANES:
            product(c + 2)
        exponentials(c)
        exponentials(c + 1)
    put_message(msg_ref, a_ref[...] + jnp.log(m_ref[...]))


def put_message(msg_ref, message):
    for d in range(msg_ref.shape[0]):
        msg_ref[d] = message


def combine(parts):
    peak = functools.reduce(jnp.maximum, parts)
    sums = [jnp.exp(x - peak) for x in parts]
    while len(sums) > 1:
        sums = [sums[i] + sums[i + 1] for i in range(0, len(sums), 2)]
    return peak + jnp.log(sums[0])


def column_kernel(*refs):
    got_ref, a_ref, logw_ref, k_ref, lt_hbm, f_ref, near_ref, msg_ref, w_ref, chunk_ref, sem = refs
    wide = a_ref.shape[0]
    tall = k_ref.shape[0] // LANES
    f = logw_ref[...] - combine([got_ref[d] for d in range(got_ref.shape[0])])
    f_ref[...] = f
    near_ref[...] = f
    fa = f + a_ref[...]
    high = jnp.max(jnp.max(fa, axis=1, keepdims=True), axis=0, keepdims=True)
    w_ref[...] = jnp.exp(fa - high)
    eye = diagonal()

    least = jnp.full((1, LANES), jnp.inf, F32)
    for j in range(tall):
        acc = jnp.zeros((LANES // 8, 8, LANES), F32)
        for c in range(wide):
            tile = k_ref[j * LANES : (j + 1) * LANES, c * LANES : (c + 1) * LANES]
            acc = acc + tile.reshape(LANES // 8, 8, LANES) * repeated(w_ref, c)[None]
        total = to_row(jnp.sum(acc.reshape(LANES, LANES), axis=1, keepdims=True), eye)
        msg_ref[j : j + 1, :] = total
        least = jnp.minimum(least, total)
    msg_ref[...] = high + jnp.log(msg_ref[...])

    @pl.when(jnp.logical_not(jnp.min(least) > SAFE))
    def _():
        def exact(j, carry):
            at = pl.ds(pl.multiple_of(j * LANES, LANES), LANES)
            copy = pltpu.make_async_copy(lt_hbm.at[at, :], chunk_ref, sem)
            copy.start()
            copy.wait()
            top = jnp.full((LANES, LANES), -jnp.inf, F32)
            for c in range(wide):
                lane = slice(c * LANES, (c + 1) * LANES)
                shifted = chunk_ref[:, lane] + spread(repeated(f_ref, c))
                chunk_ref[:, lane] = shifted
                top = jnp.maximum(top, shifted)
            top = jnp.max(top, axis=1, keepdims=True)
            acc = jnp.zeros((LANES, LANES), F32)
            for c in range(wide):
                acc = acc + jnp.exp(chunk_ref[:, c * LANES : (c + 1) * LANES] - top)
            total = top + jnp.log(jnp.sum(acc, axis=1, keepdims=True))
            msg_ref[pl.ds(j, 1), :] = to_row(total, eye)
            return carry

        lax.fori_loop(0, tall, exact, 0)


def row_kernel(n_got, *refs):
    got_refs, refs = refs[:n_got], refs[n_got:]
    logw_ref, a_ref, k_ref, lt_hbm, msg_ref, g_ref, v_ref, m_ref, top_ref, chunk_ref, sem = refs
    wide = a_ref.shape[0]
    tall = k_ref.shape[0] // LANES
    g = logw_ref[...] - combine([r[...] for r in got_refs])
    g_ref[...] = g
    high = jnp.max(jnp.max(g, axis=1, keepdims=True), axis=0, keepdims=True)
    v_ref[...] = jnp.exp(g - high)
    eye = diagonal()

    acc = [jnp.zeros((8, LANES), F32)] * wide
    for j in range(tall):
        v = to_column(repeated(v_ref, j), eye)
        for c in range(wide):
            tile = k_ref[j * LANES : (j + 1) * LANES, c * LANES : (c + 1) * LANES]
            acc[c] = acc[c] + folded(tile * v, jnp.sum)
    least = jnp.full((1, LANES), jnp.inf, F32)
    for c in range(wide):
        total = jnp.sum(acc[c], axis=0, keepdims=True)
        m_ref[c : c + 1, :] = total
        least = jnp.minimum(least, total)
    put_message(msg_ref, (a_ref[...] + high) + jnp.log(m_ref[...]))

    @pl.when(jnp.logical_not(jnp.min(least) > SAFE))
    def _():
        m_ref[...] = jnp.zeros((wide, LANES), F32)
        top_ref[...] = jnp.full((wide, LANES), -jnp.inf, F32)

        def exact(j, carry):
            at = pl.ds(pl.multiple_of(j * LANES, LANES), LANES)
            copy = pltpu.make_async_copy(lt_hbm.at[at, :], chunk_ref, sem)
            copy.start()
            copy.wait()
            column = to_column(repeated(g_ref, j), eye)
            for c in range(wide):
                row = slice(c, c + 1)
                shifted = chunk_ref[:, c * LANES : (c + 1) * LANES] + column
                before = top_ref[row, :]
                top = jnp.maximum(before, jnp.max(shifted, axis=0, keepdims=True))
                top_ref[row, :] = top
                more = jnp.sum(jnp.exp(shifted - top), axis=0, keepdims=True)
                m_ref[row, :] = m_ref[row, :] * jnp.exp(before - top) + more
            return carry

        lax.fori_loop(0, tall, exact, 0)
        put_message(msg_ref, top_ref[...] + jnp.log(m_ref[...]))


def plan_kernel(n_got, base, where_ref, *refs):
    got_refs, refs = refs[:n_got], refs[n_got:]
    logw_ref, f_ref, lt_ref, nf_ref, g_ref, p_ref, mass_ref = refs[:7]
    outs, (lhs_ref, column_ref) = refs[7:-2], refs[-2:]
    wide = f_ref.shape[0]
    tall = lt_ref.shape[0] // LANES
    g_ref[...] = logw_ref[...] - combine([r[...] for r in got_refs])
    eye = diagonal()
    for j in range(tall):
        column = to_column(repeated(g_ref, j), eye)
        column_ref[j * LANES : (j + 1) * LANES, :] = jnp.broadcast_to(column, (LANES, LANES))
    take_rows(base, where_ref, nf_ref, lhs_ref, len(outs) // 2)

    def plan(c):
        lane = slice(c * LANES, (c + 1) * LANES)
        row = spread(repeated(f_ref, c))
        total = jnp.zeros((8, LANES), F32)
        for j in range(tall):
            at = slice(j * LANES, (j + 1) * LANES)
            tile = jnp.exp(lt_ref[at, lane] + row + column_ref[at, :])
            p_ref[at, lane] = tile.astype(BF16)
            total = total + folded(tile, jnp.sum)
        mass_ref[c : c + 1, :] = jnp.sum(total, axis=0, keepdims=True)

    for c in range(0, wide, 2):
        plan(c)
        plan(c + 1)
        if c and outs:
            product(c - 2, p_ref, lhs_ref, outs)
    if outs:
        product(wide - 2, p_ref, lhs_ref, outs)


def take_rows(base, where_ref, nf_ref, lhs_ref, blocks):
    for k in range(blocks):
        r = lhs_ref.shape[0] // blocks
        lhs_ref[k * r : (k + 1) * r, :] = nf_ref[
            pl.ds(pl.multiple_of(where_ref[base + k] * r, r), r), :
        ]


def product(c, p_ref, lhs_ref, outs):
    r, half = outs[0].shape
    got = jnp.dot(
        lhs_ref[...], p_ref[:, c * LANES : (c + 2) * LANES], preferred_element_type=F32
    )
    h = c * LANES // half
    here = slice(c * LANES - h * half, (c + 2) * LANES - h * half)
    for k, out in enumerate(outs[h::2]):
        out[:, here] = got[k * r : (k + 1) * r, :].astype(out.dtype)


def old_terms_kernel(base, where_ref, nf_ref, p_ref, *refs):
    outs, lhs_ref = refs[:-1], refs[-1]
    blocks = len(outs) // 2
    r, half = outs[0].shape
    for k in range(blocks):
        lhs_ref[k * r : (k + 1) * r, :] = nf_ref[
            pl.ds(pl.multiple_of(where_ref[base + k] * r, r), r), :
        ]
    wide = 2 * LANES
    for h in range(2):

        def block(b, carry, h=h):
            at = pl.ds(pl.multiple_of(h * half + b * wide, wide), wide)
            here = pl.ds(pl.multiple_of(b * wide, wide), wide)
            got = jnp.dot(lhs_ref[...], p_ref[:, at], preferred_element_type=F32)
            for k in range(blocks):
                out = outs[2 * k + h]
                out[:, here] = got[k * r : (k + 1) * r, :].astype(out.dtype)
            return carry

        lax.fori_loop(0, half // wide, block, 0)


def new_terms_kernel(base, pieces, where_ref, of_ref, p_ref, away_ref, own_ref, lhs_ref):
    q, w = own_ref.shape
    r = lhs_ref.shape[0] // pieces
    half = of_ref.shape[1] // 2
    for h in range(2):
        side = slice(h * half, (h + 1) * half)
        for k in range(pieces):
            start = pl.multiple_of(where_ref[base + h * pieces + k] * r, r)
            lhs_ref[k * r : (k + 1) * r, side] = of_ref[pl.ds(start, r), side]
    wide = 2 * LANES

    def block(b, carry):
        at = pl.ds(pl.multiple_of(b * wide, wide), wide)
        got = lax.dot_general(
            lhs_ref[...], p_ref[at, :], (((1,), (1,)), ((), ())), preferred_element_type=F32
        )
        away_ref[:, at] = got[:q, :].astype(away_ref.dtype)
        own_ref[:, at] = got[q:, :]
        return carry

    lax.fori_loop(0, w // wide, block, 0)


def swap(x, axis, size, mask, only=None):
    return lax.ppermute(x, axis, [(i, i ^ mask) for i in range(size) if only is None or only(i)])


def maps_kernel(mass_ref, logw_ref, *refs):
    left, right, last, (old_ref, new_ref) = refs[:3], refs[3:6], refs[6:9], refs[9:]
    half = left[0].shape[1] // LANES
    for h, parts in enumerate((left, right)):
        for c in range(half):
            lane = slice(c * LANES, (c + 1) * LANES)
            out = slice((h * half + c) * LANES, (h * half + c + 1) * LANES)
            total = sum(part[:, lane].astype(F32) for part in parts)
            old_ref[:, out] = total / mass_ref[h * half + c : h * half + c + 1, :]
    for c in range(logw_ref.shape[0]):
        lane = slice(c * LANES, (c + 1) * LANES)
        total = sum(part[:, lane].astype(F32) for part in last)
        new_ref[:, lane] = total / jnp.exp(logw_ref[c : c + 1, :])


def position(n):
    return (n // 2) + (n % 2) * (7 - 2 * (n // 2))


def device_at(p):
    p = p % 8
    return 2 * p - (p // 4) * (4 * p - 15)


def turn(x, step):
    return lax.ppermute(x, NEW, [(i, device_at(position(i) + step)) for i in range(8)])


def halves(x):
    width = x.shape[1] // 2
    return [x[:, :width], x[:, width:]]


STACKS = ((0, 1, 7, 2, 6, 5, 4, 3), (0, 1, 7, 2, 6, 3, 4, 5))
EARLY = 6


def looked_up(table, index):
    return sum(jnp.where(index == i, value, 0) for i, value in enumerate(table))


def gather_old(x):
    first = halves(x)
    up, down = list(first), list(first)
    behind, ahead, opposite = [], [], [None, None]
    for hop in (1, 2, 3, 4):
        for h in (0, 1):
            if hop < 4 or h == 0:
                up[h] = turn(up[h], 1)
            if hop < 4 or h == 1:
                down[h] = turn(down[h], -1)
        if hop < 4:
            behind.append(list(up))
            ahead.append(list(down))
    opposite = [up[0], down[1]]
    return [first, *ahead, opposite, *behind[::-1]]


def gather_new(x):
    across = swap(x, OLD, 4, 2, None)
    return [x, across, swap(x, OLD, 4, 1, None), swap(across, OLD, 4, 1, None)]


def scatter_old(far, near):
    four, up3, down3 = far
    up = {3: up3, 2: near[0], 1: near[2]}
    down = {3: down3, 2: near[1], 1: near[3]}
    last = [[near[4][0]], [near[4][1]]]
    for h in (0, 1):
        for blocks, step, start in ((up, 1, 4 - h), (down, -1, 3 + h)):
            x = four[h] if start == 4 else blocks[3][h]
            for hop in range(start, 0, -1):
                x = turn(x.astype(BF16), step)
                if hop > 1:
                    x = blocks[hop - 1][h] + x.astype(F32)
            last[h].append(x)
    return last


def integers(values):
    return jnp.stack([jnp.asarray(v, jnp.int32) for v in values])


def is_tuned(n_old, n_new):
    return (n_old, n_new) == (4, 8)


def per_device(n_old, n_new, old_emb, new_emb, old_logw, new_logw):
    tuned = is_tuned(n_old, n_new)
    width, height = old_logw.shape[0], new_logw.shape[0]
    wide, tall = width // LANES, height // LANES
    depth = old_emb.shape[0] * n_new
    scale = 1.0 / (math.sqrt(depth) * EPSILON)
    if tuned:
        old_slots, new_slots = gather_old(old_emb), gather_new(new_emb)
        p, me = position(lax.axis_index(NEW)), lax.axis_index(OLD)
        owners = [device_at(p + i) for stack in STACKS for i in stack]
        owners = owners + [me, me ^ 2, me ^ 1, me ^ 3]
    else:
        old_all = lax.all_gather(old_emb, NEW, axis=0, tiled=True)
        old_slots = [[old_all[: depth // 2]], [old_all[depth // 2 :]]]
        new_slots = [lax.all_gather(new_emb, OLD, axis=0, tiled=True)]
        owners = [0, 1, 0, 1, 0]
    held = len(owners)
    if tuned:
        owners = owners + [device_at(p + i) for i in (4, 3, -3, 2, -2, 1, -1, 0)]
        for pair in ((me ^ 3, me ^ 2), (me ^ 1, me)):
            ahead = [(position(2 * o + i) - p) % 8 for o in pair for i in (0, 1)]
            for stack in STACKS:
                slot = [stack.index(i) for i in range(8)]
                owners = owners + [looked_up(slot, i) for i in ahead]
    where = integers(owners)
    old_w = old_logw.reshape(wide, LANES)
    new_w = new_logw.reshape(tall, LANES)
    cells = width * height
    n_slots = len(old_slots)
    rows = depth // n_slots
    if tuned:
        stacked = [
            (old_slots[stack[i]][h], (i * rows, h * (width // 2)), i < EARLY)
            for h, stack in enumerate(STACKS)
            for i in range(n_slots)
        ]
        known = (EARLY - 1) * rows // LANES * LANES + LANES
    else:
        stacked = [(slot[0], (i * rows, 0), i == 0) for i, slot in enumerate(old_slots)]
        known = rows
    early = [(x, at) for x, at, there in stacked if there]
    late = [(x, at) for x, at, there in stacked if not there]
    message = (n_new, wide, LANES)
    *new_rows, new_full = call(
        functools.partial(prepare_kernel, n_slots),
        [((height, depth), BF16, True)] * 2 + [((depth, height), BF16, True)],
        [pltpu.VMEM((depth, height), BF16)],
        [(where, SM)] + [(x, VM) for x in new_slots],
        8,
        flops=cells,
        nbytes=8 * depth * height,
    )
    part, part_full = call(
        functools.partial(early_kernel, [at for _, at in early], known),
        [((height, width), F32, True), ((depth, width), BF16, True)],
        [],
        [(x, STAY) for x in new_rows] + [(x, VM) for x, _ in early],
        4,
        flops=2 * cells * known,
        nbytes=4 * cells,
    )
    lt, k, old_full, a, msg = call(
        functools.partial(logits_kernel, [at for _, at in late], known, scale),
        [
            ((height, width), F32, True),
            ((height, width), F32, True),
            ((depth, width), BF16, True),
            ((wide, LANES), F32, True),
            (message, F32, False),
        ],
        [pltpu.VMEM((wide, LANES), F32)],
        [(part, STAY), (part_full, STAY)]
        + [(x, STAY) for x in new_rows]
        + [(x, VM) for x, _ in late],
        8,
        flops=2 * cells * (depth - known),
        nbytes=12 * cells,
        exps=cells,
        aliases={0: 0, 1: 2},
    )

    def over_old(message):
        return [message] + [swap(message, OLD, n_old, d) for d in range(1, n_old)]

    chunk = [pltpu.VMEM((LANES, width), F32), pltpu.SemaphoreType.DMA]
    for step in range(ITERS):
        got = lax.all_to_all(msg, NEW, 0, 0, tiled=True)
        f, f_near, columns = call(
            column_kernel,
            [((wide, LANES), F32, False), ((wide, LANES), F32, True), ((tall, LANES), F32, False)],
            [pltpu.VMEM((wide, LANES), F32)] + chunk,
            [(got, VM), (a, STAY), (old_w, VM), (k, STAY), (lt, ANY)],
            6,
            flops=2 * cells,
            nbytes=4 * cells,
        )
        columns = over_old(columns)
        if step + 1 < ITERS:
            (msg,) = call(
                functools.partial(row_kernel, n_old),
                [(message, F32, False)],
                [pltpu.VMEM((tall, LANES), F32)] * 2
                + [pltpu.VMEM((wide, LANES), F32)] * 2
                + chunk,
                [(c, VM) for c in columns]
                + [(new_w, VM), (a, STAY), (k, STAY), (lt, ANY)],
                6,
                flops=2 * cells,
                nbytes=4 * cells,
            )
    r = depth // n_new
    types = (BF16, BF16, F32, BF16, BF16, F32) if tuned else ()
    g, plan, mass, *far = call(
        functools.partial(plan_kernel, n_old, held),
        [
            ((tall, LANES), F32, False),
            ((height, width), BF16, True),
            ((wide, LANES), F32, False),
        ]
        + [((r, width // 2), dtype, False) for dtype in types],
        [pltpu.VMEM((max(1, len(types) // 2) * r, height), BF16), pltpu.VMEM((height, LANES), F32)],
        [(where, SM)]
        + [(c, VM) for c in columns]
        + [(new_w, VM), (f_near, STAY), (lt, STAY), (new_full, STAY)],
        8,
        flops=2 * cells * (1 + r * len(types) // 2),
        nbytes=6 * cells,
        exps=cells,
    )
    far = [far[i : i + 2] for i in range(0, len(far), 2)]
    if tuned:

        def old_part(base, types):
            got = call(
                functools.partial(old_terms_kernel, base),
                [((r, width // 2), dtype, False) for dtype in types],
                [pltpu.VMEM((len(types) // 2 * r, height), BF16)],
                [(where, SM), (new_full, STAY), (plan, STAY)],
                16,
                flops=cells * r * len(types),
                nbytes=2 * cells,
            )
            return [got[i : i + 2] for i in range(0, len(got), 2)]

        for d in (1, 2, 4):
            mass = mass + swap(mass, NEW, 8, d, None)
        old_parts = scatter_old(far, old_part(held + 3, (F32,) * 10))
        q = depth // n_old


        def new_part(base):
            away, own = call(
                functools.partial(new_terms_kernel, base, 4),
                [((q, height), BF16, False), ((q, height), F32, False)],
                [pltpu.VMEM((2 * q, width), BF16)],
                [(where, SM), (old_full, STAY), (plan, STAY)],
                16,
                flops=cells * depth,
                nbytes=4 * cells,
            )
            return own, swap(away, OLD, 4, 1, None)

        own, core = new_part(held + 8)
        far = swap((own + core.astype(F32)).astype(BF16), OLD, 4, 2, None)
        new_parts = [*new_part(held + 16), far]
        old_map, new_map = call(
            maps_kernel,
            [((r, width), F32, False), ((q, height), F32, False)],
            [],
            [(mass, VM), (new_w, VM)] + [(x, VM) for x in (*old_parts[0], *old_parts[1], *new_parts)],
            8,
            flops=8 * r * width,
            nbytes=16 * r * width,
        )
    else:
        mass = lax.psum(mass, NEW)
        old_terms = jnp.dot(new_full, plan, preferred_element_type=F32)
        new_terms = lax.dot_general(
            old_full, plan, (((1,), (1,)), ((), ())), preferred_element_type=F32
        )
        old_sums = lax.psum_scatter(old_terms, NEW, scatter_dimension=0, tiled=True)
        new_sums = lax.psum_scatter(new_terms, OLD, scatter_dimension=0, tiled=True)
        old_map = old_sums / mass.reshape(width)[None, :]
        new_map = new_sums / jnp.exp(new_logw)[None, :]
    return (f.reshape(width), g.reshape(height), old_map, new_map)


def solution(mesh):
    in_specs = (P(NEW, OLD), P(OLD, NEW), P(OLD), P(NEW))
    out_specs = (P(OLD), P(NEW), P(NEW, OLD), P(OLD, NEW))
    n_old, n_new = mesh.shape[OLD], mesh.shape[NEW]
    return jax.shard_map(
        functools.partial(per_device, n_old, n_new),
        mesh=mesh,
        in_specs=in_specs,
        out_specs=out_specs,
        check_vma=False,
    )
```

```python
import functools
import math

import jax
import jax.numpy as jnp
from jax import lax
from jax.experimental import pallas as pl
from jax.experimental.pallas import tpu as pltpu
from jax.sharding import PartitionSpec as P

ITERS = 3
EPSILON = 0.5
LANES = 128
SAFE = 1e-20
BF16 = jnp.bfloat16
F32 = jnp.float32
OLD, NEW = "old", "new"
MIB = 2**20
STAY, VM, SM, ANY, HBM = range(2, 7)


def call(kernel, outs, scratch, args, limit, flops=0, nbytes=0, exps=0, aliases=None):
    out_shape, arrays, in_specs = [], [], []
    for shape, dtype, resident in outs:
        out_shape.append(
            pltpu.VMEM(shape, dtype) if resident is True else jax.ShapeDtypeStruct(shape, dtype)
        )
    for array, where in args:
        if where == STAY:
            array = pltpu.with_memory_space_constraint(array, pltpu.VMEM)
        if where == HBM:
            array = pltpu.with_memory_space_constraint(array, pltpu.HBM)
        arrays.append(array)
        space = {SM: pltpu.SMEM, ANY: pl.ANY, HBM: pl.ANY}.get(where, pltpu.VMEM)
        in_specs.append(pl.BlockSpec(memory_space=space))
    return pl.pallas_call(
        kernel,
        out_shape=tuple(out_shape),
        in_specs=in_specs,
        out_specs=tuple(
            pl.BlockSpec(memory_space=pl.ANY if where == ANY else pltpu.VMEM) for _, _, where in outs
        ),
        scratch_shapes=scratch,
        input_output_aliases=aliases or {},
        compiler_params=pltpu.CompilerParams(vmem_limit_bytes=limit * MIB),
        cost_estimate=pl.CostEstimate(flops=flops, bytes_accessed=nbytes, transcendentals=exps),
    )(*arrays)


def diagonal():
    shape = (LANES, LANES)
    return lax.broadcasted_iota(jnp.int32, shape, 0) == lax.broadcasted_iota(jnp.int32, shape, 1)


def to_column(row8, eye):
    rows = jnp.concatenate([row8] * (LANES // 8), axis=0)
    return jnp.sum(jnp.where(eye, rows, 0.0), axis=1, keepdims=True)


def to_row(column, eye):
    return jnp.sum(jnp.where(eye, column, 0.0), axis=0, keepdims=True)


def folded(tile, op):
    return op(tile.reshape(LANES // 8, 8, LANES), axis=0)


def repeated(ref, row):
    return ref[pl.ds(row, 8, stride=0), :]


def spread(row8):
    return jnp.concatenate([row8] * (LANES // 8), axis=0)


def cut_kernel(x_hbm, left_ref, right_ref, sems):
    half = left_ref.shape[1]
    copies = [
        pltpu.make_async_copy(x_hbm.at[:, :half], left_ref, sems.at[0]),
        pltpu.make_async_copy(x_hbm.at[:, half:], right_ref, sems.at[1]),
    ]
    for copy in copies:
        copy.start()
    for copy in copies:
        copy.wait()


def place(pieces, places, out_ref):
    for piece, (row, column) in zip(pieces, places):
        r, w = piece.shape
        out_ref[row : row + r, column : column + w] = piece[...]


def prepare_kernel(n_slots, where_ref, *refs):
    new_refs, (left_ref, right_ref, nf_ref, ns_ref) = refs[:-4], refs[-4:]
    _, rows = nf_ref.shape
    for p, piece in enumerate(new_refs):
        r = piece.shape[0]
        start = pl.multiple_of(where_ref[2 * n_slots + p] * r, r)
        nf_ref[pl.ds(start, r), :] = piece[...]
    for h, nt_ref in enumerate((left_ref, right_ref)):
        take_rows(h * n_slots, where_ref, nf_ref, ns_ref, n_slots)
        for c in range(rows // LANES):
            nt_ref[c * LANES : (c + 1) * LANES, :] = ns_ref[:, c * LANES : (c + 1) * LANES].T


def early_kernel(places, known, left_ref, right_ref, *refs):
    pieces, (part_ref, of_ref) = refs[:-2], refs[-2:]
    place(pieces, places, of_ref)
    wide = 2 * LANES
    half = of_ref.shape[1] // 2
    for h, nt_ref in enumerate((left_ref, right_ref)):

        def block(b, carry, h=h, nt_ref=nt_ref):
            at = pl.ds(pl.multiple_of(h * half + b * wide, wide), wide)
            part_ref[:, at] = jnp.dot(
                nt_ref[:, :known], of_ref[:known, at], preferred_element_type=F32
            )
            return carry

        lax.fori_loop(0, half // wide, block, 0)


def logits_kernel(places, known, scale, part_ref, before_ref, left_ref, right_ref, *refs):
    pieces, (lt_ref, k_ref, of_ref, a_ref, msg_ref, m_ref) = refs[:-6], refs[-6:]
    columns = of_ref.shape[1]
    rows = left_ref.shape[0]
    place(pieces, places, of_ref)
    wide = 2 * LANES

    def product(c):
        at = slice(c * LANES, c * LANES + wide)
        nt_ref = left_ref if 2 * c * LANES < columns else right_ref
        got = jnp.dot(nt_ref[:, known:], of_ref[known:, at], preferred_element_type=F32)
        lt_ref[:, at] = (part_ref[:, at] + got) * scale

    def exponentials(c):
        lane = slice(c * LANES, (c + 1) * LANES)
        top = jnp.full((8, LANES), -jnp.inf, F32)
        for j in range(rows // LANES):
            top = jnp.maximum(top, folded(lt_ref[j * LANES : (j + 1) * LANES, lane], jnp.max))
        top = jnp.max(top, axis=0, keepdims=True)
        a_ref[c : c + 1, :] = top
        high = spread(jnp.broadcast_to(top, (8, LANES)))
        total = jnp.zeros((8, LANES), F32)
        for j in range(rows // LANES):
            down = slice(j * LANES, (j + 1) * LANES)
            tile = jnp.exp(lt_ref[down, lane] - high)
            k_ref[down, lane] = tile
            total = total + folded(tile, jnp.sum)
        m_ref[c : c + 1, :] = jnp.sum(total, axis=0, keepdims=True)

    product(0)
    for c in range(0, columns // LANES, 2):
        if c + 2 < columns // LANES:
            product(c + 2)
        exponentials(c)
        exponentials(c + 1)
    put_message(msg_ref, a_ref[...] + jnp.log(m_ref[...]))


def put_message(msg_ref, message):
    for d in range(msg_ref.shape[0]):
        msg_ref[d] = message


def combine(parts):
    peak = functools.reduce(jnp.maximum, parts)
    sums = [jnp.exp(x - peak) for x in parts]
    while len(sums) > 1:
        sums = [sums[i] + sums[i + 1] for i in range(0, len(sums), 2)]
    return peak + jnp.log(sums[0])


def column_kernel(*refs):
    got_ref, a_ref, logw_ref, k_ref, lt_hbm, f_ref, near_ref, msg_ref, w_ref, chunk_ref, sem = refs
    wide = a_ref.shape[0]
    tall = k_ref.shape[0] // LANES
    f = logw_ref[...] - combine([got_ref[d] for d in range(got_ref.shape[0])])
    f_ref[...] = f
    near_ref[...] = f
    fa = f + a_ref[...]
    high = jnp.max(jnp.max(fa, axis=1, keepdims=True), axis=0, keepdims=True)
    w_ref[...] = jnp.exp(fa - high)
    eye = diagonal()

    least = jnp.full((1, LANES), jnp.inf, F32)
    for j in range(tall):
        acc = jnp.zeros((LANES // 8, 8, LANES), F32)
        for c in range(wide):
            tile = k_ref[j * LANES : (j + 1) * LANES, c * LANES : (c + 1) * LANES]
            acc = acc + tile.reshape(LANES // 8, 8, LANES) * repeated(w_ref, c)[None]
        total = to_row(jnp.sum(acc.reshape(LANES, LANES), axis=1, keepdims=True), eye)
        msg_ref[j : j + 1, :] = total
        least = jnp.minimum(least, total)
    msg_ref[...] = high + jnp.log(msg_ref[...])

    @pl.when(jnp.logical_not(jnp.min(least) > SAFE))
    def _():
        def exact(j, carry):
            at = pl.ds(pl.multiple_of(j * LANES, LANES), LANES)
            copy = pltpu.make_async_copy(lt_hbm.at[at, :], chunk_ref, sem)
            copy.start()
            copy.wait()
            top = jnp.full((LANES, LANES), -jnp.inf, F32)
            for c in range(wide):
                lane = slice(c * LANES, (c + 1) * LANES)
                shifted = chunk_ref[:, lane] + spread(repeated(f_ref, c))
                chunk_ref[:, lane] = shifted
                top = jnp.maximum(top, shifted)
            top = jnp.max(top, axis=1, keepdims=True)
            acc = jnp.zeros((LANES, LANES), F32)
            for c in range(wide):
                acc = acc + jnp.exp(chunk_ref[:, c * LANES : (c + 1) * LANES] - top)
            total = top + jnp.log(jnp.sum(acc, axis=1, keepdims=True))
            msg_ref[pl.ds(j, 1), :] = to_row(total, eye)
            return carry

        lax.fori_loop(0, tall, exact, 0)


def row_kernel(n_got, *refs):
    got_refs, refs = refs[:n_got], refs[n_got:]
    logw_ref, a_ref, k_ref, lt_hbm, msg_ref, g_ref, v_ref, m_ref, top_ref, chunk_ref, sem = refs
    wide = a_ref.shape[0]
    tall = k_ref.shape[0] // LANES
    g = logw_ref[...] - combine([r[...] for r in got_refs])
    g_ref[...] = g
    high = jnp.max(jnp.max(g, axis=1, keepdims=True), axis=0, keepdims=True)
    v_ref[...] = jnp.exp(g - high)
    eye = diagonal()

    acc = [jnp.zeros((8, LANES), F32)] * wide
    for j in range(tall):
        v = to_column(repeated(v_ref, j), eye)
        for c in range(wide):
            tile = k_ref[j * LANES : (j + 1) * LANES, c * LANES : (c + 1) * LANES]
            acc[c] = acc[c] + folded(tile * v, jnp.sum)
    least = jnp.full((1, LANES), jnp.inf, F32)
    for c in range(wide):
        total = jnp.sum(acc[c], axis=0, keepdims=True)
        m_ref[c : c + 1, :] = total
        least = jnp.minimum(least, total)
    put_message(msg_ref, (a_ref[...] + high) + jnp.log(m_ref[...]))

    @pl.when(jnp.logical_not(jnp.min(least) > SAFE))
    def _():
        m_ref[...] = jnp.zeros((wide, LANES), F32)
        top_ref[...] = jnp.full((wide, LANES), -jnp.inf, F32)

        def exact(j, carry):
            at = pl.ds(pl.multiple_of(j * LANES, LANES), LANES)
            copy = pltpu.make_async_copy(lt_hbm.at[at, :], chunk_ref, sem)
            copy.start()
            copy.wait()
            column = to_column(repeated(g_ref, j), eye)
            for c in range(wide):
                row = slice(c, c + 1)
                shifted = chunk_ref[:, c * LANES : (c + 1) * LANES] + column
                before = top_ref[row, :]
                top = jnp.maximum(before, jnp.max(shifted, axis=0, keepdims=True))
                top_ref[row, :] = top
                more = jnp.sum(jnp.exp(shifted - top), axis=0, keepdims=True)
                m_ref[row, :] = m_ref[row, :] * jnp.exp(before - top) + more
            return carry

        lax.fori_loop(0, tall, exact, 0)
        put_message(msg_ref, top_ref[...] + jnp.log(m_ref[...]))


def plan_kernel(n_got, base, where_ref, *refs):
    got_refs, refs = refs[:n_got], refs[n_got:]
    logw_ref, f_ref, lt_ref, nf_ref, g_ref, p_ref, mass_ref = refs[:7]
    outs, (lhs_ref, column_ref) = refs[7:-2], refs[-2:]
    wide = f_ref.shape[0]
    tall = lt_ref.shape[0] // LANES
    g_ref[...] = logw_ref[...] - combine([r[...] for r in got_refs])
    eye = diagonal()
    for j in range(tall):
        column = to_column(repeated(g_ref, j), eye)
        column_ref[j * LANES : (j + 1) * LANES, :] = jnp.broadcast_to(column, (LANES, LANES))
    take_rows(base, where_ref, nf_ref, lhs_ref, len(outs) // 2)

    def plan(c):
        lane = slice(c * LANES, (c + 1) * LANES)
        row = spread(repeated(f_ref, c))
        total = jnp.zeros((8, LANES), F32)
        for j in range(tall):
            at = slice(j * LANES, (j + 1) * LANES)
            tile = jnp.exp(lt_ref[at, lane] + row + column_ref[at, :])
            p_ref[at, lane] = tile.astype(BF16)
            total = total + folded(tile, jnp.sum)
        mass_ref[c : c + 1, :] = jnp.sum(total, axis=0, keepdims=True)

    for c in range(0, wide, 2):
        plan(c)
        plan(c + 1)
        if c and outs:
            product(c - 2, p_ref, lhs_ref, outs)
    if outs:
        product(wide - 2, p_ref, lhs_ref, outs)


def take_rows(base, where_ref, nf_ref, lhs_ref, blocks):
    for k in range(blocks):
        r = lhs_ref.shape[0] // blocks
        lhs_ref[k * r : (k + 1) * r, :] = nf_ref[
            pl.ds(pl.multiple_of(where_ref[base + k] * r, r), r), :
        ]


def product(c, p_ref, lhs_ref, outs):
    r, half = outs[0].shape
    got = jnp.dot(
        lhs_ref[...], p_ref[:, c * LANES : (c + 2) * LANES], preferred_element_type=F32
    )
    h = c * LANES // half
    here = slice(c * LANES - h * half, (c + 2) * LANES - h * half)
    for k, out in enumerate(outs[h::2]):
        out[:, here] = got[k * r : (k + 1) * r, :].astype(out.dtype)


def old_terms_kernel(base, where_ref, nf_ref, p_ref, *refs):
    outs, lhs_ref = refs[:-1], refs[-1]
    blocks = len(outs) // 2
    r, half = outs[0].shape
    for k in range(blocks):
        lhs_ref[k * r : (k + 1) * r, :] = nf_ref[
            pl.ds(pl.multiple_of(where_ref[base + k] * r, r), r), :
        ]
    wide = 2 * LANES
    for h in range(2):

        def block(b, carry, h=h):
            at = pl.ds(pl.multiple_of(h * half + b * wide, wide), wide)
            here = pl.ds(pl.multiple_of(b * wide, wide), wide)
            got = jnp.dot(lhs_ref[...], p_ref[:, at], preferred_element_type=F32)
            for k in range(blocks):
                out = outs[2 * k + h]
                out[:, here] = got[k * r : (k + 1) * r, :].astype(out.dtype)
            return carry

        lax.fori_loop(0, half // wide, block, 0)


def new_terms_kernel(base, pieces, where_ref, of_ref, p_ref, away_ref, own_ref, lhs_ref):
    q, w = own_ref.shape
    r = lhs_ref.shape[0] // pieces
    half = of_ref.shape[1] // 2
    for h in range(2):
        side = slice(h * half, (h + 1) * half)
        for k in range(pieces):
            start = pl.multiple_of(where_ref[base + h * pieces + k] * r, r)
            lhs_ref[k * r : (k + 1) * r, side] = of_ref[pl.ds(start, r), side]
    wide = 2 * LANES

    def block(b, carry):
        at = pl.ds(pl.multiple_of(b * wide, wide), wide)
        got = lax.dot_general(
            lhs_ref[...], p_ref[at, :], (((1,), (1,)), ((), ())), preferred_element_type=F32
        )
        away_ref[:, at] = got[:q, :].astype(away_ref.dtype)
        own_ref[:, at] = got[q:, :]
        return carry

    lax.fori_loop(0, w // wide, block, 0)


def swap(x, axis, size, mask, only=None):
    return lax.ppermute(x, axis, [(i, i ^ mask) for i in range(size) if only is None or only(i)])


def maps_kernel(mass_ref, logw_ref, *refs):
    parts, (old_hbm, new_hbm, left_ref, right_ref, last_ref, sems) = refs[:9], refs[9:]
    width = left_ref.shape[1]
    copies = [
        pltpu.make_async_copy(last_ref, new_hbm, sems.at[0]),
        pltpu.make_async_copy(left_ref, old_hbm.at[:, :width], sems.at[1]),
        pltpu.make_async_copy(right_ref, old_hbm.at[:, width:], sems.at[2]),
    ]
    order = ((last_ref, parts[6:]), (left_ref, parts[:3]), (right_ref, parts[3:6]))
    for i, (out_ref, terms) in enumerate(order):
        for c in range(out_ref.shape[1] // LANES):
            lane = slice(c * LANES, (c + 1) * LANES)
            total = sum(term[:, lane].astype(F32) for term in terms)
            if i == 0:
                out_ref[:, lane] = total / jnp.exp(logw_ref[c : c + 1, :])
            else:
                row = (i - 1) * (width // LANES) + c
                out_ref[:, lane] = total / mass_ref[row : row + 1, :]
        copies[i].start()
    for copy in copies:
        copy.wait()


def position(n):
    return (n // 2) + (n % 2) * (7 - 2 * (n // 2))


def device_at(p):
    p = p % 8
    return 2 * p - (p // 4) * (4 * p - 15)


def turn(x, step):
    return lax.ppermute(x, NEW, [(i, device_at(position(i) + step)) for i in range(8)])


STACKS = ((0, 1, 7, 2, 6, 5, 4, 3), (0, 1, 7, 2, 6, 3, 4, 5))
EARLY = 6


def looked_up(table, index):
    return sum(jnp.where(index == i, value, 0) for i, value in enumerate(table))


def gather_old(first):
    up, down = list(first), list(first)
    behind, ahead, opposite = [], [], [None, None]
    for hop in (1, 2, 3, 4):
        for h in (0, 1):
            if hop < 4 or h == 0:
                up[h] = turn(up[h], 1)
            if hop < 4 or h == 1:
                down[h] = turn(down[h], -1)
        if hop < 4:
            behind.append(list(up))
            ahead.append(list(down))
    opposite = [up[0], down[1]]
    return [first, *ahead, opposite, *behind[::-1]]


def gather_new(x):
    across = swap(x, OLD, 4, 2, None)
    return [x, across, swap(x, OLD, 4, 1, None), swap(across, OLD, 4, 1, None)]


def scatter_old(far, near):
    four, up3, down3 = far
    up = {3: up3, 2: near[0], 1: near[2]}
    down = {3: down3, 2: near[1], 1: near[3]}
    last = [[near[4][0]], [near[4][1]]]
    for h in (0, 1):
        for blocks, step, start in ((up, 1, 4 - h), (down, -1, 3 + h)):
            x = four[h] if start == 4 else blocks[3][h]
            for hop in range(start, 0, -1):
                x = turn(x.astype(BF16), step)
                if hop > 1:
                    x = blocks[hop - 1][h] + x.astype(F32)
            last[h].append(x)
    return last


def integers(values):
    return jnp.stack([jnp.asarray(v, jnp.int32) for v in values])


def is_tuned(n_old, n_new):
    return (n_old, n_new) == (4, 8)


def per_device(n_old, n_new, old_emb, new_emb, old_logw, new_logw):
    tuned = is_tuned(n_old, n_new)
    width, height = old_logw.shape[0], new_logw.shape[0]
    wide, tall = width // LANES, height // LANES
    depth = old_emb.shape[0] * n_new
    scale = 1.0 / (math.sqrt(depth) * EPSILON)
    if tuned:
        own = call(
            cut_kernel,
            [((old_emb.shape[0], width // 2), BF16, True)] * 2,
            [pltpu.SemaphoreType.DMA((2,))],
            [(old_emb, HBM)],
            2,
            nbytes=4 * old_emb.size,
        )
        old_slots, new_slots = gather_old(own), gather_new(new_emb)
        p, me = position(lax.axis_index(NEW)), lax.axis_index(OLD)
        owners = [device_at(p + i) for stack in STACKS for i in stack]
        owners = owners + [me, me ^ 2, me ^ 1, me ^ 3]
    else:
        old_all = lax.all_gather(old_emb, NEW, axis=0, tiled=True)
        old_slots = [[old_all[: depth // 2]], [old_all[depth // 2 :]]]
        new_slots = [lax.all_gather(new_emb, OLD, axis=0, tiled=True)]
        owners = [0, 1, 0, 1, 0]
    held = len(owners)
    if tuned:
        owners = owners + [device_at(p + i) for i in (4, 3, -3, 2, -2, 1, -1, 0)]
        for pair in ((me ^ 3, me ^ 2), (me ^ 1, me)):
            ahead = [(position(2 * o + i) - p) % 8 for o in pair for i in (0, 1)]
            for stack in STACKS:
                slot = [stack.index(i) for i in range(8)]
                owners = owners + [looked_up(slot, i) for i in ahead]
    where = integers(owners)
    old_w = old_logw.reshape(wide, LANES)
    new_w = new_logw.reshape(tall, LANES)
    cells = width * height
    n_slots = len(old_slots)
    rows = depth // n_slots
    if tuned:
        stacked = [
            (old_slots[stack[i]][h], (i * rows, h * (width // 2)), i < EARLY)
            for h, stack in enumerate(STACKS)
            for i in range(n_slots)
        ]
        known = (EARLY - 1) * rows // LANES * LANES + LANES
    else:
        stacked = [(slot[0], (i * rows, 0), i == 0) for i, slot in enumerate(old_slots)]
        known = rows
    early = [(x, at) for x, at, there in stacked if there]
    late = [(x, at) for x, at, there in stacked if not there]
    message = (n_new, wide, LANES)
    *new_rows, new_full = call(
        functools.partial(prepare_kernel, n_slots),
        [((height, depth), BF16, True)] * 2 + [((depth, height), BF16, True)],
        [pltpu.VMEM((depth, height), BF16)],
        [(where, SM)] + [(x, VM) for x in new_slots],
        8,
        flops=cells,
        nbytes=8 * depth * height,
    )
    part, part_full = call(
        functools.partial(early_kernel, [at for _, at in early], known),
        [((height, width), F32, True), ((depth, width), BF16, True)],
        [],
        [(x, STAY) for x in new_rows] + [(x, VM) for x, _ in early],
        4,
        flops=2 * cells * known,
        nbytes=4 * cells,
    )
    lt, k, old_full, a, msg = call(
        functools.partial(logits_kernel, [at for _, at in late], known, scale),
        [
            ((height, width), F32, True),
            ((height, width), F32, True),
            ((depth, width), BF16, True),
            ((wide, LANES), F32, True),
            (message, F32, False),
        ],
        [pltpu.VMEM((wide, LANES), F32)],
        [(part, STAY), (part_full, STAY)]
        + [(x, STAY) for x in new_rows]
        + [(x, VM) for x, _ in late],
        8,
        flops=2 * cells * (depth - known),
        nbytes=12 * cells,
        exps=cells,
        aliases={0: 0, 1: 2},
    )

    def over_old(message):
        return [message] + [swap(message, OLD, n_old, d, None) for d in range(1, n_old)]

    chunk = [pltpu.VMEM((LANES, width), F32), pltpu.SemaphoreType.DMA]
    for step in range(ITERS):
        got = lax.all_to_all(msg, NEW, 0, 0, tiled=True)
        f, f_near, columns = call(
            column_kernel,
            [((wide, LANES), F32, False), ((wide, LANES), F32, True), ((tall, LANES), F32, False)],
            [pltpu.VMEM((wide, LANES), F32)] + chunk,
            [(got, VM), (a, STAY), (old_w, VM), (k, STAY), (lt, ANY)],
            6,
            flops=2 * cells,
            nbytes=4 * cells,
        )
        columns = over_old(columns)
        if step + 1 < ITERS:
            (msg,) = call(
                functools.partial(row_kernel, n_old),
                [(message, F32, False)],
                [pltpu.VMEM((tall, LANES), F32)] * 2
                + [pltpu.VMEM((wide, LANES), F32)] * 2
                + chunk,
                [(c, VM) for c in columns]
                + [(new_w, VM), (a, STAY), (k, STAY), (lt, ANY)],
                6,
                flops=2 * cells,
                nbytes=4 * cells,
            )
    r = depth // n_new
    types = (BF16, BF16, F32, BF16, BF16, F32) if tuned else ()
    g, plan, mass, *far = call(
        functools.partial(plan_kernel, n_old, held),
        [
            ((tall, LANES), F32, False),
            ((height, width), BF16, True),
            ((wide, LANES), F32, False),
        ]
        + [((r, width // 2), dtype, False) for dtype in types],
        [pltpu.VMEM((max(1, len(types) // 2) * r, height), BF16), pltpu.VMEM((height, LANES), F32)],
        [(where, SM)]
        + [(c, VM) for c in columns]
        + [(new_w, VM), (f_near, STAY), (lt, STAY), (new_full, STAY)],
        8,
        flops=2 * cells * (1 + r * len(types) // 2),
        nbytes=6 * cells,
        exps=cells,
    )
    far = [far[i : i + 2] for i in range(0, len(far), 2)]
    if tuned:

        def old_part(base, types):
            got = call(
                functools.partial(old_terms_kernel, base),
                [((r, width // 2), dtype, False) for dtype in types],
                [pltpu.VMEM((len(types) // 2 * r, height), BF16)],
                [(where, SM), (new_full, STAY), (plan, STAY)],
                16,
                flops=cells * r * len(types),
                nbytes=2 * cells,
            )
            return [got[i : i + 2] for i in range(0, len(got), 2)]

        for d in (1, 2, 4):
            mass = mass + swap(mass, NEW, 8, d, None)
        old_parts = scatter_old(far, old_part(held + 3, (F32,) * 10))
        q = depth // n_old


        def new_part(base):
            away, own = call(
                functools.partial(new_terms_kernel, base, 4),
                [((q, height), BF16, False), ((q, height), F32, False)],
                [pltpu.VMEM((2 * q, width), BF16)],
                [(where, SM), (old_full, STAY), (plan, STAY)],
                16,
                flops=cells * depth,
                nbytes=4 * cells,
            )
            return own, swap(away, OLD, 4, 1, None)

        own, core = new_part(held + 8)
        far = swap((own + core.astype(F32)).astype(BF16), OLD, 4, 2, None)
        new_parts = [*new_part(held + 16), far]
        old_map, new_map = call(
            maps_kernel,
            [((r, width), F32, ANY), ((q, height), F32, ANY)],
            [pltpu.VMEM((r, width // 2), F32)] * 2
            + [pltpu.VMEM((q, height), F32), pltpu.SemaphoreType.DMA((3,))],
            [(mass, VM), (new_w, VM)] + [(x, VM) for x in (*old_parts[0], *old_parts[1], *new_parts)],
            8,
            flops=8 * r * width,
            nbytes=16 * r * width,
        )
    else:
        mass = lax.psum(mass, NEW)
        old_terms = jnp.dot(new_full, plan, preferred_element_type=F32)
        new_terms = lax.dot_general(
            old_full, plan, (((1,), (1,)), ((), ())), preferred_element_type=F32
        )
        old_sums = lax.psum_scatter(old_terms, NEW, scatter_dimension=0, tiled=True)
        new_sums = lax.psum_scatter(new_terms, OLD, scatter_dimension=0, tiled=True)
        old_map = old_sums / mass.reshape(width)[None, :]
        new_map = new_sums / jnp.exp(new_logw)[None, :]
    return (f.reshape(width), g.reshape(height), old_map, new_map)


def solution(mesh):
    in_specs = (P(NEW, OLD), P(OLD, NEW), P(OLD), P(NEW))
    out_specs = (P(OLD), P(NEW), P(NEW, OLD), P(OLD, NEW))
    n_old, n_new = mesh.shape[OLD], mesh.shape[NEW]
    return jax.shard_map(
        functools.partial(per_device, n_old, n_new),
        mesh=mesh,
        in_specs=in_specs,
        out_specs=out_specs,
        check_vma=False,
    )
```

```python
import functools
import math

import jax
import jax.numpy as jnp
from jax import lax
from jax.experimental import pallas as pl
from jax.experimental.pallas import tpu as pltpu
from jax.sharding import PartitionSpec as P

ITERS = 3
EPSILON = 0.5
LANES = 128
SAFE = 1e-20
BF16 = jnp.bfloat16
F32 = jnp.float32
OLD, NEW = "old", "new"
MIB = 2**20
STAY, VM, SM, ANY, HBM = range(2, 7)


def call(kernel, outs, scratch, args, limit, flops=0, nbytes=0, exps=0, aliases=None):
    out_shape, arrays, in_specs = [], [], []
    for shape, dtype, resident in outs:
        out_shape.append(
            pltpu.VMEM(shape, dtype) if resident is True else jax.ShapeDtypeStruct(shape, dtype)
        )
    for array, where in args:
        if where == STAY:
            array = pltpu.with_memory_space_constraint(array, pltpu.VMEM)
        if where == HBM:
            array = pltpu.with_memory_space_constraint(array, pltpu.HBM)
        arrays.append(array)
        space = {SM: pltpu.SMEM, ANY: pl.ANY, HBM: pl.ANY}.get(where, pltpu.VMEM)
        in_specs.append(pl.BlockSpec(memory_space=space))
    return pl.pallas_call(
        kernel,
        out_shape=tuple(out_shape),
        in_specs=in_specs,
        out_specs=tuple(
            pl.BlockSpec(memory_space=pl.ANY if where == ANY else pltpu.VMEM) for _, _, where in outs
        ),
        scratch_shapes=scratch,
        input_output_aliases=aliases or {},
        compiler_params=pltpu.CompilerParams(vmem_limit_bytes=limit * MIB),
        cost_estimate=pl.CostEstimate(flops=flops, bytes_accessed=nbytes, transcendentals=exps),
    )(*arrays)


def diagonal():
    shape = (LANES, LANES)
    return lax.broadcasted_iota(jnp.int32, shape, 0) == lax.broadcasted_iota(jnp.int32, shape, 1)


def to_column(row8, eye):
    rows = jnp.concatenate([row8] * (LANES // 8), axis=0)
    return jnp.sum(jnp.where(eye, rows, 0.0), axis=1, keepdims=True)


def to_row(column, eye):
    return jnp.sum(jnp.where(eye, column, 0.0), axis=0, keepdims=True)


def folded(tile, op):
    return op(tile.reshape(LANES // 8, 8, LANES), axis=0)


def repeated(ref, row):
    return ref[pl.ds(row, 8, stride=0), :]


def spread(row8):
    return jnp.concatenate([row8] * (LANES // 8), axis=0)


def cut_kernel(x_hbm, left_ref, right_ref, sems):
    half = left_ref.shape[1]
    copies = [
        pltpu.make_async_copy(x_hbm.at[:, :half], left_ref, sems.at[0]),
        pltpu.make_async_copy(x_hbm.at[:, half:], right_ref, sems.at[1]),
    ]
    for copy in copies:
        copy.start()
    for copy in copies:
        copy.wait()


def place(pieces, places, out_ref):
    for piece, (row, column) in zip(pieces, places):
        r, w = piece.shape
        out_ref[row : row + r, column : column + w] = piece[...]


def prepare_kernel(n_slots, where_ref, *refs):
    new_refs, (left_ref, right_ref, nf_ref, ns_ref) = refs[:-4], refs[-4:]
    _, rows = nf_ref.shape
    for p, piece in enumerate(new_refs):
        r = piece.shape[0]
        start = pl.multiple_of(where_ref[2 * n_slots + p] * r, r)
        nf_ref[pl.ds(start, r), :] = piece[...]
    for h, nt_ref in enumerate((left_ref, right_ref)):
        take_rows(h * n_slots, where_ref, nf_ref, ns_ref, n_slots)
        for c in range(rows // LANES):
            nt_ref[c * LANES : (c + 1) * LANES, :] = ns_ref[:, c * LANES : (c + 1) * LANES].T


def early_kernel(places, known, left_ref, right_ref, *refs):
    pieces, (part_ref, of_ref) = refs[:-2], refs[-2:]
    place(pieces, places, of_ref)
    wide = 2 * LANES
    half = of_ref.shape[1] // 2
    for h, nt_ref in enumerate((left_ref, right_ref)):

        def block(b, carry, h=h, nt_ref=nt_ref):
            at = pl.ds(pl.multiple_of(h * half + b * wide, wide), wide)
            part_ref[:, at] = jnp.dot(
                nt_ref[:, :known], of_ref[:known, at], preferred_element_type=F32
            )
            return carry

        lax.fori_loop(0, half // wide, block, 0)


def logits_kernel(places, known, scale, part_ref, before_ref, left_ref, right_ref, *refs):
    pieces, (lt_ref, k_ref, of_ref, a_ref, msg_ref, m_ref) = refs[:-6], refs[-6:]
    columns = of_ref.shape[1]
    rows = left_ref.shape[0]
    place(pieces, places, of_ref)
    wide = 2 * LANES

    def product(c):
        at = slice(c * LANES, c * LANES + wide)
        nt_ref = left_ref if 2 * c * LANES < columns else right_ref
        got = jnp.dot(nt_ref[:, known:], of_ref[known:, at], preferred_element_type=F32)
        lt_ref[:, at] = (part_ref[:, at] + got) * scale

    def exponentials(c):
        lane = slice(c * LANES, (c + 1) * LANES)
        top = jnp.full((8, LANES), -jnp.inf, F32)
        for j in range(rows // LANES):
            top = jnp.maximum(top, folded(lt_ref[j * LANES : (j + 1) * LANES, lane], jnp.max))
        top = jnp.max(top, axis=0, keepdims=True)
        a_ref[c : c + 1, :] = top
        high = spread(jnp.broadcast_to(top, (8, LANES)))
        total = jnp.zeros((8, LANES), F32)
        for j in range(rows // LANES):
            down = slice(j * LANES, (j + 1) * LANES)
            tile = jnp.exp(lt_ref[down, lane] - high)
            k_ref[down, lane] = tile
            total = total + folded(tile, jnp.sum)
        m_ref[c : c + 1, :] = jnp.sum(total, axis=0, keepdims=True)

    product(0)
    for c in range(0, columns // LANES, 2):
        if c + 2 < columns // LANES:
            product(c + 2)
        exponentials(c)
        exponentials(c + 1)
    put_message(msg_ref, a_ref[...] + jnp.log(m_ref[...]))


def put_message(msg_ref, message):
    for d in range(msg_ref.shape[0]):
        msg_ref[d] = message


def combine(parts):
    peak = functools.reduce(jnp.maximum, parts)
    sums = [jnp.exp(x - peak) for x in parts]
    while len(sums) > 1:
        sums = [sums[i] + sums[i + 1] for i in range(0, len(sums), 2)]
    return peak + jnp.log(sums[0])


def column_kernel(keep, *refs):
    got_ref, a_ref, logw_ref, k_ref, lt_hbm, f_ref, msg_ref, w_ref, chunk_ref, sem = refs
    if not keep:
        f_ref, msg_ref = msg_ref, f_ref
    wide = a_ref.shape[0]
    tall = k_ref.shape[0] // LANES
    f = logw_ref[...] - combine([got_ref[d] for d in range(got_ref.shape[0])])
    f_ref[...] = f
    fa = f + a_ref[...]
    high = jnp.max(jnp.max(fa, axis=1, keepdims=True), axis=0, keepdims=True)
    w_ref[...] = jnp.exp(fa - high)
    eye = diagonal()

    least = jnp.full((1, LANES), jnp.inf, F32)
    for j in range(tall):
        acc = jnp.zeros((LANES // 8, 8, LANES), F32)
        for c in range(wide):
            tile = k_ref[j * LANES : (j + 1) * LANES, c * LANES : (c + 1) * LANES]
            acc = acc + tile.reshape(LANES // 8, 8, LANES) * repeated(w_ref, c)[None]
        total = to_row(jnp.sum(acc.reshape(LANES, LANES), axis=1, keepdims=True), eye)
        msg_ref[j : j + 1, :] = total
        least = jnp.minimum(least, total)
    msg_ref[...] = high + jnp.log(msg_ref[...])

    @pl.when(jnp.logical_not(jnp.min(least) > SAFE))
    def _():
        def exact(j, carry):
            at = pl.ds(pl.multiple_of(j * LANES, LANES), LANES)
            copy = pltpu.make_async_copy(lt_hbm.at[at, :], chunk_ref, sem)
            copy.start()
            copy.wait()
            top = jnp.full((LANES, LANES), -jnp.inf, F32)
            for c in range(wide):
                lane = slice(c * LANES, (c + 1) * LANES)
                shifted = chunk_ref[:, lane] + spread(repeated(f_ref, c))
                chunk_ref[:, lane] = shifted
                top = jnp.maximum(top, shifted)
            top = jnp.max(top, axis=1, keepdims=True)
            acc = jnp.zeros((LANES, LANES), F32)
            for c in range(wide):
                acc = acc + jnp.exp(chunk_ref[:, c * LANES : (c + 1) * LANES] - top)
            total = top + jnp.log(jnp.sum(acc, axis=1, keepdims=True))
            msg_ref[pl.ds(j, 1), :] = to_row(total, eye)
            return carry

        lax.fori_loop(0, tall, exact, 0)


def row_kernel(n_got, *refs):
    got_refs, refs = refs[:n_got], refs[n_got:]
    logw_ref, a_ref, k_ref, lt_hbm, msg_ref, g_ref, v_ref, m_ref, top_ref, chunk_ref, sem = refs
    wide = a_ref.shape[0]
    tall = k_ref.shape[0] // LANES
    g = logw_ref[...] - combine([r[...] for r in got_refs])
    g_ref[...] = g
    high = jnp.max(jnp.max(g, axis=1, keepdims=True), axis=0, keepdims=True)
    v_ref[...] = jnp.exp(g - high)
    eye = diagonal()

    acc = [jnp.zeros((8, LANES), F32)] * wide
    for j in range(tall):
        v = to_column(repeated(v_ref, j), eye)
        for c in range(wide):
            tile = k_ref[j * LANES : (j + 1) * LANES, c * LANES : (c + 1) * LANES]
            acc[c] = acc[c] + folded(tile * v, jnp.sum)
    least = jnp.full((1, LANES), jnp.inf, F32)
    for c in range(wide):
        total = jnp.sum(acc[c], axis=0, keepdims=True)
        m_ref[c : c + 1, :] = total
        least = jnp.minimum(least, total)
    put_message(msg_ref, (a_ref[...] + high) + jnp.log(m_ref[...]))

    @pl.when(jnp.logical_not(jnp.min(least) > SAFE))
    def _():
        m_ref[...] = jnp.zeros((wide, LANES), F32)
        top_ref[...] = jnp.full((wide, LANES), -jnp.inf, F32)

        def exact(j, carry):
            at = pl.ds(pl.multiple_of(j * LANES, LANES), LANES)
            copy = pltpu.make_async_copy(lt_hbm.at[at, :], chunk_ref, sem)
            copy.start()
            copy.wait()
            column = to_column(repeated(g_ref, j), eye)
            for c in range(wide):
                row = slice(c, c + 1)
                shifted = chunk_ref[:, c * LANES : (c + 1) * LANES] + column
                before = top_ref[row, :]
                top = jnp.maximum(before, jnp.max(shifted, axis=0, keepdims=True))
                top_ref[row, :] = top
                more = jnp.sum(jnp.exp(shifted - top), axis=0, keepdims=True)
                m_ref[row, :] = m_ref[row, :] * jnp.exp(before - top) + more
            return carry

        lax.fori_loop(0, tall, exact, 0)
        put_message(msg_ref, top_ref[...] + jnp.log(m_ref[...]))


def plan_kernel(n_got, base, where_ref, *refs):
    got_refs, refs = refs[:n_got], refs[n_got:]
    logw_ref, f_ref, lt_ref, nf_ref, g_ref, p_ref, mass_ref = refs[:7]
    outs, (lhs_ref, column_ref) = refs[7:-2], refs[-2:]
    wide = f_ref.shape[0]
    tall = lt_ref.shape[0] // LANES
    g_ref[...] = logw_ref[...] - combine([r[...] for r in got_refs])
    eye = diagonal()
    for j in range(tall):
        column = to_column(repeated(g_ref, j), eye)
        column_ref[j * LANES : (j + 1) * LANES, :] = jnp.broadcast_to(column, (LANES, LANES))
    take_rows(base, where_ref, nf_ref, lhs_ref, len(outs) // 2)

    def plan(c):
        lane = slice(c * LANES, (c + 1) * LANES)
        row = spread(repeated(f_ref, c))
        total = jnp.zeros((8, LANES), F32)
        for j in range(tall):
            at = slice(j * LANES, (j + 1) * LANES)
            tile = jnp.exp(lt_ref[at, lane] + row + column_ref[at, :])
            p_ref[at, lane] = tile.astype(BF16)
            total = total + folded(tile, jnp.sum)
        mass_ref[c : c + 1, :] = jnp.sum(total, axis=0, keepdims=True)

    for c in range(0, wide, 2):
        plan(c)
        plan(c + 1)
        if c and outs:
            product(c - 2, p_ref, lhs_ref, outs)
    if outs:
        product(wide - 2, p_ref, lhs_ref, outs)


def take_rows(base, where_ref, nf_ref, lhs_ref, blocks):
    for k in range(blocks):
        r = lhs_ref.shape[0] // blocks
        lhs_ref[k * r : (k + 1) * r, :] = nf_ref[
            pl.ds(pl.multiple_of(where_ref[base + k] * r, r), r), :
        ]


def product(c, p_ref, lhs_ref, outs):
    r, half = outs[0].shape
    got = jnp.dot(
        lhs_ref[...], p_ref[:, c * LANES : (c + 2) * LANES], preferred_element_type=F32
    )
    h = c * LANES // half
    here = slice(c * LANES - h * half, (c + 2) * LANES - h * half)
    for k, out in enumerate(outs[h::2]):
        out[:, here] = got[k * r : (k + 1) * r, :].astype(out.dtype)


def old_terms_kernel(base, where_ref, nf_ref, p_ref, *refs):
    outs, lhs_ref = refs[:-1], refs[-1]
    blocks = len(outs) // 2
    r, half = outs[0].shape
    for k in range(blocks):
        lhs_ref[k * r : (k + 1) * r, :] = nf_ref[
            pl.ds(pl.multiple_of(where_ref[base + k] * r, r), r), :
        ]
    wide = 2 * LANES
    for h in range(2):

        def block(b, carry, h=h):
            at = pl.ds(pl.multiple_of(h * half + b * wide, wide), wide)
            here = pl.ds(pl.multiple_of(b * wide, wide), wide)
            got = jnp.dot(lhs_ref[...], p_ref[:, at], preferred_element_type=F32)
            for k in range(blocks):
                out = outs[2 * k + h]
                out[:, here] = got[k * r : (k + 1) * r, :].astype(out.dtype)
            return carry

        lax.fori_loop(0, half // wide, block, 0)


def new_terms_kernel(base, pieces, where_ref, of_ref, p_ref, away_ref, own_ref, lhs_ref):
    q, w = own_ref.shape
    r = lhs_ref.shape[0] // pieces
    half = of_ref.shape[1] // 2
    for h in range(2):
        side = slice(h * half, (h + 1) * half)
        for k in range(pieces):
            start = pl.multiple_of(where_ref[base + h * pieces + k] * r, r)
            lhs_ref[k * r : (k + 1) * r, side] = of_ref[pl.ds(start, r), side]
    wide = 2 * LANES

    def block(b, carry):
        at = pl.ds(pl.multiple_of(b * wide, wide), wide)
        got = lax.dot_general(
            lhs_ref[...], p_ref[at, :], (((1,), (1,)), ((), ())), preferred_element_type=F32
        )
        away_ref[:, at] = got[:q, :].astype(away_ref.dtype)
        own_ref[:, at] = got[q:, :]
        return carry

    lax.fori_loop(0, w // wide, block, 0)


def swap(x, axis, size, mask, only=None):
    return lax.ppermute(x, axis, [(i, i ^ mask) for i in range(size) if only is None or only(i)])


def maps_kernel(mass_ref, logw_ref, *refs):
    parts, (old_hbm, new_hbm, left_ref, right_ref, last_ref, sems) = refs[:9], refs[9:]
    width = left_ref.shape[1]
    copies = [
        pltpu.make_async_copy(last_ref, new_hbm, sems.at[0]),
        pltpu.make_async_copy(left_ref, old_hbm.at[:, :width], sems.at[1]),
        pltpu.make_async_copy(right_ref, old_hbm.at[:, width:], sems.at[2]),
    ]
    order = ((last_ref, parts[6:]), (left_ref, parts[:3]), (right_ref, parts[3:6]))
    for i, (out_ref, terms) in enumerate(order):
        for c in range(out_ref.shape[1] // LANES):
            lane = slice(c * LANES, (c + 1) * LANES)
            total = sum(term[:, lane].astype(F32) for term in terms)
            if i == 0:
                out_ref[:, lane] = total / jnp.exp(logw_ref[c : c + 1, :])
            else:
                row = (i - 1) * (width // LANES) + c
                out_ref[:, lane] = total / mass_ref[row : row + 1, :]
        copies[i].start()
    for copy in copies:
        copy.wait()


def position(n):
    return (n // 2) + (n % 2) * (7 - 2 * (n // 2))


def device_at(p):
    p = p % 8
    return 2 * p - (p // 4) * (4 * p - 15)


def turn(x, step):
    return lax.ppermute(x, NEW, [(i, device_at(position(i) + step)) for i in range(8)])


STACKS = ((0, 1, 7, 2, 6, 5, 4, 3), (0, 1, 7, 2, 6, 3, 4, 5))
EARLY = 6


def looked_up(table, index):
    return sum(jnp.where(index == i, value, 0) for i, value in enumerate(table))


def gather_old(first):
    up, down = list(first), list(first)
    behind, ahead, opposite = [], [], [None, None]
    for hop in (1, 2, 3, 4):
        for h in (0, 1):
            if hop < 4 or h == 0:
                up[h] = turn(up[h], 1)
            if hop < 4 or h == 1:
                down[h] = turn(down[h], -1)
        if hop < 4:
            behind.append(list(up))
            ahead.append(list(down))
    opposite = [up[0], down[1]]
    return [first, *ahead, opposite, *behind[::-1]]


def gather_new(x):
    across = swap(x, OLD, 4, 2, None)
    return [x, across, swap(x, OLD, 4, 1, None), swap(across, OLD, 4, 1, None)]


def scatter_old(far, near):
    four, up3, down3 = far
    up = {3: up3, 2: near[0], 1: near[2]}
    down = {3: down3, 2: near[1], 1: near[3]}
    last = [[near[4][0]], [near[4][1]]]
    for h in (0, 1):
        for blocks, step, start in ((up, 1, 4 - h), (down, -1, 3 + h)):
            x = four[h] if start == 4 else blocks[3][h]
            for hop in range(start, 0, -1):
                x = turn(x.astype(BF16), step)
                if hop > 1:
                    x = blocks[hop - 1][h] + x.astype(F32)
            last[h].append(x)
    return last


def integers(values):
    return jnp.stack([jnp.asarray(v, jnp.int32) for v in values])


def is_tuned(n_old, n_new):
    return (n_old, n_new) == (4, 8)


def per_device(n_old, n_new, old_emb, new_emb, old_logw, new_logw):
    tuned = is_tuned(n_old, n_new)
    width, height = old_logw.shape[0], new_logw.shape[0]
    wide, tall = width // LANES, height // LANES
    depth = old_emb.shape[0] * n_new
    scale = 1.0 / (math.sqrt(depth) * EPSILON)
    if tuned:
        own = call(
            cut_kernel,
            [((old_emb.shape[0], width // 2), BF16, True)] * 2,
            [pltpu.SemaphoreType.DMA((2,))],
            [(old_emb, HBM)],
            2,
            nbytes=4 * old_emb.size,
        )
        old_slots, new_slots = gather_old(own), gather_new(new_emb)
        p, me = position(lax.axis_index(NEW)), lax.axis_index(OLD)
        owners = [device_at(p + i) for stack in STACKS for i in stack]
        owners = owners + [me, me ^ 2, me ^ 1, me ^ 3]
    else:
        old_all = lax.all_gather(old_emb, NEW, axis=0, tiled=True)
        old_slots = [[old_all[: depth // 2]], [old_all[depth // 2 :]]]
        new_slots = [lax.all_gather(new_emb, OLD, axis=0, tiled=True)]
        owners = [0, 1, 0, 1, 0]
    held = len(owners)
    if tuned:
        owners = owners + [device_at(p + i) for i in (4, 3, -3, 2, -2, 1, -1, 0)]
        for pair in ((me ^ 3, me ^ 2), (me ^ 1, me)):
            ahead = [(position(2 * o + i) - p) % 8 for o in pair for i in (0, 1)]
            for stack in STACKS:
                slot = [stack.index(i) for i in range(8)]
                owners = owners + [looked_up(slot, i) for i in ahead]
    where = integers(owners)
    old_w = old_logw.reshape(wide, LANES)
    new_w = new_logw.reshape(tall, LANES)
    cells = width * height
    n_slots = len(old_slots)
    rows = depth // n_slots
    if tuned:
        stacked = [
            (old_slots[stack[i]][h], (i * rows, h * (width // 2)), i < EARLY)
            for h, stack in enumerate(STACKS)
            for i in range(n_slots)
        ]
        known = (EARLY - 1) * rows // LANES * LANES + LANES
    else:
        stacked = [(slot[0], (i * rows, 0), i == 0) for i, slot in enumerate(old_slots)]
        known = rows
    early = [(x, at) for x, at, there in stacked if there]
    late = [(x, at) for x, at, there in stacked if not there]
    message = (n_new, wide, LANES)
    *new_rows, new_full = call(
        functools.partial(prepare_kernel, n_slots),
        [((height, depth), BF16, True)] * 2 + [((depth, height), BF16, True)],
        [pltpu.VMEM((depth, height), BF16)],
        [(where, SM)] + [(x, VM) for x in new_slots],
        8,
        flops=cells,
        nbytes=8 * depth * height,
    )
    part, part_full = call(
        functools.partial(early_kernel, [at for _, at in early], known),
        [((height, width), F32, True), ((depth, width), BF16, True)],
        [],
        [(x, STAY) for x in new_rows] + [(x, VM) for x, _ in early],
        4,
        flops=2 * cells * known,
        nbytes=4 * cells,
    )
    lt, k, old_full, a, msg = call(
        functools.partial(logits_kernel, [at for _, at in late], known, scale),
        [
            ((height, width), F32, True),
            ((height, width), F32, True),
            ((depth, width), BF16, True),
            ((wide, LANES), F32, True),
            (message, F32, False),
        ],
        [pltpu.VMEM((wide, LANES), F32)],
        [(part, STAY), (part_full, STAY)]
        + [(x, STAY) for x in new_rows]
        + [(x, VM) for x, _ in late],
        8,
        flops=2 * cells * (depth - known),
        nbytes=12 * cells,
        exps=cells,
        aliases={0: 0, 1: 2},
    )

    def over_old(message):
        return [message] + [swap(message, OLD, n_old, d) for d in range(1, n_old)]

    chunk = [pltpu.VMEM((LANES, width), F32), pltpu.SemaphoreType.DMA]
    for step in range(ITERS):
        got = lax.all_to_all(msg, NEW, 0, 0, tiled=True)
        keep = step + 1 == ITERS
        kept = [((wide, LANES), F32, True)] if keep else []
        *f, columns = call(
            functools.partial(column_kernel, keep),
            kept + [((tall, LANES), F32, True)],
            [pltpu.VMEM((wide, LANES), F32)] * (1 if keep else 2) + chunk,
            [(got, VM), (a, STAY), (old_w, VM), (k, STAY), (lt, ANY)],
            6,
            flops=2 * cells,
            nbytes=4 * cells,
        )
        columns = over_old(columns)
        if step + 1 < ITERS:
            (msg,) = call(
                functools.partial(row_kernel, n_old),
                [(message, F32, False)],
                [pltpu.VMEM((tall, LANES), F32)] * 2
                + [pltpu.VMEM((wide, LANES), F32)] * 2
                + chunk,
                [(c, VM) for c in columns]
                + [(new_w, VM), (a, STAY), (k, STAY), (lt, ANY)],
                6,
                flops=2 * cells,
                nbytes=4 * cells,
            )
    r = depth // n_new
    types = (BF16, BF16, F32, BF16, BF16, F32) if tuned else ()
    g, plan, mass, *far = call(
        functools.partial(plan_kernel, n_old, held),
        [
            ((tall, LANES), F32, True),
            ((height, width), BF16, True),
            ((wide, LANES), F32, True),
        ]
        + [((r, width // 2), dtype, False) for dtype in types],
        [pltpu.VMEM((max(1, len(types) // 2) * r, height), BF16), pltpu.VMEM((height, LANES), F32)],
        [(where, SM)]
        + [(c, VM) for c in columns]
        + [(new_w, VM), (f[0], STAY), (lt, STAY), (new_full, STAY)],
        8,
        flops=2 * cells * (1 + r * len(types) // 2),
        nbytes=6 * cells,
        exps=cells,
    )
    far = [far[i : i + 2] for i in range(0, len(far), 2)]
    if tuned:

        def old_part(base, types):
            got = call(
                functools.partial(old_terms_kernel, base),
                [((r, width // 2), dtype, False) for dtype in types],
                [pltpu.VMEM((len(types) // 2 * r, height), BF16)],
                [(where, SM), (new_full, STAY), (plan, STAY)],
                16,
                flops=cells * r * len(types),
                nbytes=2 * cells,
            )
            return [got[i : i + 2] for i in range(0, len(got), 2)]

        for d in (1, 2, 4):
            mass = mass + swap(mass, NEW, 8, d, None)
        old_parts = scatter_old(far, old_part(held + 3, (F32,) * 10))
        q = depth // n_old


        def new_part(base):
            away, own = call(
                functools.partial(new_terms_kernel, base, 4),
                [((q, height), BF16, False), ((q, height), F32, False)],
                [pltpu.VMEM((2 * q, width), BF16)],
                [(where, SM), (old_full, STAY), (plan, STAY)],
                16,
                flops=cells * depth,
                nbytes=4 * cells,
            )
            return own, swap(away, OLD, 4, 1, None)

        own, core = new_part(held + 8)
        far = swap((own + core.astype(F32)).astype(BF16), OLD, 4, 2, None)
        new_parts = [*new_part(held + 16), far]
        old_map, new_map = call(
            maps_kernel,
            [((r, width), F32, ANY), ((q, height), F32, ANY)],
            [pltpu.VMEM((r, width // 2), F32)] * 2
            + [pltpu.VMEM((q, height), F32), pltpu.SemaphoreType.DMA((3,))],
            [(mass, VM), (new_w, VM)] + [(x, VM) for x in (*old_parts[0], *old_parts[1], *new_parts)],
            8,
            flops=8 * r * width,
            nbytes=16 * r * width,
        )
    else:
        mass = lax.psum(mass, NEW)
        old_terms = jnp.dot(new_full, plan, preferred_element_type=F32)
        new_terms = lax.dot_general(
            old_full, plan, (((1,), (1,)), ((), ())), preferred_element_type=F32
        )
        old_sums = lax.psum_scatter(old_terms, NEW, scatter_dimension=0, tiled=True)
        new_sums = lax.psum_scatter(new_terms, OLD, scatter_dimension=0, tiled=True)
        old_map = old_sums / mass.reshape(width)[None, :]
        new_map = new_sums / jnp.exp(new_logw)[None, :]
    return (f[0].reshape(width), g.reshape(height), old_map, new_map)


def solution(mesh):
    in_specs = (P(NEW, OLD), P(OLD, NEW), P(OLD), P(NEW))
    out_specs = (P(OLD), P(NEW), P(NEW, OLD), P(OLD, NEW))
    n_old, n_new = mesh.shape[OLD], mesh.shape[NEW]
    return jax.shard_map(
        functools.partial(per_device, n_old, n_new),
        mesh=mesh,
        in_specs=in_specs,
        out_specs=out_specs,
        check_vma=False,
    )
```
